768 devices in a mesh: tile: 128 (over y, z_lo, x), lev: 6 (over z_hi, core).
Axes of the slice: x: 4, y: 8, z: 12 (z_hi: 3, z_lo: 4; z = z_hi * 4 + z_lo), core: 2. Of those that a mesh axis runs over, the one named last changes fastest.
Arguments:
- sources: float32 [2, 6, 384, 1024], P(None, 'lev', 'tile'), may hold values from -60 to 60
- mass_coef: float32 [384, 1024], P('tile'), may hold values from 0.0005 to 0.002
- neighbour_sub: int32 [384, 4], replicated, may hold values from 0 to 383, as said below
- neighbour_side: int32 [384, 4], replicated, may hold values from 0 to 3
- side_flip: int32 [384, 4], replicated, may hold values from 0 to 1
Outputs:
- solution: float32 [2, 6, 384, 1024], P(None, 'lev', 'tile')
- residual: float32 [2, 6, 384, 1024], P(None, 'lev', 'tile')
The draws below stay inside these ranges and needn't reach their ends.
Inputs may be any that keep to these rules, and one draw needn't show every extreme that they name: `neighbour_sub`: the sides pair up as the sides of the subdomains on the six faces of a cube, 8 x 8 subdomains a face, with the subdomains numbered and oriented arbitrarily; a side's neighbour lists it back.
All inputs are finite; a program needn't handle non-finite values.
Results may differ from the reference program's by a relative error of at most 0.0003.
Values sent between devices are 32-bit elements; how exact they have to be, the bound alone decides.
A program may use at most 32 MiB of HBM per device.

```python
import math
import jax
import jax.numpy as jnp
from jax import lax

SIDE = 32
CELLS = 1024
LEVELS = 6
BLOCKS = 8
SUBS = 384
ITERS = 2


def unit_rows(axis_ids):
    return (axis_ids[..., None] == jnp.arange(3, dtype=jnp.int32)).astype(jnp.int32)


def cube_tables(key):
    blocks = BLOCKS
    count_all = 6 * blocks * blocks
    geo_ids = jnp.arange(count_all, dtype=jnp.int32)
    face_id = geo_ids // (blocks * blocks)
    row_blk = geo_ids // blocks % blocks
    col_blk = geo_ids % blocks
    normal = face_id // 2
    sign_n = 1 - 2 * (face_id % 2)
    tan_one = (normal + 1) % 3
    tan_two = (normal + 2) % 3
    normal_vec = sign_n[:, None] * unit_rows(normal)
    centre = blocks * normal_vec + (2 * row_blk + 1 - blocks)[:, None] * unit_rows(tan_one) + (2 * col_blk + 1 - blocks)[:, None] * unit_rows(tan_two)
    swapped = jax.random.randint(jax.random.fold_in(key, 101), (count_all,), 0, 2)
    sign_a = 1 - 2 * jax.random.randint(jax.random.fold_in(key, 102), (count_all,), 0, 2)
    sign_b = 1 - 2 * jax.random.randint(jax.random.fold_in(key, 103), (count_all,), 0, 2)
    axis_i = jnp.where(swapped == 1, tan_two, tan_one)
    axis_j = jnp.where(swapped == 1, tan_one, tan_two)
    vec_i = sign_a[:, None] * unit_rows(axis_i)
    vec_j = sign_b[:, None] * unit_rows(axis_j)
    outward = jnp.stack([-vec_i, vec_j, vec_i, -vec_j], axis=1)
    running = jnp.stack([vec_j, vec_i, vec_j, vec_i], axis=1)
    stepped = centre[:, None, :] + 2 * outward
    leaves = (jnp.max(jnp.abs(stepped), axis=-1) > blocks)[..., None]
    landing = jnp.where(leaves, centre[:, None, :] + outward - normal_vec[:, None, :], stepped)
    backward = jnp.where(leaves, normal_vec[:, None, :] + 0 * outward, -outward)
    on_axis = (jnp.abs(landing) == blocks).astype(jnp.int32)
    new_axis = jnp.sum(on_axis * jnp.arange(3, dtype=jnp.int32), axis=-1)
    new_val = jnp.sum(on_axis * landing, axis=-1)
    new_face = 2 * new_axis + (new_val < 0).astype(jnp.int32)
    coord_one = jnp.sum(landing * unit_rows((new_axis + 1) % 3), axis=-1)
    coord_two = jnp.sum(landing * unit_rows((new_axis + 2) % 3), axis=-1)
    geo_nbr = new_face * blocks * blocks + (coord_one + blocks - 1) // 2 * blocks + (coord_two + blocks - 1) // 2
    their_out = outward[geo_nbr]
    matched = jnp.all(their_out == backward[:, :, None, :], axis=-1).astype(jnp.int32)
    geo_side = jnp.sum(matched * jnp.arange(4, dtype=jnp.int32), axis=-1)
    their_run = jnp.take_along_axis(running[geo_nbr], geo_side[..., None, None], axis=2)[:, :, 0, :]
    geo_flip = (jnp.sum(running * their_run, axis=-1) < 0).astype(jnp.int32)
    shuffle = jax.random.permutation(jax.random.fold_in(key, 104), count_all)
    placed = jnp.argsort(shuffle).astype(jnp.int32)
    nbr_store = placed[geo_nbr][shuffle]
    return (nbr_store.astype(jnp.int32), geo_side[shuffle].astype(jnp.int32), geo_flip[shuffle].astype(jnp.int32))


def draw_neighbour_sub(key, part):
    return cube_tables(key)[0]


def draw_neighbour_side(key, part):
    return cube_tables(key)[1]


def draw_side_flip(key, part):
    return cube_tables(key)[2]


def draw_sources(key, part):
    shape = (2, LEVELS, SUBS, CELLS)
    level_ramp = 1.0 + 2.0 * jnp.arange(LEVELS, dtype=jnp.float32) / max(LEVELS - 1, 1)
    sub_ramp = 1.0 + 2.0 * jnp.arange(SUBS, dtype=jnp.float32) / (SUBS - 1)
    noise = jnp.clip(jax.random.normal(jax.random.fold_in(key, 1), shape, jnp.float32), -4.0, 4.0)
    jitter = jnp.exp(jax.random.uniform(jax.random.fold_in(key, 2), (2, 1, SUBS, 1), jnp.float32, -0.35, 0.35))
    return noise * level_ramp[None, :, None, None] * sub_ramp[None, None, :, None] * jitter


def level_of(own_key, shape, cuts, least, high):
    loudness = 1.0
    for axis_at, parts in cuts:
        draws = jax.random.uniform(jax.random.fold_in(jax.random.fold_in(own_key, 6), axis_at), (parts,), jnp.float32, least / len(cuts), high / len(cuts))
        loudness = loudness * jnp.repeat(jnp.exp(draws), shape[axis_at] // parts).reshape((-1,) + (1,) * (len(shape) - 1 - axis_at))
    return loudness


def setup_inputs(seed: int = 0) -> dict:
    streams_of = jax.random.split(jax.random.key(seed), 6)
    return {
        "sources": draw_sources(jax.random.fold_in(streams_of[5], 71), 0),
        "mass_coef": jnp.clip(jnp.exp(math.log(0.002) - 1.3862944 * jax.random.uniform(streams_of[1], (SUBS, CELLS), jnp.float32) ** level_of(streams_of[1], (SUBS, CELLS), ((0, 128),), -0.2, 0.2)), 0.0005, 0.002),
        "neighbour_sub": draw_neighbour_sub(jax.random.fold_in(streams_of[5], 71), 0),
        "neighbour_side": draw_neighbour_side(jax.random.fold_in(streams_of[5], 71), 0),
        "side_flip": draw_side_flip(jax.random.fold_in(streams_of[5], 71), 0),
    }


HIGH = lax.Precision.HIGHEST

def sine_table(edge_len):
    ordinal = jnp.arange(edge_len, dtype=jnp.float32) + 1.0
    step_angle = math.pi / (edge_len + 1.0)
    sine_rows = math.sqrt(2.0 / (edge_len + 1.0)) * jnp.sin(step_angle * ordinal[:, None] * ordinal[None, :])
    spectrum = 2.0 - 2.0 * jnp.cos(step_angle * ordinal)
    return (sine_rows, spectrum)

def local_solve(vector, edge_len):
    sine_rows, spectrum = sine_table(edge_len)
    divisor = spectrum[:, None] + spectrum[None, :]
    spectral = jnp.einsum('ij,abnjk->abnik', sine_rows, vector, precision=HIGH)
    spectral = jnp.einsum('abnik,kl->abnil', spectral, sine_rows, precision=HIGH)
    spectral = spectral / divisor
    restored = jnp.einsum('ij,abnjk->abnik', sine_rows, spectral, precision=HIGH)
    return jnp.einsum('abnik,kl->abnil', restored, sine_rows, precision=HIGH)

def field_rims(vector):
    return jnp.stack([vector[..., 0, :], vector[..., :, -1], vector[..., -1, :], vector[..., :, 0]], axis=-2)

def operate(vector, mass_grid, received):
    padded = jnp.pad(vector, ((0, 0), (0, 0), (0, 0), (1, 1), (1, 1)))
    beside = padded[..., 2:, 1:-1] + padded[..., :-2, 1:-1] + padded[..., 1:-1, 2:] + padded[..., 1:-1, :-2]
    beside = beside.at[..., 0, :].add(received[..., 0, :])
    beside = beside.at[..., :, -1].add(received[..., 1, :])
    beside = beside.at[..., -1, :].add(received[..., 2, :])
    beside = beside.at[..., :, 0].add(received[..., 3, :])
    return (4.0 + mass_grid) * vector - beside

def coarse_factor(mass_sums, neighbour_sub, edge_len):
    count_all = mass_sums.shape[0]
    sub_ids = jnp.arange(count_all, dtype=jnp.int32)
    adjacency = lax.optimization_barrier(jnp.sum((neighbour_sub[:, :, None] == sub_ids[None, None, :]).astype(jnp.float32), axis=1))
    matrix = edge_len * (4.0 * jnp.eye(count_all, dtype=jnp.float32) - adjacency) + jnp.diag(mass_sums)
    return jnp.linalg.cholesky(matrix)

def coarse_solve(factor, sums):
    count_all = factor.shape[0]
    columns = sums.reshape(-1, count_all).T
    middle = lax.linalg.triangular_solve(factor, columns, left_side=True, lower=True, transpose_a=False)
    solved = lax.linalg.triangular_solve(factor, middle, left_side=True, lower=True, transpose_a=True)
    return solved.T.reshape(sums.shape)

def spread(scalars):
    return scalars[:, None, None, None, None]

def dot_local(left, right):
    return lax.optimization_barrier(jnp.sum(left * right, axis=(1, 2, 3, 4)))

def reference(sources, mass_coef, neighbour_sub, neighbour_side, side_flip):
    grid_shape = (2, LEVELS, SUBS, SIDE, SIDE)
    residual = sources.reshape(grid_shape)
    mass_grid = mass_coef.reshape(SUBS, SIDE, SIDE)
    factor = coarse_factor(lax.optimization_barrier(jnp.sum(mass_coef, axis=-1)), neighbour_sub, SIDE)
    flipped = (side_flip == 1)[..., None]

    def received(vector):
        picked = field_rims(vector)[:, :, neighbour_sub, neighbour_side]
        return jnp.where(flipped, picked[..., ::-1], picked)

    def precondition(vector):
        local_part = local_solve(vector, SIDE)
        coarse = coarse_solve(factor, lax.optimization_barrier(jnp.sum(vector, axis=(3, 4))))
        return local_part + coarse[..., None, None]
    solution = jnp.zeros(grid_shape, jnp.float32)
    corrected = precondition(residual)
    direction = corrected
    prec_norm = dot_local(residual, corrected)
    for step in range(ITERS):
        image = operate(direction, mass_grid, received(direction))
        step_size = prec_norm / dot_local(direction, image)
        solution = solution + spread(step_size) * direction
        residual = residual - spread(step_size) * image
        if step + 1 < ITERS:
            corrected = precondition(residual)
            norm_next = dot_local(residual, corrected)
            direction = corrected + spread(norm_next / prec_norm) * direction
            prec_norm = norm_next
    out_shape = (2, LEVELS, SUBS, CELLS)
    return (solution.reshape(out_shape), residual.reshape(out_shape))
```

```python
import math

import jax
import jax.numpy as jnp
import numpy as np
from jax import lax
from jax.experimental import pallas as pl
from jax.experimental.pallas import tpu as pltpu
from jax.sharding import PartitionSpec as P

F32 = jnp.float32
BF16 = jnp.bfloat16
SIDE = 32
SUBS = 384
PLANE = 16
COLUMN = 8
LEVS = 6
EACH = 3
FIELDS = 6
ROWS = FIELDS * SIDE

SHIFT = 1.28
SIGMA = 3.0
LOW = 32.0 * 0.06486 + SHIFT
TOP = 32.0 * 8.0 + SHIFT
RHO = 0.7681 / LOW
CHEB = 7


def roll(x, shift, axis):
    return pltpu.roll(x, shift, axis)


def iota(shape, dim):
    return lax.broadcasted_iota(jnp.int32, shape, dim)


def dot(a, b):
    return jnp.dot(a, b, preferred_element_type=F32)


def split(x, n):
    parts = []
    for _ in range(n):
        part = x.astype(BF16)
        parts.append(part)
        x = x - part.astype(F32)
    return parts


def pick(onehot, x):
    a, b, c = split(x, 3)
    return dot(onehot, a) + dot(onehot, b) + dot(onehot, c)


def spread(x, onehot):
    a, b, c = split(x, 3)
    return dot(a, onehot) + dot(b, onehot) + dot(c, onehot)


def mm3(a, b):
    ah, al = a
    bh, bl = b
    return dot(ah, bh) + (dot(ah, bl) + dot(al, bh))


def np_split(x):
    hi = x.astype(np.float32).astype(jnp.bfloat16)
    lo = (x - hi.astype(np.float64)).astype(np.float32).astype(jnp.bfloat16)
    return hi, lo


def polynomial():
    deg = 7
    nodes = np.cos(np.pi * (np.arange(deg + 1) + 0.5) / (deg + 1))
    g = 4.0 * nodes
    x = 128.0 + SHIFT - 32.0 * g

    def cheb(n, t):
        return np.where(
            np.abs(t) <= 1,
            np.cos(n * np.arccos(np.clip(t, -1, 1))),
            np.sign(t) ** n * np.cosh(n * np.arccosh(np.maximum(np.abs(t), 1))),
        )

    def tau(v):
        return (TOP + LOW - 2 * v) / (TOP - LOW)

    top = cheb(deg + 1, tau(0.0))
    vals = (1.0 - cheb(deg + 1, tau(x)) / top) / x
    coef = np.polynomial.polynomial.polyfit(nodes, vals, deg)
    at_one = np.polynomial.polynomial.polyval(1.0, coef)
    const = (1.0 / (SHIFT + SIGMA) - at_one) / SUBS
    return [float(c / 4.0**k) for k, c in enumerate(coef)], float(const), float(1.0 / top)


def constants():
    o = np.arange(SIDE) + 1.0
    step = math.pi / (SIDE + 1.0)
    sine = math.sqrt(2.0 / (SIDE + 1.0)) * np.sin(step * o[:, None] * o[None, :])
    lam = 2.0 - 2.0 * np.cos(step * o)
    s6 = np.kron(np.eye(FIELDS), sine)
    k = np.arange(SIDE)
    bt = np.zeros((SIDE, 4, SIDE))
    bt[k, 0, k] = 1
    bt[k, 2, k] = 1
    bt[31, 1, :] = 1
    bt[0, 3, :] = 1
    bt = bt.reshape(SIDE, 128)
    sr = np.zeros((SIDE, 256))
    sr[:, :SIDE] = sine
    sr[:, 128:] = sine @ bt
    rows = np.arange(ROWS)
    i = rows % SIDE
    field = rows // SIDE
    lanes = np.arange(128)
    side, kk = lanes // SIDE, lanes % SIDE
    mask2 = (
        ((side == 0)[None] & (i == 0)[:, None])
        | ((side == 2)[None] & (i == 31)[:, None])
        | (((side == 1) | (side == 3))[None] & (kk[None] == i[:, None]))
    )
    grp = field[None, :] == np.arange(8)[:, None]
    m = np.arange(SUBS)
    cmp = ((lanes // 8)[:, None] == (m // EACH % PLANE)[None]) & ((lanes % 8)[:, None] == (m % EACH)[None])
    rev = (side[:, None] == side[None]) & (kk[:, None] == 31 - kk[None])
    oo = np.arange(32)
    op, os_ = oo // 16, oo % 16
    n = field % EACH
    gp = ((field // EACH)[:, None] == op[None]) & (
        ((os_ < 12)[None] & ((os_ // 4)[None] == n[:, None])) | ((os_ - 12)[None] == n[:, None])
    )
    o16 = np.arange(16)
    lm = np.zeros((16, 256))
    lm[:, :128] = (o16 < 12)[:, None] & ((o16 % 4)[:, None] == side[None])
    lm[:, 128:] = ((o16 >= 12) & (o16 < 15))[:, None]
    b16 = lambda a: a.astype(np.float32).astype(jnp.bfloat16)
    f32 = lambda a: a.astype(np.float32)
    inv = 1.0 / (lam[:, None] + lam[None, :])
    return dict(
        s6=np_split(s6),
        s=np_split(sine),
        sr=np_split(sr),
        inv=(f32(np.tile(inv, (FIELDS, 1))),),
        mask2=(f32(mask2),),
        grp=(b16(grp),),
        grpt=(b16(grp.T),),
        bm=(b16(bt.T),),
        cmp=(b16(cmp),),
        rev=(b16(rev),),
        gp=(b16(gp),),
        lm=(f32(lm),),
    )


def local_part(r, c):
    v = mm3(c["s6"], split(r, 2))
    v = mm3(split(v, 2), c["s"]) * c["inv"][0]
    v = mm3(split(v, 2), c["sr"])
    v = mm3(c["s6"], split(v, 2))
    rims = pick(c["grp"][0], v[:, 128:] * c["mask2"][0])
    return v[:, :SIDE], rims


def packed(v, q, per):
    total = jnp.sum(v, axis=1, keepdims=True)
    shape = (v.shape[0], 128)
    at = iota(shape, 1) == q * 8 + lax.shift_right_logical(iota(shape, 0), 5)
    return jnp.sum(jnp.where(at, total, 0.0), axis=0, keepdims=True)


def tile_a(rims, sums, mass):
    row = iota((8, 128), 0)
    return jnp.where(row == 6, sums, jnp.where(row == 7, mass, rims))


def choose_matrix(colidx):
    return (iota((256, 512), 1) == colidx).astype(BF16)


def tiles_b(buf, choose):
    flat = buf.reshape(128, 128)
    turned = jnp.concatenate([flat] + [roll(flat, 32 * t, 1) for t in (1, 2, 3)], axis=0)
    got = pick(choose, turned)
    group = lax.shift_right_logical(iota((64, 128), 1), 5)
    out = jnp.where(group == 0, got[:64], 0.0)
    for s in (1, 2, 3):
        out = jnp.where(group == s, got[64 * s : 64 * s + 64], out)
    row = iota((8, 128), 0)
    plane = jnp.where(row >= 6, jnp.sum(buf, axis=0), 0.0)
    return out.reshape(8, 8, 128) + plane[None]


def graph(nb):
    lane = iota((SUBS, SUBS), 1)
    total = jnp.zeros((SUBS, SUBS), F32)
    for s in range(4):
        total = total + (nb[:, s : s + 1] == lane).astype(F32)
    return total


def start_inverse(g32):
    coef, const, rho = polynomial()
    g = g32.astype(BF16)
    g2 = dot(g, g)
    g2b = g2.astype(BF16)
    g3 = dot(g2b, g)
    g4 = dot(g2b, g2b)
    g3b, g4b = g3.astype(BF16), g4.astype(BF16)
    eye = (iota((SUBS, SUBS), 0) == iota((SUBS, SUBS), 1)).astype(F32)
    x = coef[0] * eye + const + coef[1] * g32 + coef[2] * g2 + coef[3] * g3 + coef[4] * g4
    x = x + coef[5] * dot(g4b, g) + coef[6] * dot(g4b, g2b) + coef[7] * dot(g4b, g3b)
    return x, rho


def newton(x, g, rho, last):
    xs = split(x, 3)
    gx = dot(g, xs[0]) + (dot(g, xs[1]) + dot(g, xs[2]))
    ones = (SIGMA / SUBS) * jnp.sum(x, axis=0, keepdims=True)
    eye = (iota((SUBS, SUBS), 0) == iota((SUBS, SUBS), 1)).astype(F32)
    rest = eye - ((128.0 + SHIFT) * x - 32.0 * gx + ones)
    x = x + mm3(xs[:2], split(rest, 2))
    if last:
        return x, 0.0
    scale = 2.0 / (2.0 - rho * rho)
    return scale * x, rho * rho / (2.0 - rho * rho)


def wanted_rows(eidx):
    lane = iota((16, SUBS), 1)
    plus = (eidx[:, 0:1] == lane).astype(F32)
    minus = (eidx[:, 1:2] == lane).astype(F32)
    ones = (iota((16, SUBS), 0) == 15).astype(F32)
    return (plus - minus + ones).astype(BF16)


def to_vectors(slots, c):
    wide = spread(slots, c["cmp"][0])
    rows = []
    for k in range(slots.shape[0] // 8):
        row, lane = iota((8, SUBS), 0), iota((8, SUBS), 1)
        keep = (lane >= row * 48) & (lane < row * 48 + 48)
        rows.append(jnp.sum(jnp.where(keep, wide[8 * k : 8 * k + 8], 0.0), axis=0, keepdims=True))
    return rows


def inverse_rows(first, xh, xl, mass):
    delta = mass - SHIFT

    def apply(d, fine):
        e = d * delta
        eh, el = split(e, 2)
        if fine:
            return d + (dot(eh, xh) + (dot(el, xh) + dot(eh, xl)))
        return d + dot(eh, xh)

    sig = 1.0 / RHO
    rk = 1.0 / sig
    rest = first
    d = rest
    y = d
    for k in range(CHEB):
        rest = rest - apply(d, k < 4)
        nxt = 1.0 / (2.0 * sig - rk)
        d = (nxt * rk) * d + (2.0 * nxt / RHO) * rest
        y = y + d
        rk = nxt
    u = y[15:16]
    t = jnp.sum(u, axis=1, keepdims=True)
    w = jnp.sum(y, axis=1, keepdims=True)
    share = (SIGMA / SUBS) / (1.0 - (SIGMA / SUBS) * t)
    return y + (w * share) * u


def coarse_edges(y, s0, s1, c):
    parts = []
    for s in (s0, s1):
        parts.append(jnp.sum(y * s, axis=1, keepdims=True) * c["lm"][0])
    return jnp.concatenate(parts, axis=0)


def finish(r, local, mass2, rims, flip, y, s0, s1, c):
    turned = spread(rims, c["rev"][0])
    rims = jnp.where(flip > 0.5, turned, rims)
    w = coarse_edges(y, s0, s1, c)
    wide = pick(c["gp"][0], w)
    edges = wide[:, :128] - pick(c["grpt"][0], rims)
    z = local + wide[:, 128 : 128 + SIDE]
    image = r + mass2 * z + spread(edges * c["mask2"][0], c["bm"][0])
    return z, image


def dots_row(pairs):
    rows = []
    for p in range(2):
        for a, b in pairs:
            half = slice(96 * p, 96 * p + 96)
            rows.append(jnp.sum(a[half] * b[half], axis=0, keepdims=True))
    block = jnp.concatenate(rows + [jnp.zeros((16 - len(rows), SIDE), F32)], axis=0)
    col = jnp.sum(block, axis=1, keepdims=True)
    at = iota((16, 128), 0) == iota((16, 128), 1)
    return jnp.sum(jnp.where(at, col, 0.0), axis=0, keepdims=True)


def steps(row, p):
    ga, de, rw, qw, zv, wv = [row[:, 6 * p + k : 6 * p + k + 1] for k in range(6)]
    a0 = ga / de
    g1 = ga - a0 * (de + rw) + a0 * a0 * qw
    d1 = de - a0 * (qw + zv) + a0 * a0 * wv
    beta = g1 / ga
    cross = de - a0 * (0.5 * (qw + zv))
    den = d1 + 2.0 * beta * cross + beta * beta * de
    a1 = g1 / den
    return a0 + a1 * (1.0 + beta), a1 * a0


def kernel(names, *refs):
    ins = refs[: 6 + sum(k for _, k in names)]
    r_ref, mass_ref, nb_ref, col_ref, eidx_ref, flip_ref = ins[:6]
    c, at = {}, 6
    for name, k in names:
        c[name] = [ref[...] for ref in ins[at : at + k]]
        at += k
    sol_ref, res_ref = refs[at : at + 2]
    (stga0, stga1, bufa0, bufa1, stgb0, stgb1, bufb0, bufb1) = refs[at + 2 : at + 10]
    (st3a, st3b, st3c, buf3a, buf3b, buf3c) = refs[at + 10 : at + 16]
    ssem, rsem = refs[at + 16 :]

    t = lax.axis_index("tile")
    lev = lax.axis_index("lev")
    plane = t // PLANE
    q = t % PLANE

    def peer_a(k):
        return (plane * PLANE + (q + k) % PLANE, lev)

    def peer_b(k):
        return (((plane + k) % COLUMN) * PLANE + q, lev)

    def peer_c(k):
        return (t, (lev + k) % LEVS)

    groups = ((peer_a, PLANE), (peer_b, COLUMN), (peer_c, LEVS))

    barrier = pltpu.get_barrier_semaphore()
    for peer, size in groups:
        for k in range(1, size):
            pl.semaphore_signal(barrier, 1, device_id=peer(k), device_id_type=pl.DeviceIdType.MESH)

    def send(group, src_of, dst, n):
        peer, size = groups[group]
        for k in range(1, size):
            target = peer(k)
            pltpu.make_async_remote_copy(
                src_ref=src_of(k), dst_ref=dst, send_sem=ssem.at[n], recv_sem=rsem.at[n],
                device_id=target, device_id_type=pl.DeviceIdType.MESH,
            ).start()

    def done(group, buf, n, recv):
        peer, size = groups[group]
        view = buf.at[pl.ds(0, size - 1)]
        copy = pltpu.make_async_remote_copy(
            src_ref=view, dst_ref=view, send_sem=ssem.at[n], recv_sem=rsem.at[n],
            device_id=peer(1), device_id_type=pl.DeviceIdType.MESH,
        )
        if recv:
            copy.wait_recv()
        else:
            copy.wait_send()

    r = r_ref[...]
    mass = mass_ref[...]
    mass2 = jnp.concatenate([mass, mass], axis=0)
    zrow = jnp.zeros((1, 128), F32)

    l0, rims = local_part(r, c)
    tile = tile_a(rims, packed(r, q, 0), packed(mass, q, 0))
    stga0[...] = tile
    bufa0[q] = tile
    pl.semaphore_wait(barrier, (PLANE - 1) + (COLUMN - 1) + (LEVS - 1))
    send(0, lambda k: stga0, bufa0.at[q], 0)

    choose = choose_matrix(col_ref[...])
    g32 = graph(nb_ref[...])
    x, rho = start_inverse(g32)
    g = g32.astype(BF16)

    done(0, bufa0, 0, True)
    stgb0[...] = tiles_b(bufa0[...], choose)
    bufb0[plane] = stgb0[plane]
    send(1, lambda k: stgb0.at[(plane + k) % COLUMN], bufb0.at[plane], 1)

    x, rho = newton(x, g, rho, False)
    x, rho = newton(x, g, rho, False)
    x, rho = newton(x, g, rho, True)
    xs = split(x, 3)
    e0 = wanted_rows(eidx_ref[...])
    first = dot(e0, xs[0]) + (dot(e0, xs[1]) + dot(e0, xs[2]))
    flip = flip_ref[...]

    done(1, bufb0, 1, True)
    got = bufb0[...]
    sums = bufb0[:, 6, :]
    masses = bufb0[:, 7, :]
    three = jnp.concatenate([masses, sums, roll(sums, 128 - EACH, 1)], axis=0)
    dvec, s0, s1 = to_vectors(three, c)
    y = inverse_rows(first, xs[0], xs[1], dvec)
    z0, q0 = finish(r, l0, mass2, jnp.sum(got, axis=0), flip, y, s0, s1, c)

    l1, rims = local_part(q0, c)
    tile = tile_a(rims, packed(q0, q, 0), zrow)
    stga1[...] = tile
    bufa1[q] = tile
    send(0, lambda k: stga1, bufa1.at[q], 2)
    done(0, bufa1, 2, True)
    stgb1[...] = tiles_b(bufa1[...], choose)
    bufb1[plane] = stgb1[plane]
    send(1, lambda k: stgb1.at[(plane + k) % COLUMN], bufb1.at[plane], 3)
    done(1, bufb1, 3, True)
    got = bufb1[...]
    sums = bufb1[:, 6, :]
    two = jnp.concatenate([sums, roll(sums, 128 - EACH, 1)], axis=0)
    s0, s1 = to_vectors(two, c)
    w, v = finish(q0, l1, mass2, jnp.sum(got, axis=0), flip, y, s0, s1, c)

    row = dots_row(((r, z0), (z0, q0), (r, w), (q0, w), (z0, v), (w, v)))
    for n, (group, me, stg, buf) in enumerate(
        ((0, q, st3a, buf3a), (1, plane, st3b, buf3b), (2, lev, st3c, buf3c))
    ):
        stg[...] = row
        buf[me] = row
        send(group, lambda k: stg, buf.at[me], 4 + n)
        done(group, buf, 4 + n, True)
        row = jnp.sum(buf[...], axis=0)

    for p in range(2):
        a, b = steps(row, p)
        half = slice(96 * p, 96 * p + 96)
        sol_ref[half, :] = a * z0[half] - b * w[half]
        res_ref[half, :] = r[half] - a * q0[half] + b * v[half]

    done(0, bufa0, 0, False)
    done(1, bufb0, 1, False)
    done(0, bufa1, 2, False)
    done(1, bufb1, 3, False)
    done(0, buf3a, 4, False)
    done(1, buf3b, 5, False)
    done(2, buf3c, 6, False)


def tables(neighbour_sub, neighbour_side, side_flip, t):
    plane, q = t // PLANE, t % PLANE

    def mine(a):
        return lax.dynamic_index_in_dim(a.reshape(COLUMN, PLANE, EACH, 4), q, 1, keepdims=False)

    nb, ns = mine(neighbour_sub), mine(neighbour_side)
    device = nb // EACH
    inside = device // PLANE == plane
    src = (device % PLANE) * 8 + nb % EACH
    turn = (jnp.arange(4, dtype=jnp.int32) - ns) % 4
    col = jnp.where(inside, turn * 128 + src, -1024)
    col = jnp.stack([col, col + EACH], axis=1).reshape(COLUMN, FIELDS, 4)
    col = jnp.pad(col, ((0, 0), (0, 2), (0, 0)), constant_values=-1)
    col = jnp.moveaxis(col, 2, 0).reshape(256, 1)
    own = t * EACH + jnp.arange(EACH, dtype=jnp.int32)
    mynb = lax.dynamic_slice_in_dim(neighbour_sub, t * EACH, EACH, 0)
    plus = jnp.concatenate([jnp.repeat(own, 4), own, jnp.full((1,), -1, jnp.int32)])
    minus = jnp.concatenate([mynb.reshape(-1), jnp.full((4,), -1, jnp.int32)])
    myflip = lax.dynamic_slice_in_dim(side_flip, t * EACH, EACH, 0).astype(F32)
    flip = jnp.repeat(myflip, SIDE, axis=1)
    flip = jnp.concatenate([flip, flip, jnp.zeros((2, 128), F32)], axis=0)
    return col, jnp.stack([plus, minus], axis=1), flip


def shards(sources, mass_coef, neighbour_sub, neighbour_side, side_flip):
    t = lax.axis_index("tile")
    col, eidx, flip = tables(neighbour_sub, neighbour_side, side_flip, t)
    consts = constants()
    names = tuple((k, len(v)) for k, v in consts.items())
    flat = [jnp.asarray(a) for v in consts.values() for a in v]
    vm = pl.BlockSpec(memory_space=pltpu.VMEM)
    args = [sources.reshape(ROWS, SIDE), mass_coef.reshape(EACH * SIDE, SIDE), neighbour_sub, col, eidx, flip, *flat]
    scratch = [
        pltpu.VMEM((8, 128), F32), pltpu.VMEM((8, 128), F32),
        pltpu.VMEM((PLANE, 8, 128), F32), pltpu.VMEM((PLANE, 8, 128), F32),
        pltpu.VMEM((COLUMN, 8, 128), F32), pltpu.VMEM((COLUMN, 8, 128), F32),
        pltpu.VMEM((COLUMN, 8, 128), F32), pltpu.VMEM((COLUMN, 8, 128), F32),
        pltpu.VMEM((1, 128), F32), pltpu.VMEM((1, 128), F32), pltpu.VMEM((1, 128), F32),
        pltpu.VMEM((PLANE, 1, 128), F32), pltpu.VMEM((COLUMN, 1, 128), F32), pltpu.VMEM((LEVS, 1, 128), F32),
        pltpu.SemaphoreType.DMA((7,)), pltpu.SemaphoreType.DMA((7,)),
    ]
    out = jax.ShapeDtypeStruct((ROWS, SIDE), F32)
    sol, res = pl.pallas_call(
        lambda *refs: kernel(names, *refs),
        out_shape=(out, out),
        in_specs=[vm] * len(args),
        out_specs=(vm, vm),
        scratch_shapes=scratch,
        compiler_params=pltpu.CompilerParams(collective_id=0, has_side_effects=True, vmem_limit_bytes=48 << 20),
        name="schwarz",
    )(*args)
    return sol.reshape(sources.shape), res.reshape(sources.shape)


def solution(mesh):
    placed = (P(None, "lev", "tile", None), P("tile", None), P(), P(), P())
    return jax.shard_map(
        shards,
        mesh=mesh,
        in_specs=placed,
        out_specs=(P(None, "lev", "tile", None), P(None, "lev", "tile", None)),
        check_vma=False,
    )
```

```python
import math

import jax
import jax.numpy as jnp
import numpy as np
from jax import lax
from jax.experimental import pallas as pl
from jax.experimental.pallas import tpu as pltpu
from jax.sharding import PartitionSpec as P

F32 = jnp.float32
BF16 = jnp.bfloat16
SIDE = 32
SUBS = 384
PLANE = 16
COLUMN = 8
LEVS = 6
EACH = 3
LINE = 4
ROWS = 8 * SIDE

SHIFT = 1.28
SIGMA = 3.0
LOW = 32.0 * 0.06486 + SHIFT
TOP = 32.0 * 8.0 + SHIFT
RHO = 0.7681 / LOW
CHEB = 7


def roll(x, shift, axis):
    return pltpu.roll(x, shift, axis)


def iota(shape, dim):
    return lax.broadcasted_iota(jnp.int32, shape, dim)


def dot(a, b):
    return jnp.dot(a, b, preferred_element_type=F32)


def split(x, n):
    parts = []
    for _ in range(n):
        part = x.astype(BF16)
        parts.append(part)
        x = x - part.astype(F32)
    return parts


def pick(onehot, x):
    a, b, c = split(x, 3)
    return dot(onehot, a) + dot(onehot, b) + dot(onehot, c)


def spread(x, onehot):
    a, b, c = split(x, 3)
    return dot(a, onehot) + dot(b, onehot) + dot(c, onehot)


def mm3(a, b):
    ah, al = a
    bh, bl = b
    return dot(ah, bh) + (dot(ah, bl) + dot(al, bh))


def np_split(x):
    hi = x.astype(np.float32).astype(jnp.bfloat16)
    lo = (x - hi.astype(np.float64)).astype(np.float32).astype(jnp.bfloat16)
    return hi, lo


def polynomial():
    deg = 7
    nodes = np.cos(np.pi * (np.arange(deg + 1) + 0.5) / (deg + 1))
    g = 4.0 * nodes
    x = 128.0 + SHIFT - 32.0 * g

    def cheb(n, t):
        return np.where(
            np.abs(t) <= 1,
            np.cos(n * np.arccos(np.clip(t, -1, 1))),
            np.sign(t) ** n * np.cosh(n * np.arccosh(np.maximum(np.abs(t), 1))),
        )

    def tau(v):
        return (TOP + LOW - 2 * v) / (TOP - LOW)

    top = cheb(deg + 1, tau(0.0))
    vals = (1.0 - cheb(deg + 1, tau(x)) / top) / x
    coef = np.polynomial.polynomial.polyfit(nodes, vals, deg)
    at_one = np.polynomial.polynomial.polyval(1.0, coef)
    const = (1.0 / (SHIFT + SIGMA) - at_one) / SUBS
    return [float(c / 4.0**k) for k, c in enumerate(coef)], float(const), float(1.0 / top)


def constants():
    o = np.arange(SIDE) + 1.0
    step = math.pi / (SIDE + 1.0)
    sine = math.sqrt(2.0 / (SIDE + 1.0)) * np.sin(step * o[:, None] * o[None, :])
    lam = 2.0 - 2.0 * np.cos(step * o)
    inv = np.repeat(1.0 / (lam[:, None] + lam[None, :]), 8, axis=0)
    lanes = np.arange(128)
    side, kk = lanes // SIDE, lanes % SIDE
    m = np.arange(SUBS)
    cmp = ((lanes // 8)[:, None] == (m // EACH % PLANE)[None]) & ((lanes % 8)[:, None] == (m % EACH)[None])
    rev = (side[:, None] == side[None]) & (kk[:, None] == 31 - kk[None])
    s8 = np.concatenate(np_split(np.kron(sine, np.eye(8))), axis=0)
    s = np.concatenate([np.pad(a, ((0, 0), (0, 128 - SIDE))) for a in np_split(sine)], axis=0)
    small = np.concatenate([s, rev.astype(np.float32).astype(jnp.bfloat16)], axis=0)
    wide = cmp.astype(np.float32).astype(jnp.bfloat16)
    return s8, small, wide, inv.astype(np.float32)


def by_row(v):
    return v.reshape(SIDE, 8, 128)


def stack_fields(first, second):
    return jnp.concatenate([first, second, jnp.zeros((2, first.shape[1]), F32)], axis=0)


def to_field(x):
    lane = iota((8, 128), 1)
    rows = []
    for i in range(SIDE):
        g, h = i // 4, i % 4
        part = x[:, 128 * g : 128 * g + 128]
        part = part if h == 0 else roll(part, 128 - 32 * h, 1)
        rows.append(jnp.where(lane < SIDE, part, 0.0))
    return jnp.concatenate(rows, axis=0)


def from_field(v):
    parts = []
    for g in range(8):
        total = v[4 * g]
        for h in (1, 2, 3):
            total = total + roll(v[4 * g + h], 32 * h, 1)
        parts.append(total)
    return jnp.concatenate(parts, axis=1)


def local_part(r, c):
    v = mm3(c["s8"], split(r[:, :SIDE], 2))
    v = mm3(split(v, 2), c["s"])[:, :SIDE] * c["inv"]
    v = mm3(split(v, 2), c["s"])
    v = mm3(c["s8"], split(v, 2))
    f = by_row(v)
    lane = iota((8, 128), 1)
    right = jnp.zeros((8, 128), F32)
    left = jnp.zeros((8, 128), F32)
    for i in range(SIDE):
        moved = roll(f[i], i + 1, 1)
        right = jnp.where(lane == 32 + i, moved, right)
        left = jnp.where(lane == 1 + i, moved, left)
    rims = (f[0] + roll(f[31], 64, 1)) + (right + roll(left, 95, 1))
    return v, rims


def packed(v, q):
    total = jnp.sum(jnp.sum(by_row(v), axis=0), axis=1, keepdims=True)
    at = iota((8, 128), 1) == q * 8 + iota((8, 128), 0)
    return jnp.sum(jnp.where(at, total, 0.0), axis=0, keepdims=True)


def tile_a(rims, sums, mass):
    row = iota((8, 128), 0)
    return jnp.where(row == 6, sums, jnp.where(row == 7, mass, rims))


def tables(nb, ns, fl, t):
    plane, q = t // PLANE, t % PLANE
    row, lane = iota((72, SUBS), 0), iota((72, SUBS), 1)
    y = jnp.where(row < 64, lax.shift_right_logical(row, jnp.int32(3)), plane)
    field = row & 7
    sub = (y * PLANE + q) * EACH + jnp.where(field >= EACH, field - EACH, field)
    take = (lane == sub) & (field < 6)

    def column(a, s):
        return jnp.sum(jnp.where(take, a[s : s + 1].astype(F32), 0.0), axis=1, keepdims=True)

    nbs = [column(nb, s).astype(jnp.int32) for s in range(4)]
    nss = [column(ns, s).astype(jnp.int32) for s in range(4)]
    fls = [column(fl, s) for s in range(4)]

    field = iota((64, 1), 0) & 7
    third = jnp.where(field >= EACH, EACH, 0)
    cols = iota((64, 512), 1)
    choose = []
    for s in range(4):
        sub = nbs[s][:64]
        device = lax.shift_right_logical(sub * 21846, jnp.int32(16))
        at = ((s - nss[s][:64]) & 3) * 128 + (device & 15) * 8 + (sub - EACH * device) + third
        inside = (lax.shift_right_logical(device, jnp.int32(4)) == plane) & (field < 6)
        choose.append((cols == jnp.where(inside, at, -1)).astype(F32).astype(BF16))

    field, lane = iota((8, SUBS), 0), iota((8, SUBS), 1)
    own = (lane == t * EACH + jnp.where(field >= EACH, field - EACH, field)).astype(F32)
    rows = []
    for s in range(4):
        rows.append(jnp.where(field < 6, own - (lane == nbs[s][64:72]).astype(F32), 0.0))
    rows.append(jnp.where(field < 6, own, jnp.where(field == 6, 1.0, 0.0)))
    group = lax.shift_right_logical(iota((8, 128), 1), jnp.int32(5))
    flip = jnp.zeros((8, 128), F32)
    for s in range(4):
        flip = jnp.where(group == s, fls[s][64:72], flip)
    return jnp.concatenate(choose, axis=0), jnp.concatenate(rows, axis=0).astype(BF16), flip


def tiles_b(buf, choose):
    flat = buf.reshape(128, 128)
    turned = jnp.concatenate([flat] + [roll(flat, 32 * t, 1) for t in (1, 2, 3)], axis=0)
    got = pick(choose, turned)
    group = lax.shift_right_logical(iota((64, 128), 1), jnp.int32(5))
    out = jnp.where(group == 0, got[:64], 0.0)
    for s in (1, 2, 3):
        out = jnp.where(group == s, got[64 * s : 64 * s + 64], out)
    row = iota((8, 128), 0)
    plane = jnp.where(row >= 6, jnp.sum(buf, axis=0), 0.0)
    return out.reshape(8, 8, 128) + plane[None]


def graph(nb):
    row = iota((SUBS, SUBS), 0)
    total = jnp.zeros((SUBS, SUBS), F32)
    for s in range(4):
        total = total + (row == nb[s : s + 1]).astype(F32)
    return total


def start_inverse(g32):
    coef, const, rho = polynomial()
    g = g32.astype(BF16)
    g2 = dot(g, g)
    g2b = g2.astype(BF16)
    g3 = dot(g2b, g)
    g4 = dot(g2b, g2b)
    g3b, g4b = g3.astype(BF16), g4.astype(BF16)
    eye = (iota((SUBS, SUBS), 0) == iota((SUBS, SUBS), 1)).astype(F32)
    x = coef[0] * eye + const + coef[1] * g32 + coef[2] * g2 + coef[3] * g3 + coef[4] * g4
    x = x + coef[5] * dot(g4b, g) + coef[6] * dot(g4b, g2b) + coef[7] * dot(g4b, g3b)
    return x, rho


def newton(x, g, rho, last):
    xs = split(x, 3)
    gx = dot(g, xs[0]) + (dot(g, xs[1]) + dot(g, xs[2]))
    ones = (SIGMA / SUBS) * jnp.sum(x, axis=0, keepdims=True)
    eye = (iota((SUBS, SUBS), 0) == iota((SUBS, SUBS), 1)).astype(F32)
    rest = eye - ((128.0 + SHIFT) * x - 32.0 * gx + ones)
    x = x + mm3(xs[:2], split(rest, 2))
    if last:
        return x, 0.0
    scale = 2.0 / (2.0 - rho * rho)
    return scale * x, rho * rho / (2.0 - rho * rho)


def to_vectors(slots, c):
    wide = spread(slots, c["cmp"])
    rows = []
    for k in range(slots.shape[0] // 8):
        row, lane = iota((8, SUBS), 0), iota((8, SUBS), 1)
        keep = (lane >= row * 48) & (lane < row * 48 + 48)
        rows.append(jnp.sum(jnp.where(keep, wide[8 * k : 8 * k + 8], 0.0), axis=0, keepdims=True))
    return rows


def inverse_rows(first, xh, xl, mass):
    delta = mass - SHIFT

    def apply(d, fine):
        e = d * delta
        eh, el = split(e, 2)
        if fine:
            return d + (dot(eh, xh) + (dot(el, xh) + dot(eh, xl)))
        return d + dot(eh, xh)

    sig = 1.0 / RHO
    rk = 1.0 / sig
    rest = first
    d = rest
    y = d
    for k in range(CHEB):
        rest = rest - apply(d, k < 4)
        nxt = 1.0 / (2.0 * sig - rk)
        d = (nxt * rk) * d + (2.0 * nxt / RHO) * rest
        y = y + d
        rk = nxt
    u = y[38:39]
    t = jnp.sum(u, axis=1, keepdims=True)
    w = jnp.sum(y, axis=1, keepdims=True)
    share = (SIGMA / SUBS) / (1.0 - (SIGMA / SUBS) * t)
    return y + (w * share) * u


def coarse_parts(y, s0, s1):
    row = iota((8, SUBS), 0)
    s = jnp.where(row < EACH, s0, s1)
    group = lax.shift_right_logical(iota((8, 128), 1), jnp.int32(5))
    edges = jnp.zeros((8, 128), F32)
    for k in range(4):
        edges = jnp.where(group == k, jnp.sum(y[8 * k : 8 * k + 8] * s, axis=1, keepdims=True), edges)
    own = jnp.sum(y[32:40] * s, axis=1, keepdims=True)
    at = (iota((8, 128), 1) < SIDE) & (iota((8, 128), 0) < 6)
    return edges, jnp.where(at, own, 0.0)


def finish(r, local, mass, rims, flip, y, s0, s1, c):
    turned = spread(rims, c["rev"])
    rims = jnp.where(flip > 0.5, turned, rims)
    edges, own = coarse_parts(y, s0, s1)
    e = jnp.where(iota((8, 128), 0) < 6, edges - rims, 0.0)
    lane = iota((8, 128), 1)
    left = roll(e, 33, 1)
    both = jnp.where((lane >= 1) & (lane < 32), left, jnp.where((lane >= 32) & (lane < 64), e, 0.0))
    f, fr, fm = by_row(local), by_row(r), by_row(mass)
    z, image = [], []
    for i in range(SIDE):
        zi = f[i] + own
        moved = roll(both, 127 - i, 1)
        if i == 31:
            moved = jnp.where(lane == 0, roll(left, 96, 1), moved)
        extra = jnp.where((lane == 0) | (lane == 31), moved, 0.0)
        if i == 0:
            extra = extra + jnp.where(lane < SIDE, e, 0.0)
        if i == 31:
            extra = extra + jnp.where(lane < SIDE, roll(e, 64, 1), 0.0)
        z.append(zi)
        image.append(fr[i] + fm[i] * zi + extra)
    return jnp.concatenate(z, axis=0), jnp.concatenate(image, axis=0)


def dots_row(pairs):
    lane, row = iota((8, 128), 1), iota((8, 128), 0)
    total = jnp.zeros((8, 128), F32)
    for k, (a, b) in enumerate(pairs):
        one = jnp.sum(jnp.sum(by_row(a * b), axis=0), axis=1, keepdims=True)
        at = ((lane == k) & (row < EACH)) | ((lane == 6 + k) & (row >= EACH) & (row < 6))
        total = jnp.where(at, one, total)
    return jnp.sum(total, axis=0, keepdims=True)


def steps(row, p):
    ga, de, rw, qw, zv, wv = [row[:, 6 * p + k : 6 * p + k + 1] for k in range(6)]
    a0 = ga / de
    g1 = ga - a0 * (de + rw) + a0 * a0 * qw
    d1 = de - a0 * (qw + zv) + a0 * a0 * wv
    beta = g1 / ga
    cross = de - a0 * (0.5 * (qw + zv))
    den = d1 + 2.0 * beta * cross + beta * beta * de
    a1 = g1 / den
    return a0 + a1 * (1.0 + beta), a1 * a0


def kernel(src_hbm, mass_hbm, nb_hbm, ns_hbm, fl_hbm, s8_hbm, small_hbm, wide_hbm, inv_hbm, sol_hbm, res_hbm,
           src_v, mass_v, nb_v, ns_v, fl_v, s8_v, small_v, wide_v, inv_v,
           r_v, m_v, l_v, choose_v, e0_v, flip_v, x_v, g_v, xh_v, xl_v, first_v,
           stga0, stga1, bufa0, bufa1, stgb0, stgb1, bufb0, bufb1, st3a, st3b, buf3a, buf3b,
           out_v, insem, outsem, ssem, rsem):
    t = lax.axis_index("tile")
    lev = lax.axis_index("lev")
    plane, q = t // PLANE, t % PLANE
    line, x_at = q // LINE, q % LINE
    ready = t >= 0

    def at(dy, dz, dx, dl):
        where = ((plane + dy) % COLUMN * LINE + (line + dz) % LINE) * LINE + (x_at + dx) % LINE
        return (where, (lev + dl) % LEVS)

    a_peers = [(0, dz, dx, 0) for dz in (3, 2, 1, 0) for dx in (2, 1, 3, 0) if dz or dx]
    b_peers = [(dy, 0, 0, 0) for dy in (4, 3, 5, 2, 6, 1, 7)]
    xy_peers = [(dy, 0, dx, 0) for dy in (4, 3, 5, 2, 6, 1, 7, 0) for dx in (2, 1, 3, 0) if dy or dx]
    zc_peers = [(0, dz, 0, dl) for dz in (3, 2, 1, 0) for dl in range(LEVS) if dz or dl]
    everyone = list(dict.fromkeys(xy_peers + zc_peers + a_peers))

    moves = [(src_hbm.at[p, n], src_v.at[pl.ds(p * EACH + n, 1)]) for p in range(2) for n in range(EACH)]
    moves += [(mass_hbm, mass_v), (s8_hbm, s8_v), (small_hbm, small_v), (inv_hbm, inv_v),
              (nb_hbm, nb_v), (ns_hbm, ns_v), (fl_hbm, fl_v), (wide_hbm, wide_v)]
    copies = [pltpu.make_async_copy(a, b, insem.at[k]) for k, (a, b) in enumerate(moves)]
    for copy in copies:
        copy.start()

    barrier = pltpu.get_barrier_semaphore()
    for peer in everyone:
        pl.semaphore_signal(barrier, 1, device_id=at(*peer), device_id_type=pl.DeviceIdType.MESH)

    for copy in copies:
        copy.wait()

    def send(peers, src_of, dst, n):
        for peer in peers:
            pltpu.make_async_remote_copy(
                src_ref=src_of(peer), dst_ref=dst, send_sem=ssem.at[n], recv_sem=rsem.at[n],
                device_id=at(*peer), device_id_type=pl.DeviceIdType.MESH,
            ).start()

    def done(peers, buf, n, recv):
        view = buf.at[pl.ds(0, len(peers))]
        copy = pltpu.make_async_remote_copy(
            src_ref=view, dst_ref=view, send_sem=ssem.at[n], recv_sem=rsem.at[n],
            device_id=at(*peers[0]), device_id_type=pl.DeviceIdType.MESH,
        )
        if recv:
            copy.wait_recv()
        else:
            copy.wait_send()

    def consts():
        return {
            "s8": (s8_v[:256], s8_v[256:]),
            "s": (small_v[:SIDE], small_v[SIDE : 2 * SIDE]),
            "rev": small_v[2 * SIDE :],
            "inv": inv_v[...],
            "cmp": wide_v[...],
        }

    c = consts()
    zrow = jnp.zeros((1, 128), F32)

    first = src_v[...]
    r = to_field(jnp.where(iota(first.shape, 0) < 6, first, 0.0))
    mass = to_field(stack_fields(mass_v[...], mass_v[...]))
    r_v[...] = r
    m_v[...] = mass
    l0, rims = local_part(r, c)
    l_v[...] = l0
    tile = tile_a(rims, packed(r, q), packed(mass, q))
    stga0[...] = tile
    bufa0[q] = tile
    pl.semaphore_wait(barrier, len(everyone))
    send(a_peers, lambda peer: stga0, bufa0.at[q], 0)

    polys = polynomial()[2]
    rhos = [polys]
    for _ in range(2):
        rhos.append(rhos[-1] ** 2 / (2.0 - rhos[-1] ** 2))

    @pl.when(ready)
    def _():
        choose, e0, flip = tables(nb_v[...], ns_v[...], fl_v[...], t)
        choose_v[...] = choose
        e0_v[...] = e0
        flip_v[...] = flip
        g32 = graph(nb_v[...])
        g_v[...] = g32.astype(BF16)
        x_v[...] = start_inverse(g32)[0]

    @pl.when(ready)
    def _():
        x_v[...] = newton(x_v[...], g_v[...], rhos[0], False)[0]

    done(a_peers, bufa0, 0, True)
    stgb0[...] = tiles_b(bufa0[...], choose_v[...])
    bufb0[plane] = stgb0[plane]
    send(b_peers, lambda peer: stgb0.at[(plane + peer[0]) % COLUMN], bufb0.at[plane], 1)

    @pl.when(ready)
    def _():
        x_v[...] = newton(x_v[...], g_v[...], rhos[1], False)[0]

    @pl.when(ready)
    def _():
        x = newton(x_v[...], g_v[...], rhos[2], True)[0]
        xs = split(x, 3)
        e0 = e0_v[...]
        first_v[...] = dot(e0, xs[0]) + (dot(e0, xs[1]) + dot(e0, xs[2]))
        xh_v[...] = xs[0]
        xl_v[...] = xs[1]

    done(b_peers, bufb0, 1, True)
    c = consts()
    flip = flip_v[...]
    r, mass = r_v[...], m_v[...]
    sums = bufb0[:, 6, :]
    three = jnp.concatenate([bufb0[:, 7, :], sums, roll(sums, 128 - EACH, 1)], axis=0)
    dvec, s0, s1 = to_vectors(three, c)
    y = inverse_rows(first_v[...], xh_v[...], xl_v[...], dvec)
    z0, q0 = finish(r, l_v[...], mass, jnp.sum(bufb0[...], axis=0), flip, y, s0, s1, c)

    l1, rims = local_part(q0, c)
    tile = tile_a(rims, packed(q0, q), zrow)
    stga1[...] = tile
    bufa1[q] = tile
    send(a_peers, lambda peer: stga1, bufa1.at[q], 2)
    done(a_peers, bufa1, 2, True)
    stgb1[...] = tiles_b(bufa1[...], choose_v[...])
    bufb1[plane] = stgb1[plane]
    send(b_peers, lambda peer: stgb1.at[(plane + peer[0]) % COLUMN], bufb1.at[plane], 3)
    done(b_peers, bufb1, 3, True)
    sums = bufb1[:, 6, :]
    s0, s1 = to_vectors(jnp.concatenate([sums, roll(sums, 128 - EACH, 1)], axis=0), c)
    w, v = finish(q0, l1, mass, jnp.sum(bufb1[...], axis=0), flip, y, s0, s1, c)

    row = dots_row(((r, z0), (z0, q0), (r, w), (q0, w), (z0, v), (w, v)))
    for n, (peers, me, stg, buf) in enumerate(
        ((xy_peers, plane * LINE + x_at, st3a, buf3a), (zc_peers, line * LEVS + lev, st3b, buf3b))
    ):
        stg[...] = row
        buf[me] = row
        send(peers, lambda peer: stg, buf.at[me], 4 + n)
        done(peers, buf, 4 + n, True)
        row = jnp.sum(buf[...], axis=0)

    upper = iota((8, 128), 0) < EACH
    a0, b0 = steps(row, 0)
    a1, b1 = steps(row, 1)
    a, b = jnp.where(upper, a0, a1), jnp.where(upper, b0, b1)
    outs = [
        from_field(a[None] * by_row(z0) - b[None] * by_row(w)),
        from_field(by_row(r) - a[None] * by_row(q0) + b[None] * by_row(v)),
    ]
    last = []
    for k, (out, dst) in enumerate(zip(outs, (sol_hbm, res_hbm))):
        out_v[k] = out
        for p in range(2):
            for n in range(EACH):
                last.append(pltpu.make_async_copy(
                    out_v.at[k, pl.ds(p * EACH + n, 1)], dst.at[p, n], outsem.at[len(last)]))
    for copy in last:
        copy.start()
    for copy in last:
        copy.wait()

    done(a_peers, bufa0, 0, False)
    done(b_peers, bufb0, 1, False)
    done(a_peers, bufa1, 2, False)
    done(b_peers, bufb1, 3, False)
    done(xy_peers, buf3a, 4, False)
    done(zc_peers, buf3b, 5, False)


def shards(sources, mass_coef, neighbour_sub, neighbour_side, side_flip):
    s8, small, wide, inv = [jnp.asarray(a) for a in constants()]
    hbm = pl.BlockSpec(memory_space=pltpu.HBM)
    rows = sources.transpose(0, 2, 1, 3)
    args = [rows, mass_coef, neighbour_sub.T, neighbour_side.T, side_flip.T, s8, small, wide, inv]
    one = pltpu.VMEM((8, 128), F32)
    line = pltpu.VMEM((1, 128), F32)
    field = pltpu.VMEM((ROWS, 128), F32)
    square = lambda kind: pltpu.VMEM((SUBS, SUBS), kind)
    plane = pltpu.VMEM((PLANE, 8, 128), F32)
    column = pltpu.VMEM((COLUMN, 8, 128), F32)
    scratch = [pltpu.VMEM((8, SIDE * SIDE), F32)] + [pltpu.VMEM(a.shape, a.dtype) for a in args[1:]] + [
        field, field, field, pltpu.VMEM((256, 512), BF16), pltpu.VMEM((40, SUBS), BF16), one,
        square(F32), square(BF16), square(BF16), square(BF16), pltpu.VMEM((40, SUBS), F32),
        one, one, plane, plane, column, column, column, column, line, line,
        pltpu.VMEM((COLUMN * LINE, 1, 128), F32), pltpu.VMEM((LINE * LEVS, 1, 128), F32),
        pltpu.VMEM((2, 8, SIDE * SIDE), F32), pltpu.SemaphoreType.DMA((14,)), pltpu.SemaphoreType.DMA((12,)),
        pltpu.SemaphoreType.DMA((6,)), pltpu.SemaphoreType.DMA((6,)),
    ]
    out = jax.ShapeDtypeStruct(rows.shape, F32)
    sol, res = pl.pallas_call(
        kernel,
        out_shape=(out, out),
        in_specs=[hbm] * len(args),
        out_specs=(hbm, hbm),
        scratch_shapes=scratch,
        compiler_params=pltpu.CompilerParams(collective_id=0, has_side_effects=True, vmem_limit_bytes=67043328),
        name="schwarz",
    )(*args)
    return sol.transpose(0, 2, 1, 3), res.transpose(0, 2, 1, 3)


def solution(mesh):
    placed = (P(None, "lev", "tile", None), P("tile", None), P(), P(), P())
    return jax.shard_map(
        shards,
        mesh=mesh,
        in_specs=placed,
        out_specs=(P(None, "lev", "tile", None), P(None, "lev", "tile", None)),
        check_vma=False,
    )
```

```python
import math

import jax
import jax.numpy as jnp
import numpy as np
from jax import lax
from jax.experimental import pallas as pl
from jax.experimental.pallas import tpu as pltpu
from jax.sharding import PartitionSpec as P

F32 = jnp.float32
BF16 = jnp.bfloat16
SIDE = 32
SUBS = 384
PLANE = 16
COLUMN = 8
LEVS = 6
EACH = 3
LINE = 4
ROWS = 8 * SIDE

SHIFT = 1.28
SIGMA = 3.0
LOW = 32.0 * 0.06486 + SHIFT
TOP = 32.0 * 8.0 + SHIFT
RHO = 0.7681 / LOW
CHEB = 6


def roll(x, shift, axis):
    return pltpu.roll(x, shift, axis)


def iota(shape, dim):
    return lax.broadcasted_iota(jnp.int32, shape, dim)


def dot(a, b):
    return jnp.dot(a, b, preferred_element_type=F32)


def split(x, n):
    parts = []
    for _ in range(n):
        part = x.astype(BF16)
        parts.append(part)
        x = x - part.astype(F32)
    return parts


def stack(parts):
    return jnp.concatenate([part.astype(F32) for part in parts], axis=0).astype(BF16)


def spread(x, onehot):
    n = x.shape[0]
    out = dot(stack(split(x, 3)), onehot)
    return out[:n] + out[n : 2 * n] + out[2 * n :]


def mm3(a, b):
    ah, al = a
    bh, bl = b
    return dot(ah, bh) + (dot(ah, bl) + dot(al, bh))


def np_split(x):
    hi = x.astype(np.float32).astype(jnp.bfloat16)
    lo = (x - hi.astype(np.float64)).astype(np.float32).astype(jnp.bfloat16)
    return hi, lo


def polynomial():
    deg = 7
    nodes = np.cos(np.pi * (np.arange(deg + 1) + 0.5) / (deg + 1))
    g = 4.0 * nodes
    x = 128.0 + SHIFT - 32.0 * g

    def cheb(n, t):
        return np.where(
            np.abs(t) <= 1,
            np.cos(n * np.arccos(np.clip(t, -1, 1))),
            np.sign(t) ** n * np.cosh(n * np.arccosh(np.maximum(np.abs(t), 1))),
        )

    def tau(v):
        return (TOP + LOW - 2 * v) / (TOP - LOW)

    top = cheb(deg + 1, tau(0.0))
    vals = (1.0 - cheb(deg + 1, tau(x)) / top) / x
    coef = np.polynomial.polynomial.polyfit(nodes, vals, deg)
    at_one = np.polynomial.polynomial.polyval(1.0, coef)
    const = (1.0 / (SHIFT + SIGMA) - at_one) / SUBS
    return [float(c / 4.0**k) for k, c in enumerate(coef)], float(const), float(1.0 / top)


def constants():
    o = np.arange(SIDE) + 1.0
    step = math.pi / (SIDE + 1.0)
    sine = math.sqrt(2.0 / (SIDE + 1.0)) * np.sin(step * o[:, None] * o[None, :])
    lam = 2.0 - 2.0 * np.cos(step * o)
    inv = np.repeat(1.0 / (lam[:, None] + lam[None, :]), 8, axis=0)
    lanes = np.arange(128)
    side, kk = lanes // SIDE, lanes % SIDE
    m = np.arange(SUBS)
    cmp = ((lanes // 8)[:, None] == (m // EACH // PLANE)[None]) & ((lanes % 8)[:, None] == (m % EACH)[None])
    rev = (side[:, None] == side[None]) & (kk[:, None] == 31 - kk[None])
    s8 = np.concatenate(np_split(np.kron(sine, np.eye(8))), axis=0)
    s = np.concatenate([np.pad(a, ((0, 0), (0, 128 - SIDE))) for a in np_split(sine)], axis=0)
    small = np.concatenate([s, rev.astype(np.float32).astype(jnp.bfloat16)], axis=0)
    wide = cmp.astype(np.float32).astype(jnp.bfloat16)
    return s8, small, wide, inv.astype(np.float32)


def by_row(v):
    return v.reshape(SIDE, 8, 128)


def stack_fields(first, second):
    return jnp.concatenate([first, second, jnp.zeros((2, first.shape[1]), F32)], axis=0)


def to_field(x):
    lane = iota((8, 128), 1)
    rows = []
    for i in range(SIDE):
        g, h = i // 4, i % 4
        part = x[:, 128 * g : 128 * g + 128]
        part = part if h == 0 else roll(part, 128 - 32 * h, 1)
        rows.append(jnp.where(lane < SIDE, part, 0.0))
    return jnp.concatenate(rows, axis=0)


def from_field(v):
    parts = []
    for g in range(8):
        total = v[4 * g]
        for h in (1, 2, 3):
            total = total + roll(v[4 * g + h], 32 * h, 1)
        parts.append(total)
    return jnp.concatenate(parts, axis=1)


def local_part(r, c):
    v = mm3(c["s8"], split(r[:, :SIDE], 2))
    v = mm3(split(v, 2), c["s"])[:, :SIDE] * c["inv"]
    v = mm3(split(v, 2), c["s"])
    v = mm3(c["s8"], split(v, 2))
    f = by_row(v)
    lane = iota((8, 128), 1)
    right = jnp.zeros((8, 128), F32)
    left = jnp.zeros((8, 128), F32)
    for i in range(SIDE):
        moved = roll(f[i], i + 1, 1)
        right = jnp.where(lane == 32 + i, moved, right)
        left = jnp.where(lane == 1 + i, moved, left)
    rims = (f[0] + roll(f[31], 64, 1)) + (right + roll(left, 95, 1))
    return v, rims


def packed(v, place):
    total = jnp.sum(jnp.sum(by_row(v), axis=0), axis=1, keepdims=True)
    at = iota((8, 128), 1) == place * 8 + iota((8, 128), 0)
    return jnp.sum(jnp.where(at, total, 0.0), axis=0, keepdims=True)


def tile_a(rims, sums, mass):
    row = iota((8, 128), 0)
    return jnp.where(row == 6, sums, jnp.where(row == 7, mass, rims))


def tables(nb, ns, fl, t):
    plane, q = t // PLANE, t % PLANE
    row, lane = iota((136, SUBS), 0), iota((136, SUBS), 1)
    target = jnp.where(row < 128, lax.shift_right_logical(row, jnp.int32(3)), q)
    field = row & 7
    sub = (plane * PLANE + target) * EACH + jnp.where(field >= EACH, field - EACH, field)
    take = (lane == sub) & (field < 6)

    def column(a, s):
        return jnp.sum(jnp.where(take, a[s : s + 1].astype(F32), 0.0), axis=1, keepdims=True)

    nbs = [column(nb, s).astype(jnp.int32) for s in range(4)]
    nss = [column(ns, s).astype(jnp.int32) for s in range(4)]
    fls = [column(fl, s) for s in range(4)]

    field = iota((128, 1), 0) & 7
    third = jnp.where(field >= EACH, EACH, 0)
    cols = iota((128, 256), 1)
    choose = []
    for s in range(4):
        sub = nbs[s][:128]
        device = lax.shift_right_logical(sub * 21846, jnp.int32(16))
        at = ((s - nss[s][:128]) & 3) * 64 + lax.shift_right_logical(device, jnp.int32(4)) * 8 + (sub - EACH * device) + third
        inside = ((device & 15) == q) & (field < 6)
        choose.append((cols == jnp.where(inside, at, -1)).astype(F32).astype(BF16))

    field, lane = iota((8, SUBS), 0), iota((8, SUBS), 1)
    own = (lane == t * EACH + jnp.where(field >= EACH, field - EACH, field)).astype(F32)
    rows = []
    for s in range(4):
        rows.append(jnp.where(field < 6, own - (lane == nbs[s][128:136]).astype(F32), 0.0))
    rows.append(jnp.where(field < 6, own, jnp.where(field == 6, 1.0, 0.0)))
    group = lax.shift_right_logical(iota((8, 128), 1), jnp.int32(5))
    flip = jnp.zeros((8, 128), F32)
    for s in range(4):
        flip = jnp.where(group == s, fls[s][128:136], flip)
    return jnp.concatenate(choose, axis=0), jnp.concatenate(rows, axis=0).astype(BF16), flip


def tiles_b(buf, choose):
    flat = buf.reshape(64, 128)
    turned = jnp.concatenate([flat] + [roll(flat, 32 * t, 1) for t in (1, 2, 3)], axis=0)
    a, b, c = split(turned, 3)
    wide = dot(choose, jnp.concatenate([a, b], axis=1))
    got = (wide[:, :128] + wide[:, 128:]) + dot(choose, c)
    group = lax.shift_right_logical(iota((128, 128), 1), jnp.int32(5))
    out = jnp.where(group == 0, got[:128], 0.0)
    for s in (1, 2, 3):
        out = jnp.where(group == s, got[128 * s : 128 * s + 128], out)
    row = iota((8, 128), 0)
    column = jnp.where(row >= 6, jnp.sum(buf, axis=0), 0.0)
    return out.reshape(PLANE, 8, 128) + column[None]


def graph(nb):
    row = iota((SUBS, SUBS), 0)
    total = jnp.zeros((SUBS, SUBS), F32)
    for s in range(4):
        total = total + (row == nb[s : s + 1]).astype(F32)
    return total


def start_inverse(g32):
    coef, const, rho = polynomial()
    g = g32.astype(BF16)
    g2 = dot(g, g)
    g2b = g2.astype(BF16)
    g3 = dot(g2b, g)
    g4 = dot(g2b, g2b)
    g3b, g4b = g3.astype(BF16), g4.astype(BF16)
    eye = (iota((SUBS, SUBS), 0) == iota((SUBS, SUBS), 1)).astype(F32)
    x = coef[0] * eye + const + coef[1] * g32 + coef[2] * g2 + coef[3] * g3 + coef[4] * g4
    x = x + coef[5] * dot(g4b, g) + coef[6] * dot(g4b, g2b) + coef[7] * dot(g4b, g3b)
    return x, rho


def newton(x, g, rho, last):
    xs = split(x, 3)
    gx = dot(g, xs[0]) + (dot(g, xs[1]) + dot(g, xs[2]))
    ones = (SIGMA / SUBS) * jnp.sum(x, axis=0, keepdims=True)
    eye = (iota((SUBS, SUBS), 0) == iota((SUBS, SUBS), 1)).astype(F32)
    rest = eye - ((128.0 + SHIFT) * x - 32.0 * gx + ones)
    x = x + mm3(xs[:2], split(rest, 2))
    if last:
        return x, 0.0
    scale = 2.0 / (2.0 - rho * rho)
    return scale * x, rho * rho / (2.0 - rho * rho)


def to_vectors(slots, c):
    wide = spread(slots, c["cmp"])
    row, lane = iota((PLANE, SUBS), 0), iota((PLANE, SUBS), 1)
    keep = (lax.shift_right_logical(lane * 21846, jnp.int32(16)) & 15) == row
    rows = []
    for k in range(slots.shape[0] // PLANE):
        block = wide[PLANE * k : PLANE * k + PLANE]
        rows.append(jnp.sum(jnp.where(keep, block, 0.0), axis=0, keepdims=True))
    return rows


def inverse_rows(first, xh, xl, mass):
    delta = mass - SHIFT

    def apply(d, fine):
        e = d * delta
        if not fine:
            return d + dot(e.astype(BF16), xh)
        eh, el = split(e, 2)
        n = e.shape[0]
        high = dot(stack([eh, el]), xh)
        return d + (high[:n] + (high[n:] + dot(eh, xl)))

    sig = 1.0 / RHO
    rk = 1.0 / sig
    rest = first
    d = rest
    y = d
    for k in range(CHEB):
        rest = rest - apply(d, k < 3)
        nxt = 1.0 / (2.0 * sig - rk)
        d = (nxt * rk) * d + (2.0 * nxt / RHO) * rest
        y = y + d
        rk = nxt
    u = y[38:39]
    t = jnp.sum(u, axis=1, keepdims=True)
    w = jnp.sum(y, axis=1, keepdims=True)
    share = (SIGMA / SUBS) / (1.0 - (SIGMA / SUBS) * t)
    return y + (w * share) * u


def coarse_parts(y, s0, s1):
    row = iota((8, SUBS), 0)
    s = jnp.where(row < EACH, s0, s1)
    group = lax.shift_right_logical(iota((8, 128), 1), jnp.int32(5))
    edges = jnp.zeros((8, 128), F32)
    for k in range(4):
        edges = jnp.where(group == k, jnp.sum(y[8 * k : 8 * k + 8] * s, axis=1, keepdims=True), edges)
    own = jnp.sum(y[32:40] * s, axis=1, keepdims=True)
    at = (iota((8, 128), 1) < SIDE) & (iota((8, 128), 0) < 6)
    return edges, jnp.where(at, own, 0.0)


def finish(r, local, mass, rims, flip, y, s0, s1, c):
    turned = spread(rims, c["rev"])
    rims = jnp.where(flip > 0.5, turned, rims)
    edges, own = coarse_parts(y, s0, s1)
    e = jnp.where(iota((8, 128), 0) < 6, edges - rims, 0.0)
    lane = iota((8, 128), 1)
    left = roll(e, 33, 1)
    both = jnp.where((lane >= 1) & (lane < 32), left, jnp.where((lane >= 32) & (lane < 64), e, 0.0))
    f, fr, fm = by_row(local), by_row(r), by_row(mass)
    z, image = [], []
    for i in range(SIDE):
        zi = f[i] + own
        moved = roll(both, 127 - i, 1)
        if i == 31:
            moved = jnp.where(lane == 0, roll(left, 96, 1), moved)
        extra = jnp.where((lane == 0) | (lane == 31), moved, 0.0)
        if i == 0:
            extra = extra + jnp.where(lane < SIDE, e, 0.0)
        if i == 31:
            extra = extra + jnp.where(lane < SIDE, roll(e, 64, 1), 0.0)
        z.append(zi)
        image.append(fr[i] + fm[i] * zi + extra)
    return jnp.concatenate(z, axis=0), jnp.concatenate(image, axis=0)


def dots_row(pairs):
    lane, row = iota((8, 128), 1), iota((8, 128), 0)
    total = jnp.zeros((8, 128), F32)
    for k, (a, b) in enumerate(pairs):
        one = jnp.sum(jnp.sum(by_row(a * b), axis=0), axis=1, keepdims=True)
        at = ((lane == k) & (row < EACH)) | ((lane == 6 + k) & (row >= EACH) & (row < 6))
        total = jnp.where(at, one, total)
    return jnp.sum(total, axis=0, keepdims=True)


def steps(row, p):
    ga, de, rw, qw, zv, wv = [row[:, 6 * p + k : 6 * p + k + 1] for k in range(6)]
    a0 = ga / de
    g1 = ga - a0 * (de + rw) + a0 * a0 * qw
    d1 = de - a0 * (qw + zv) + a0 * a0 * wv
    beta = g1 / ga
    cross = de - a0 * (0.5 * (qw + zv))
    den = d1 + 2.0 * beta * cross + beta * beta * de
    a1 = g1 / den
    return a0 + a1 * (1.0 + beta), a1 * a0


def kernel(src_hbm, mass_hbm, nb_hbm, ns_hbm, fl_hbm, s8_hbm, small_hbm, wide_hbm, inv_hbm, out_hbm,
           src_v, mass_v, nb_v, ns_v, fl_v, s8_v, small_v, wide_v, inv_v,
           r_v, m_v, l_v, choose_v, e0_v, flip_v, x_v, g_v, xh_v, xl_v, first_v,
           stga0, stga1, bufa0, bufa1, stgb0, stgb1, bufb0, bufb1, st3a, st3b, buf3a, buf3b,
           out_v, nat_v, insem, outsem, ssem, rsem):
    t = lax.axis_index("tile")
    lev = lax.axis_index("lev")
    plane, q = t // PLANE, t % PLANE
    line, x_at = q // LINE, q % LINE
    ready = t >= 0

    def at(dy, dz, dx, dl):
        where = ((plane + dy) % COLUMN * LINE + (line + dz) % LINE) * LINE + (x_at + dx) % LINE
        return (where, (lev + dl) % LEVS)

    a_peers = [(dy, 0, 0, 0) for dy in (4, 3, 5, 2, 6, 1, 7)]
    b_peers = [(0, dz, dx, 0) for dz in (3, 2, 1, 0) for dx in (2, 1, 3, 0) if dz or dx]
    xy_peers = [(dy, 0, dx, 0) for dy in (4, 3, 5, 2, 6, 1, 7, 0) for dx in (2, 1, 3, 0) if dy or dx]
    zc_peers = [(0, dz, 0, dl) for dz in (3, 2, 1, 0) for dl in range(LEVS) if dz or dl]
    everyone = list(dict.fromkeys(a_peers + b_peers + xy_peers + zc_peers))

    moves = [(src_hbm.at[p, n], src_v.at[pl.ds(p * EACH + n, 1)]) for p in range(2) for n in range(EACH)]
    moves += [(mass_hbm, mass_v), (s8_hbm, s8_v), (small_hbm, small_v), (inv_hbm, inv_v),
              (nb_hbm, nb_v), (ns_hbm, ns_v), (fl_hbm, fl_v), (wide_hbm, wide_v)]
    copies = [pltpu.make_async_copy(a, b, insem.at[k]) for k, (a, b) in enumerate(moves)]
    for copy in copies:
        copy.start()

    barrier = pltpu.get_barrier_semaphore()
    for peer in everyone:
        pl.semaphore_signal(barrier, 1, device_id=at(*peer), device_id_type=pl.DeviceIdType.MESH)

    for copy in copies:
        copy.wait()

    def spot(peer):
        return (line + peer[1]) % LINE * LINE + (x_at + peer[2]) % LINE

    def send(peers, src_of, dst, n):
        for peer in peers:
            pltpu.make_async_remote_copy(
                src_ref=src_of(peer), dst_ref=dst, send_sem=ssem.at[n], recv_sem=rsem.at[n],
                device_id=at(*peer), device_id_type=pl.DeviceIdType.MESH,
            ).start()

    def done(peers, buf, n, recv):
        view = buf.at[pl.ds(0, len(peers))]
        copy = pltpu.make_async_remote_copy(
            src_ref=view, dst_ref=view, send_sem=ssem.at[n], recv_sem=rsem.at[n],
            device_id=at(*peers[0]), device_id_type=pl.DeviceIdType.MESH,
        )
        if recv:
            copy.wait_recv()
        else:
            copy.wait_send()

    def consts():
        return {
            "s8": (s8_v[:256], s8_v[256:]),
            "s": (small_v[:SIDE], small_v[SIDE : 2 * SIDE]),
            "rev": small_v[2 * SIDE :],
            "inv": inv_v[...],
            "cmp": wide_v[...],
        }

    c = consts()
    zrow = jnp.zeros((1, 128), F32)

    first = src_v[...]
    r = to_field(jnp.where(iota(first.shape, 0) < 6, first, 0.0))
    mass = to_field(stack_fields(mass_v[...], mass_v[...]))
    r_v[...] = r
    m_v[...] = mass
    l0, rims = local_part(r, c)
    l_v[...] = l0
    tile = tile_a(rims, packed(r, plane), packed(mass, plane))
    stga0[...] = tile
    bufa0[plane] = tile
    pl.semaphore_wait(barrier, len(everyone))
    send(a_peers, lambda peer: stga0, bufa0.at[plane], 0)

    polys = polynomial()[2]
    rhos = [polys]
    for _ in range(2):
        rhos.append(rhos[-1] ** 2 / (2.0 - rhos[-1] ** 2))

    @pl.when(ready)
    def _():
        choose, e0, flip = tables(nb_v[...], ns_v[...], fl_v[...], t)
        choose_v[...] = choose
        e0_v[...] = e0
        flip_v[...] = flip
        g32 = graph(nb_v[...])
        g_v[...] = g32.astype(BF16)
        x_v[...] = start_inverse(g32)[0]

    @pl.when(ready)
    def _():
        x_v[...] = newton(x_v[...], g_v[...], rhos[0], False)[0]

    done(a_peers, bufa0, 0, True)
    stgb0[...] = tiles_b(bufa0[...], choose_v[...])
    bufb0[q] = stgb0[q]
    send(b_peers, lambda peer: stgb0.at[spot(peer)], bufb0.at[q], 1)

    @pl.when(ready)
    def _():
        x_v[...] = newton(x_v[...], g_v[...], rhos[1], False)[0]

    @pl.when(ready)
    def _():
        x = newton(x_v[...], g_v[...], rhos[2], True)[0]
        xs = split(x, 3)
        e0 = e0_v[...]
        first_v[...] = dot(e0, xs[0]) + (dot(e0, xs[1]) + dot(e0, xs[2]))
        xh_v[...] = xs[0]
        xl_v[...] = xs[1]

    done(b_peers, bufb0, 1, True)
    c = consts()
    flip = flip_v[...]
    r, mass = r_v[...], m_v[...]
    sums = bufb0[:, 6, :]
    three = jnp.concatenate([bufb0[:, 7, :], sums, roll(sums, 128 - EACH, 1)], axis=0)
    dvec, s0, s1 = to_vectors(three, c)
    y = inverse_rows(first_v[...], xh_v[...], xl_v[...], dvec)
    z0, q0 = finish(r, l_v[...], mass, jnp.sum(bufb0[...], axis=0), flip, y, s0, s1, c)

    l1, rims = local_part(q0, c)
    tile = tile_a(rims, packed(q0, plane), zrow)
    stga1[...] = tile
    bufa1[plane] = tile
    send(a_peers, lambda peer: stga1, bufa1.at[plane], 2)
    done(a_peers, bufa1, 2, True)
    stgb1[...] = tiles_b(bufa1[...], choose_v[...])
    bufb1[q] = stgb1[q]
    send(b_peers, lambda peer: stgb1.at[spot(peer)], bufb1.at[q], 3)
    done(b_peers, bufb1, 3, True)
    sums = bufb1[:, 6, :]
    s0, s1 = to_vectors(jnp.concatenate([sums, roll(sums, 128 - EACH, 1)], axis=0), c)
    w, v = finish(q0, l1, mass, jnp.sum(bufb1[...], axis=0), flip, y, s0, s1, c)

    row = dots_row(((r, z0), (z0, q0), (r, w), (q0, w), (z0, v), (w, v)))
    st3a[...] = row
    buf3a[plane * LINE + x_at] = row
    send(xy_peers, lambda peer: st3a, buf3a.at[plane * LINE + x_at], 4)

    @pl.when(ready)
    def _():
        for k, field in enumerate((z0, q0, w, v)):
            nat_v[k] = from_field(by_row(field))

    done(xy_peers, buf3a, 4, True)
    row = jnp.sum(buf3a[...], axis=0)
    st3b[...] = row
    buf3b[line * LEVS + lev] = row
    send(zc_peers, lambda peer: st3b, buf3b.at[line * LEVS + lev], 5)
    done(zc_peers, buf3b, 5, True)
    row = jnp.sum(buf3b[...], axis=0)

    upper = iota((8, 1), 0) < EACH
    a0, b0 = steps(row, 0)
    a1, b1 = steps(row, 1)
    a, b = jnp.where(upper, a0, a1), jnp.where(upper, b0, b1)
    outs = [a * nat_v[0] - b * nat_v[2], src_v[...] - a * nat_v[1] + b * nat_v[3]]
    last = []
    for k, (out, dst) in enumerate(zip(outs, (out_hbm.at[0], out_hbm.at[1]))):
        out_v[k] = out
        for p in range(2):
            for n in range(EACH):
                last.append(pltpu.make_async_copy(
                    out_v.at[k, pl.ds(p * EACH + n, 1)], dst.at[p, n], outsem.at[len(last)]))
    for copy in last:
        copy.start()
    for copy in last:
        copy.wait()

    done(a_peers, bufa0, 0, False)
    done(b_peers, bufb0, 1, False)
    done(a_peers, bufa1, 2, False)
    done(b_peers, bufb1, 3, False)
    done(xy_peers, buf3a, 4, False)
    done(zc_peers, buf3b, 5, False)


def shards(sources, mass_coef, neighbour_sub, neighbour_side, side_flip):
    s8, small, wide, inv = [jnp.asarray(a) for a in constants()]
    hbm = pl.BlockSpec(memory_space=pltpu.HBM)
    rows = sources.transpose(0, 2, 1, 3)
    args = [rows, mass_coef, neighbour_sub.T, neighbour_side.T, side_flip.T, s8, small, wide, inv]
    one = pltpu.VMEM((8, 128), F32)
    line = pltpu.VMEM((1, 128), F32)
    field = pltpu.VMEM((ROWS, 128), F32)
    square = lambda kind: pltpu.VMEM((SUBS, SUBS), kind)
    plane = pltpu.VMEM((PLANE, 8, 128), F32)
    column = pltpu.VMEM((COLUMN, 8, 128), F32)
    scratch = [pltpu.VMEM((8, SIDE * SIDE), F32)] + [pltpu.VMEM(a.shape, a.dtype) for a in args[1:]] + [
        field, field, field, pltpu.VMEM((512, 256), BF16), pltpu.VMEM((40, SUBS), BF16), one,
        square(F32), square(BF16), square(BF16), square(BF16), pltpu.VMEM((40, SUBS), F32),
        one, one, column, column, plane, plane, plane, plane, line, line,
        pltpu.VMEM((COLUMN * LINE, 1, 128), F32), pltpu.VMEM((LINE * LEVS, 1, 128), F32),
        pltpu.VMEM((2, 8, SIDE * SIDE), F32), pltpu.VMEM((4, 8, SIDE * SIDE), F32), pltpu.SemaphoreType.DMA((14,)), pltpu.SemaphoreType.DMA((12,)),
        pltpu.SemaphoreType.DMA((6,)), pltpu.SemaphoreType.DMA((6,)),
    ]
    out = jax.ShapeDtypeStruct((2,) + rows.shape, F32)
    both = pl.pallas_call(
        kernel,
        out_shape=out,
        in_specs=[hbm] * len(args),
        out_specs=hbm,
        scratch_shapes=scratch,
        compiler_params=pltpu.CompilerParams(collective_id=0, has_side_effects=True, vmem_limit_bytes=67043328),
        name="schwarz",
    )(*args)
    both = both.transpose(0, 1, 3, 2, 4)
    return both[0], both[1]


def solution(mesh):
    placed = (P(None, "lev", "tile", None), P("tile", None), P(), P(), P())
    return jax.shard_map(
        shards,
        mesh=mesh,
        in_specs=placed,
        out_specs=(P(None, "lev", "tile", None), P(None, "lev", "tile", None)),
        check_vma=False,
    )
```

```python
import math

import jax
import jax.numpy as jnp
import numpy as np
from jax import lax
from jax.experimental import pallas as pl
from jax.experimental.pallas import tpu as pltpu
from jax.sharding import PartitionSpec as P

F32 = jnp.float32
BF16 = jnp.bfloat16
SIDE = 32
SUBS = 384
PLANE = 16
COLUMN = 8
LEVS = 6
EACH = 3
LINE = 4
ROWS = 8 * SIDE

SHIFT = 1.28
SIGMA = 3.0
LOW = 32.0 * 0.06486 + SHIFT
TOP = 32.0 * 8.0 + SHIFT
RHO = 0.7681 / LOW
CHEB = 6


def roll(x, shift, axis):
    return pltpu.roll(x, shift, axis)


def iota(shape, dim):
    return lax.broadcasted_iota(jnp.int32, shape, dim)


def dot(a, b):
    return jnp.dot(a, b, preferred_element_type=F32)


def split(x, n):
    parts = []
    for _ in range(n):
        part = x.astype(BF16)
        parts.append(part)
        x = x - part.astype(F32)
    return parts


def stack(parts):
    return jnp.concatenate([part.astype(F32) for part in parts], axis=0).astype(BF16)


def spread(x, onehot):
    n = x.shape[0]
    out = dot(stack(split(x, 3)), onehot)
    return out[:n] + out[n : 2 * n] + out[2 * n :]


def mm3(a, b):
    ah, al = a
    bh, bl = b
    return dot(ah, bh) + (dot(ah, bl) + dot(al, bh))


def np_split(x):
    hi = x.astype(np.float32).astype(jnp.bfloat16)
    lo = (x - hi.astype(np.float64)).astype(np.float32).astype(jnp.bfloat16)
    return hi, lo


def polynomial():
    deg = 7
    nodes = np.cos(np.pi * (np.arange(deg + 1) + 0.5) / (deg + 1))
    g = 4.0 * nodes
    x = 128.0 + SHIFT - 32.0 * g

    def cheb(n, t):
        return np.where(
            np.abs(t) <= 1,
            np.cos(n * np.arccos(np.clip(t, -1, 1))),
            np.sign(t) ** n * np.cosh(n * np.arccosh(np.maximum(np.abs(t), 1))),
        )

    def tau(v):
        return (TOP + LOW - 2 * v) / (TOP - LOW)

    top = cheb(deg + 1, tau(0.0))
    vals = (1.0 - cheb(deg + 1, tau(x)) / top) / x
    coef = np.polynomial.polynomial.polyfit(nodes, vals, deg)
    at_one = np.polynomial.polynomial.polyval(1.0, coef)
    const = (1.0 / (SHIFT + SIGMA) - at_one) / SUBS
    return [float(c / 4.0**k) for k, c in enumerate(coef)], float(const), float(1.0 / top)


def constants():
    o = np.arange(SIDE) + 1.0
    step = math.pi / (SIDE + 1.0)
    sine = math.sqrt(2.0 / (SIDE + 1.0)) * np.sin(step * o[:, None] * o[None, :])
    lam = 2.0 - 2.0 * np.cos(step * o)
    inv = np.repeat(1.0 / (lam[:, None] + lam[None, :]), 8, axis=0)
    lanes = np.arange(128)
    side, kk = lanes // SIDE, lanes % SIDE
    m = np.arange(SUBS)
    cmp = ((lanes // 8)[:, None] == (m // EACH // PLANE)[None]) & ((lanes % 8)[:, None] == (m % EACH)[None])
    rev = (side[:, None] == side[None]) & (kk[:, None] == 31 - kk[None])
    s8 = np.concatenate(np_split(np.kron(sine, np.eye(8))), axis=0)
    s = np.concatenate([np.pad(a, ((0, 0), (0, 128 - SIDE))) for a in np_split(sine)], axis=0)
    ends = np.zeros((SIDE, 128))
    ends[:, 32:64] = sine[:, 31:32]
    ends[:, 96:] = sine[:, 0:1]
    quad = np.kron(np.eye(4), sine)
    rev = rev.astype(np.float32).astype(jnp.bfloat16)
    small = np.concatenate([s, *np_split(ends), *np_split(quad), rev], axis=0)
    wide = cmp.astype(np.float32).astype(jnp.bfloat16)
    return s8, small, wide, inv.astype(np.float32)


def by_row(v):
    return v.reshape(SIDE, 8, 128)


def stack_fields(first, second):
    return jnp.concatenate([first, second, jnp.zeros((2, first.shape[1]), F32)], axis=0)


def to_field(x):
    lane = iota((8, 128), 1)
    rows = []
    for i in range(SIDE):
        g, h = i // 4, i % 4
        part = x[:, 128 * g : 128 * g + 128]
        part = part if h == 0 else roll(part, 128 - 32 * h, 1)
        rows.append(jnp.where(lane < SIDE, part, 0.0))
    return jnp.concatenate(rows, axis=0)


def from_field(v):
    parts = []
    for g in range(8):
        total = v[4 * g]
        for h in (1, 2, 3):
            total = total + roll(v[4 * g + h], 32 * h, 1)
        parts.append(total)
    return jnp.concatenate(parts, axis=1)


def coefficients(r, c):
    v = mm3(c["s8"], split(r[:, :SIDE], 2))
    return mm3(split(v, 2), c["s"])[:, :SIDE] * c["inv"]


def local_rims(x, c):
    w = by_row(mm3(split(x, 2), c["ends"]))
    f = x.reshape(SIDE, 8, SIDE)
    lane = iota((8, 128), 1) & 63
    scale = [math.sqrt(2.0 / 33.0) * math.sin(math.pi * (i + 1) / 33.0) for i in range(SIDE)]
    even = sum(scale[i] * f[i] for i in range(0, SIDE, 2))
    odd = sum(scale[i] * f[i] for i in range(1, SIDE, 2))
    blank = jnp.zeros((8, SIDE), F32)
    tile = jnp.concatenate([even + odd, blank, even - odd, blank], axis=1)
    for i in range(SIDE):
        tile = jnp.where(lane == 32 + i, w[i], tile)
    th, tl = split(tile, 2)
    qh, ql = c["quad"]
    both = dot(stack([th, tl]), qh)
    return both[:8] + (both[8:] + dot(th, ql))


def local_field(x, c):
    v = mm3(split(x, 2), c["s"])
    return mm3(c["s8"], split(v, 2))


def packed(v, place):
    total = jnp.sum(jnp.sum(by_row(v), axis=0), axis=1, keepdims=True)
    at = iota((8, 128), 1) == place * 8 + iota((8, 128), 0)
    return jnp.sum(jnp.where(at, total, 0.0), axis=0, keepdims=True)


def tile_a(rims, sums, mass):
    row = iota((8, 128), 0)
    return jnp.where(row == 6, sums, jnp.where(row == 7, mass, rims))


def tables(nb, ns, fl, t):
    plane, q = t // PLANE, t % PLANE
    row, lane = iota((136, SUBS), 0), iota((136, SUBS), 1)
    target = jnp.where(row < 128, lax.shift_right_logical(row, jnp.int32(3)), q)
    field = row & 7
    sub = (plane * PLANE + target) * EACH + jnp.where(field >= EACH, field - EACH, field)
    take = (lane == sub) & (field < 6)

    def column(a, s):
        return jnp.sum(jnp.where(take, a[s : s + 1].astype(F32), 0.0), axis=1, keepdims=True)

    nbs = [column(nb, s).astype(jnp.int32) for s in range(4)]
    nss = [column(ns, s).astype(jnp.int32) for s in range(4)]
    fls = [column(fl, s) for s in range(4)]

    field = iota((128, 1), 0) & 7
    third = jnp.where(field >= EACH, EACH, 0)
    cols = iota((128, 256), 1)
    choose = []
    for s in range(4):
        sub = nbs[s][:128]
        device = lax.shift_right_logical(sub * 21846, jnp.int32(16))
        at = ((s - nss[s][:128]) & 3) * 64 + lax.shift_right_logical(device, jnp.int32(4)) * 8 + (sub - EACH * device) + third
        inside = ((device & 15) == q) & (field < 6)
        choose.append((cols == jnp.where(inside, at, -1)).astype(F32).astype(BF16))

    field, lane = iota((8, SUBS), 0), iota((8, SUBS), 1)
    own = (lane == t * EACH + jnp.where(field >= EACH, field - EACH, field)).astype(F32)
    rows = []
    for s in range(4):
        rows.append(jnp.where(field < 6, own - (lane == nbs[s][128:136]).astype(F32), 0.0))
    rows.append(jnp.where(field < 6, own, jnp.where(field == 6, 1.0, 0.0)))
    group = lax.shift_right_logical(iota((8, 128), 1), jnp.int32(5))
    flip = jnp.zeros((8, 128), F32)
    for s in range(4):
        flip = jnp.where(group == s, fls[s][128:136], flip)
    return jnp.concatenate(choose, axis=0), jnp.concatenate(rows, axis=0).astype(BF16), flip


def tiles_b(buf, choose):
    flat = buf.reshape(64, 128)
    turned = jnp.concatenate([flat] + [roll(flat, 32 * t, 1) for t in (1, 2, 3)], axis=0)
    a, b, c = split(turned, 3)
    wide = dot(choose, jnp.concatenate([a, b], axis=1))
    got = (wide[:, :128] + wide[:, 128:]) + dot(choose, c)
    group = lax.shift_right_logical(iota((128, 128), 1), jnp.int32(5))
    out = jnp.where(group == 0, got[:128], 0.0)
    for s in (1, 2, 3):
        out = jnp.where(group == s, got[128 * s : 128 * s + 128], out)
    row = iota((8, 128), 0)
    column = jnp.where(row >= 6, jnp.sum(buf, axis=0), 0.0)
    return out.reshape(PLANE, 8, 128) + column[None]


def graph(nb):
    row = iota((SUBS, SUBS), 0)
    total = jnp.zeros((SUBS, SUBS), F32)
    for s in range(4):
        total = total + (row == nb[s : s + 1]).astype(F32)
    return total


def start_inverse(g32):
    coef, const, rho = polynomial()
    g = g32.astype(BF16)
    g2 = dot(g, g)
    g2b = g2.astype(BF16)
    g3 = dot(g2b, g)
    g4 = dot(g2b, g2b)
    g3b, g4b = g3.astype(BF16), g4.astype(BF16)
    eye = (iota((SUBS, SUBS), 0) == iota((SUBS, SUBS), 1)).astype(F32)
    x = coef[0] * eye + const + coef[1] * g32 + coef[2] * g2 + coef[3] * g3 + coef[4] * g4
    x = x + coef[5] * dot(g4b, g) + coef[6] * dot(g4b, g2b) + coef[7] * dot(g4b, g3b)
    return x, rho


def newton(x, g, rho, last):
    xs = split(x, 3)
    gx = dot(g, xs[0]) + (dot(g, xs[1]) + dot(g, xs[2]))
    ones = (SIGMA / SUBS) * jnp.sum(x, axis=0, keepdims=True)
    eye = (iota((SUBS, SUBS), 0) == iota((SUBS, SUBS), 1)).astype(F32)
    rest = eye - ((128.0 + SHIFT) * x - 32.0 * gx + ones)
    x = x + mm3(xs[:2], split(rest, 2))
    if last:
        return x, 0.0
    scale = 2.0 / (2.0 - rho * rho)
    return scale * x, rho * rho / (2.0 - rho * rho)


def to_vectors(slots, c):
    wide = spread(slots, c["cmp"])
    row, lane = iota((PLANE, SUBS), 0), iota((PLANE, SUBS), 1)
    keep = (lax.shift_right_logical(lane * 21846, jnp.int32(16)) & 15) == row
    rows = []
    for k in range(slots.shape[0] // PLANE):
        block = wide[PLANE * k : PLANE * k + PLANE]
        rows.append(jnp.sum(jnp.where(keep, block, 0.0), axis=0, keepdims=True))
    return rows


def inverse_rows(first, xh, xl, mass):
    delta = mass - SHIFT

    def apply(d, fine):
        e = d * delta
        if not fine:
            return d + dot(e.astype(BF16), xh)
        eh, el = split(e, 2)
        n = e.shape[0]
        high = dot(stack([eh, el]), xh)
        return d + (high[:n] + (high[n:] + dot(eh, xl)))

    sig = 1.0 / RHO
    rk = 1.0 / sig
    rest = first
    d = rest
    y = d
    for k in range(CHEB):
        rest = rest - apply(d, k < 3)
        nxt = 1.0 / (2.0 * sig - rk)
        d = (nxt * rk) * d + (2.0 * nxt / RHO) * rest
        y = y + d
        rk = nxt
    u = y[38:39]
    t = jnp.sum(u, axis=1, keepdims=True)
    w = jnp.sum(y, axis=1, keepdims=True)
    share = (SIGMA / SUBS) / (1.0 - (SIGMA / SUBS) * t)
    return y + (w * share) * u


def coarse_parts(y, s0, s1):
    row = iota((8, SUBS), 0)
    s = jnp.where(row < EACH, s0, s1)
    group = lax.shift_right_logical(iota((8, 128), 1), jnp.int32(5))
    edges = jnp.zeros((8, 128), F32)
    for k in range(4):
        edges = jnp.where(group == k, jnp.sum(y[8 * k : 8 * k + 8] * s, axis=1, keepdims=True), edges)
    own = jnp.sum(y[32:40] * s, axis=1, keepdims=True)
    at = (iota((8, 128), 1) < SIDE) & (iota((8, 128), 0) < 6)
    return edges, jnp.where(at, own, 0.0)


def finish(r, local, mass, rims, flip, edges, own, c):
    turned = spread(rims, c["rev"])
    rims = jnp.where(flip > 0.5, turned, rims)
    e = jnp.where(iota((8, 128), 0) < 6, edges - rims, 0.0)
    lane = iota((8, 128), 1)
    left = roll(e, 33, 1)
    both = jnp.where((lane >= 1) & (lane < 32), left, jnp.where((lane >= 32) & (lane < 64), e, 0.0))
    f, fr, fm = by_row(local), by_row(r), by_row(mass)
    z, image = [], []
    for i in range(SIDE):
        zi = f[i] + own
        moved = roll(both, 127 - i, 1)
        if i == 31:
            moved = jnp.where(lane == 0, roll(left, 96, 1), moved)
        extra = jnp.where((lane == 0) | (lane == 31), moved, 0.0)
        if i == 0:
            extra = extra + jnp.where(lane < SIDE, e, 0.0)
        if i == 31:
            extra = extra + jnp.where(lane < SIDE, roll(e, 64, 1), 0.0)
        z.append(zi)
        image.append(fr[i] + fm[i] * zi + extra)
    return jnp.concatenate(z, axis=0), jnp.concatenate(image, axis=0)


def dots_row(pairs):
    lane, row = iota((8, 128), 1), iota((8, 128), 0)
    total = jnp.zeros((8, 128), F32)
    for k, (a, b) in enumerate(pairs):
        one = jnp.sum(jnp.sum(by_row(a * b), axis=0), axis=1, keepdims=True)
        at = ((lane == k) & (row < EACH)) | ((lane == 6 + k) & (row >= EACH) & (row < 6))
        total = jnp.where(at, one, total)
    return jnp.sum(total, axis=0, keepdims=True)


def steps(row, p):
    ga, de, rw, qw, zv, wv = [row[:, 6 * p + k : 6 * p + k + 1] for k in range(6)]
    a0 = ga / de
    g1 = ga - a0 * (de + rw) + a0 * a0 * qw
    d1 = de - a0 * (qw + zv) + a0 * a0 * wv
    beta = g1 / ga
    cross = de - a0 * (0.5 * (qw + zv))
    den = d1 + 2.0 * beta * cross + beta * beta * de
    a1 = g1 / den
    return a0 + a1 * (1.0 + beta), a1 * a0


def kernel(src_hbm, mass_hbm, nb_hbm, ns_hbm, fl_hbm, s8_hbm, small_hbm, wide_hbm, inv_hbm, out_hbm,
           src_v, mass_v, nb_v, ns_v, fl_v, s8_v, small_v, wide_v, inv_v,
           r_v, m_v, l_v, choose_v, e0_v, flip_v, x_v, g_v, xh_v, xl_v, first_v,
           stga0, stga1, bufa0, bufa1, stgb0, stgb1, bufb0, bufb1, st3a, st3b, buf3a, buf3b,
           out_v, nat_v, stgm, bufm, y_v, edge_v, own_v, insem, outsem, ssem, rsem):
    t = lax.axis_index("tile")
    lev = lax.axis_index("lev")
    plane, q = t // PLANE, t % PLANE
    line, x_at = q // LINE, q % LINE
    ready = t >= 0

    def at(dy, dz, dx, dl):
        where = ((plane + dy) % COLUMN * LINE + (line + dz) % LINE) * LINE + (x_at + dx) % LINE
        return (where, (lev + dl) % LEVS)

    a_peers = [(dy, 0, 0, 0) for dy in (4, 3, 5, 2, 6, 1, 7)]
    b_peers = [(0, dz, dx, 0) for dz in (3, 2, 1, 0) for dx in (2, 1, 3, 0) if dz or dx]
    xy_peers = [(dy, 0, dx, 0) for dy in (4, 3, 5, 2, 6, 1, 7, 0) for dx in (2, 1, 3, 0) if dy or dx]
    zc_peers = [(0, dz, 0, dl) for dz in (3, 2, 1, 0) for dl in range(LEVS) if dz or dl]
    everyone = list(dict.fromkeys(a_peers + b_peers + xy_peers + zc_peers))

    moves = [(src_hbm.at[p, n], src_v.at[pl.ds(p * EACH + n, 1)]) for p in range(2) for n in range(EACH)]
    moves += [(mass_hbm, mass_v), (s8_hbm, s8_v), (small_hbm, small_v), (inv_hbm, inv_v),
              (nb_hbm, nb_v), (ns_hbm, ns_v), (fl_hbm, fl_v), (wide_hbm, wide_v)]
    copies = [pltpu.make_async_copy(a, b, insem.at[k]) for k, (a, b) in enumerate(moves)]
    for copy in copies:
        copy.start()

    barrier = pltpu.get_barrier_semaphore()
    for peer in everyone:
        pl.semaphore_signal(barrier, 1, device_id=at(*peer), device_id_type=pl.DeviceIdType.MESH)

    for copy in copies:
        copy.wait()

    def spot(peer):
        return (line + peer[1]) % LINE * LINE + (x_at + peer[2]) % LINE

    def send(peers, src_of, dst, n):
        for peer in peers:
            pltpu.make_async_remote_copy(
                src_ref=src_of(peer), dst_ref=dst, send_sem=ssem.at[n], recv_sem=rsem.at[n],
                device_id=at(*peer), device_id_type=pl.DeviceIdType.MESH,
            ).start()

    def done(peers, buf, n, recv):
        view = buf.at[pl.ds(0, len(peers))]
        copy = pltpu.make_async_remote_copy(
            src_ref=view, dst_ref=view, send_sem=ssem.at[n], recv_sem=rsem.at[n],
            device_id=at(*peers[0]), device_id_type=pl.DeviceIdType.MESH,
        )
        if recv:
            copy.wait_recv()
        else:
            copy.wait_send()

    def consts():
        return {
            "s8": (s8_v[:256], s8_v[256:]),
            "s": (small_v[:SIDE], small_v[SIDE : 2 * SIDE]),
            "ends": (small_v[64:96], small_v[96:128]),
            "quad": (small_v[128:256], small_v[256:384]),
            "rev": small_v[384:],
            "inv": inv_v[...],
            "cmp": wide_v[...],
        }

    c = consts()
    zrow = jnp.zeros((1, 128), F32)

    first = src_v[...]
    r = to_field(jnp.where(iota(first.shape, 0) < 6, first, 0.0))
    mass = to_field(stack_fields(mass_v[...], mass_v[...]))
    r_v[...] = r
    m_v[...] = mass
    x0 = coefficients(r, c)
    rims = local_rims(x0, c)
    tile = tile_a(rims, packed(r, plane), packed(mass, plane))
    stga0[...] = tile
    bufa0[plane] = tile
    pl.semaphore_wait(barrier, len(everyone))
    send(a_peers, lambda peer: stga0, bufa0.at[plane], 0)

    polys = polynomial()[2]
    rhos = [polys]
    for _ in range(2):
        rhos.append(rhos[-1] ** 2 / (2.0 - rhos[-1] ** 2))

    @pl.when(ready)
    def _():
        l_v[...] = local_field(x0, c)
        choose, e0, flip = tables(nb_v[...], ns_v[...], fl_v[...], t)
        choose_v[...] = choose
        e0_v[...] = e0
        flip_v[...] = flip
        g32 = graph(nb_v[...])
        g_v[...] = g32.astype(BF16)
        x_v[...] = start_inverse(g32)[0]

    @pl.when(ready)
    def _():
        x_v[...] = newton(x_v[...], g_v[...], rhos[0], False)[0]

    done(a_peers, bufa0, 0, True)
    total = jnp.sum(bufa0[...], axis=0)[6:8]
    stgm[...] = total
    bufm[q] = total
    send(b_peers, lambda peer: stgm, bufm.at[q], 6)
    stgb0[...] = tiles_b(bufa0[...], choose_v[...])
    bufb0[q] = stgb0[q]
    send(b_peers, lambda peer: stgb0.at[spot(peer)], bufb0.at[q], 1)

    @pl.when(ready)
    def _():
        x_v[...] = newton(x_v[...], g_v[...], rhos[1], False)[0]

    @pl.when(ready)
    def _():
        x = newton(x_v[...], g_v[...], rhos[2], True)[0]
        xs = split(x, 3)
        e0 = e0_v[...]
        first_v[...] = dot(e0, xs[0]) + (dot(e0, xs[1]) + dot(e0, xs[2]))
        xh_v[...] = xs[0]
        xl_v[...] = xs[1]

    done(b_peers, bufm, 6, True)

    @pl.when(ready)
    def _():
        sums = bufm[:, 0, :]
        three = jnp.concatenate([bufm[:, 1, :], sums, roll(sums, 128 - EACH, 1)], axis=0)
        dvec, s0, s1 = to_vectors(three, consts())
        y = inverse_rows(first_v[...], xh_v[...], xl_v[...], dvec)
        y_v[...] = y
        edge_v[...], own_v[...] = coarse_parts(y, s0, s1)

    done(b_peers, bufb0, 1, True)
    c = consts()
    flip = flip_v[...]
    r, mass = r_v[...], m_v[...]
    z0, q0 = finish(r, l_v[...], mass, jnp.sum(bufb0[...], axis=0), flip, edge_v[...], own_v[...], c)

    x1 = coefficients(q0, c)
    rims = local_rims(x1, c)
    tile = tile_a(rims, packed(q0, plane), zrow)
    stga1[...] = tile
    bufa1[plane] = tile
    send(a_peers, lambda peer: stga1, bufa1.at[plane], 2)

    @pl.when(ready)
    def _():
        l_v[...] = local_field(x1, c)

    done(a_peers, bufa1, 2, True)
    stgb1[...] = tiles_b(bufa1[...], choose_v[...])
    bufb1[q] = stgb1[q]
    send(b_peers, lambda peer: stgb1.at[spot(peer)], bufb1.at[q], 3)
    done(b_peers, bufb1, 3, True)
    sums = bufb1[:, 6, :]
    s0, s1 = to_vectors(jnp.concatenate([sums, roll(sums, 128 - EACH, 1)], axis=0), c)
    edges, own = coarse_parts(y_v[...], s0, s1)
    w, v = finish(q0, l_v[...], mass, jnp.sum(bufb1[...], axis=0), flip, edges, own, c)

    row = dots_row(((r, z0), (z0, q0), (r, w), (q0, w), (z0, v), (w, v)))
    st3a[...] = row
    buf3a[plane * LINE + x_at] = row
    send(xy_peers, lambda peer: st3a, buf3a.at[plane * LINE + x_at], 4)

    @pl.when(ready)
    def _():
        for k, field in enumerate((z0, q0, w, v)):
            nat_v[k] = from_field(by_row(field))

    done(xy_peers, buf3a, 4, True)
    row = jnp.sum(buf3a[...], axis=0)
    st3b[...] = row
    buf3b[line * LEVS + lev] = row
    send(zc_peers, lambda peer: st3b, buf3b.at[line * LEVS + lev], 5)
    done(zc_peers, buf3b, 5, True)
    row = jnp.sum(buf3b[...], axis=0)

    upper = iota((8, 1), 0) < EACH
    a0, b0 = steps(row, 0)
    a1, b1 = steps(row, 1)
    a, b = jnp.where(upper, a0, a1), jnp.where(upper, b0, b1)
    outs = [a * nat_v[0] - b * nat_v[2], src_v[...] - a * nat_v[1] + b * nat_v[3]]
    last = []
    for k, (out, dst) in enumerate(zip(outs, (out_hbm.at[0], out_hbm.at[1]))):
        out_v[k] = out
        for p in range(2):
            for n in range(EACH):
                last.append(pltpu.make_async_copy(
                    out_v.at[k, pl.ds(p * EACH + n, 1)], dst.at[p, n], outsem.at[len(last)]))
    for copy in last:
        copy.start()
    for copy in last:
        copy.wait()

    done(a_peers, bufa0, 0, False)
    done(b_peers, bufb0, 1, False)
    done(a_peers, bufa1, 2, False)
    done(b_peers, bufb1, 3, False)
    done(xy_peers, buf3a, 4, False)
    done(zc_peers, buf3b, 5, False)
    done(b_peers, bufm, 6, False)


def shards(sources, mass_coef, neighbour_sub, neighbour_side, side_flip):
    s8, small, wide, inv = [jnp.asarray(a) for a in constants()]
    hbm = pl.BlockSpec(memory_space=pltpu.HBM)
    rows = sources.transpose(0, 2, 1, 3)
    args = [rows, mass_coef, neighbour_sub.T, neighbour_side.T, side_flip.T, s8, small, wide, inv]
    one = pltpu.VMEM((8, 128), F32)
    line = pltpu.VMEM((1, 128), F32)
    field = pltpu.VMEM((ROWS, 128), F32)
    square = lambda kind: pltpu.VMEM((SUBS, SUBS), kind)
    plane = pltpu.VMEM((PLANE, 8, 128), F32)
    column = pltpu.VMEM((COLUMN, 8, 128), F32)
    scratch = [pltpu.VMEM((8, SIDE * SIDE), F32)] + [pltpu.VMEM(a.shape, a.dtype) for a in args[1:]] + [
        field, field, field, pltpu.VMEM((512, 256), BF16), pltpu.VMEM((40, SUBS), BF16), one,
        square(F32), square(BF16), square(BF16), square(BF16), pltpu.VMEM((40, SUBS), F32),
        one, one, column, column, plane, plane, plane, plane, line, line,
        pltpu.VMEM((COLUMN * LINE, 1, 128), F32), pltpu.VMEM((LINE * LEVS, 1, 128), F32),
        pltpu.VMEM((2, 8, SIDE * SIDE), F32), pltpu.VMEM((4, 8, SIDE * SIDE), F32),
        pltpu.VMEM((2, 128), F32), pltpu.VMEM((PLANE, 2, 128), F32), pltpu.VMEM((40, SUBS), F32), one, one,
        pltpu.SemaphoreType.DMA((14,)), pltpu.SemaphoreType.DMA((12,)),
        pltpu.SemaphoreType.DMA((7,)), pltpu.SemaphoreType.DMA((7,)),
    ]
    out = jax.ShapeDtypeStruct((2,) + rows.shape, F32)
    both = pl.pallas_call(
        kernel,
        out_shape=out,
        in_specs=[hbm] * len(args),
        out_specs=hbm,
        scratch_shapes=scratch,
        compiler_params=pltpu.CompilerParams(collective_id=0, has_side_effects=True, vmem_limit_bytes=67043328),
        name="schwarz",
    )(*args)
    both = both.transpose(0, 1, 3, 2, 4)
    return both[0], both[1]


def solution(mesh):
    placed = (P(None, "lev", "tile", None), P("tile", None), P(), P(), P())
    return jax.shard_map(
        shards,
        mesh=mesh,
        in_specs=placed,
        out_specs=(P(None, "lev", "tile", None), P(None, "lev", "tile", None)),
        check_vma=False,
    )
```

```python
import math

import jax
import jax.numpy as jnp
import numpy as np
from jax import lax
from jax.experimental import pallas as pl
from jax.experimental.pallas import tpu as pltpu
from jax.sharding import PartitionSpec as P

F32 = jnp.float32
BF16 = jnp.bfloat16
SIDE = 32
SUBS = 384
PLANE = 16
COLUMN = 8
LEVS = 6
EACH = 3
LINE = 4
ROWS = 8 * SIDE

SHIFT = 1.28
SIGMA = 3.0
LOW = 32.0 * 0.06486 + SHIFT
TOP = 32.0 * 8.0 + SHIFT
RHO = 0.7681 / LOW
CHEB = 6


def roll(x, shift, axis):
    return pltpu.roll(x, shift, axis)


def iota(shape, dim):
    return lax.broadcasted_iota(jnp.int32, shape, dim)


def dot(a, b):
    return jnp.dot(a, b, preferred_element_type=F32)


def split(x, n):
    parts = []
    for _ in range(n):
        part = x.astype(BF16)
        parts.append(part)
        x = x - part.astype(F32)
    return parts


def stack(parts):
    return jnp.concatenate([part.astype(F32) for part in parts], axis=0).astype(BF16)


def spread(x, onehot):
    n = x.shape[0]
    out = dot(stack(split(x, 3)), onehot)
    return out[:n] + out[n : 2 * n] + out[2 * n :]


def mm3(a, b):
    ah, al = a
    bh, bl = b
    return dot(ah, bh) + (dot(ah, bl) + dot(al, bh))


def np_split(x):
    hi = x.astype(np.float32).astype(jnp.bfloat16)
    lo = (x - hi.astype(np.float64)).astype(np.float32).astype(jnp.bfloat16)
    return hi, lo


def polynomial():
    deg = 7
    nodes = np.cos(np.pi * (np.arange(deg + 1) + 0.5) / (deg + 1))
    g = 4.0 * nodes
    x = 128.0 + SHIFT - 32.0 * g

    def cheb(n, t):
        return np.where(
            np.abs(t) <= 1,
            np.cos(n * np.arccos(np.clip(t, -1, 1))),
            np.sign(t) ** n * np.cosh(n * np.arccosh(np.maximum(np.abs(t), 1))),
        )

    def tau(v):
        return (TOP + LOW - 2 * v) / (TOP - LOW)

    top = cheb(deg + 1, tau(0.0))
    vals = (1.0 - cheb(deg + 1, tau(x)) / top) / x
    coef = np.polynomial.polynomial.polyfit(nodes, vals, deg)
    at_one = np.polynomial.polynomial.polyval(1.0, coef)
    const = (1.0 / (SHIFT + SIGMA) - at_one) / SUBS
    return [float(c / 4.0**k) for k, c in enumerate(coef)], float(const), float(1.0 / top)


def constants():
    o = np.arange(SIDE) + 1.0
    step = math.pi / (SIDE + 1.0)
    sine = math.sqrt(2.0 / (SIDE + 1.0)) * np.sin(step * o[:, None] * o[None, :])
    lam = 2.0 - 2.0 * np.cos(step * o)
    inv = np.repeat(1.0 / (lam[:, None] + lam[None, :]), 8, axis=0)
    lanes = np.arange(128)
    side, kk = lanes // SIDE, lanes % SIDE
    m = np.arange(SUBS)
    cmp = ((lanes // 8)[:, None] == (m // EACH // PLANE)[None]) & ((lanes % 8)[:, None] == (m % EACH)[None])
    rev = (side[:, None] == side[None]) & (kk[:, None] == 31 - kk[None])
    s8 = np.concatenate(np_split(np.kron(sine, np.eye(8))), axis=0)
    s = np.concatenate([np.pad(a, ((0, 0), (0, 128 - SIDE))) for a in np_split(sine)], axis=0)
    ends = np.zeros((SIDE, 128))
    ends[:, 32:64] = sine[:, 31:32]
    ends[:, 96:] = sine[:, 0:1]
    quad = np.kron(np.eye(4), sine)
    rev = rev.astype(np.float32).astype(jnp.bfloat16)
    small = np.concatenate([s, *np_split(ends), *np_split(quad), rev], axis=0)
    wide = cmp.astype(np.float32).astype(jnp.bfloat16)
    return s8, small, wide, inv.astype(np.float32)


def by_row(v):
    return v.reshape(SIDE, 8, 128)


def stack_fields(first, second):
    return jnp.concatenate([first, second, jnp.zeros((2, first.shape[1]), F32)], axis=0)


def to_field(x):
    lane = iota((8, 128), 1)
    rows = []
    for i in range(SIDE):
        g, h = i // 4, i % 4
        part = x[:, 128 * g : 128 * g + 128]
        part = part if h == 0 else roll(part, 128 - 32 * h, 1)
        rows.append(jnp.where(lane < SIDE, part, 0.0))
    return jnp.concatenate(rows, axis=0)


def from_field(v):
    parts = []
    for g in range(8):
        total = v[4 * g]
        for h in (1, 2, 3):
            total = total + roll(v[4 * g + h], 32 * h, 1)
        parts.append(total)
    return jnp.concatenate(parts, axis=1)


def coefficients(r, c):
    v = mm3(c["s8"], split(r[:, :SIDE], 2))
    return mm3(split(v, 2), c["s"])[:, :SIDE] * c["inv"]


def local_rims(x, c):
    w = by_row(mm3(split(x, 2), c["ends"]))
    f = x.reshape(SIDE, 8, SIDE)
    lane = iota((8, 128), 1) & 63
    scale = [math.sqrt(2.0 / 33.0) * math.sin(math.pi * (i + 1) / 33.0) for i in range(SIDE)]
    even = sum(scale[i] * f[i] for i in range(0, SIDE, 2))
    odd = sum(scale[i] * f[i] for i in range(1, SIDE, 2))
    blank = jnp.zeros((8, SIDE), F32)
    tile = jnp.concatenate([even + odd, blank, even - odd, blank], axis=1)
    for i in range(SIDE):
        tile = jnp.where(lane == 32 + i, w[i], tile)
    th, tl = split(tile, 2)
    qh, ql = c["quad"]
    both = dot(stack([th, tl]), qh)
    return both[:8] + (both[8:] + dot(th, ql))


def local_field(x, c):
    v = mm3(split(x, 2), c["s"])
    return mm3(c["s8"], split(v, 2))


def packed(v, place):
    total = jnp.sum(jnp.sum(by_row(v), axis=0), axis=1, keepdims=True)
    at = iota((8, 128), 1) == place * 8 + iota((8, 128), 0)
    return jnp.sum(jnp.where(at, total, 0.0), axis=0, keepdims=True)


def tile_a(rims, sums, mass):
    row = iota((8, 128), 0)
    return jnp.where(row == 6, sums, jnp.where(row == 7, mass, rims))


def tables(nb, ns, fl, t):
    plane, q = t // PLANE, t % PLANE
    row, lane = iota((136, SUBS), 0), iota((136, SUBS), 1)
    target = jnp.where(row < 128, lax.shift_right_logical(row, jnp.int32(3)), q)
    field = row & 7
    sub = (plane * PLANE + target) * EACH + jnp.where(field >= EACH, field - EACH, field)
    take = (lane == sub) & (field < 6)

    def column(a, s):
        return jnp.sum(jnp.where(take, a[s : s + 1].astype(F32), 0.0), axis=1, keepdims=True)

    nbs = [column(nb, s).astype(jnp.int32) for s in range(4)]
    nss = [column(ns, s).astype(jnp.int32) for s in range(4)]
    fls = [column(fl, s) for s in range(4)]

    field = iota((128, 1), 0) & 7
    third = jnp.where(field >= EACH, EACH, 0)
    cols = iota((128, 256), 1)
    choose = []
    for s in range(4):
        sub = nbs[s][:128]
        device = lax.shift_right_logical(sub * 21846, jnp.int32(16))
        at = ((s - nss[s][:128]) & 3) * 64 + lax.shift_right_logical(device, jnp.int32(4)) * 8 + (sub - EACH * device) + third
        inside = ((device & 15) == q) & (field < 6)
        choose.append((cols == jnp.where(inside, at, -1)).astype(F32).astype(BF16))

    field, lane = iota((8, SUBS), 0), iota((8, SUBS), 1)
    own = (lane == t * EACH + jnp.where(field >= EACH, field - EACH, field)).astype(F32)
    rows = []
    for s in range(4):
        rows.append(jnp.where(field < 6, own - (lane == nbs[s][128:136]).astype(F32), 0.0))
    rows.append(jnp.where(field < 6, own, jnp.where(field == 6, 1.0, 0.0)))
    group = lax.shift_right_logical(iota((8, 128), 1), jnp.int32(5))
    flip = jnp.zeros((8, 128), F32)
    for s in range(4):
        flip = jnp.where(group == s, fls[s][128:136], flip)
    return jnp.concatenate(choose, axis=0), jnp.concatenate(rows, axis=0).astype(BF16), flip


def tiles_b(buf, choose):
    flat = buf.reshape(64, 128)
    turned = jnp.concatenate([flat] + [roll(flat, 32 * t, 1) for t in (1, 2, 3)], axis=0)
    a, b, c = split(turned, 3)
    wide = dot(choose, jnp.concatenate([a, b], axis=1))
    got = (wide[:, :128] + wide[:, 128:]) + dot(choose, c)
    group = lax.shift_right_logical(iota((128, 128), 1), jnp.int32(5))
    out = jnp.where(group == 0, got[:128], 0.0)
    for s in (1, 2, 3):
        out = jnp.where(group == s, got[128 * s : 128 * s + 128], out)
    row = iota((8, 128), 0)
    column = jnp.where(row >= 6, jnp.sum(buf, axis=0), 0.0)
    return out.reshape(PLANE, 8, 128) + column[None]


def graph(nb):
    row = iota((SUBS, SUBS), 0)
    total = jnp.zeros((SUBS, SUBS), F32)
    for s in range(4):
        total = total + (row == nb[s : s + 1]).astype(F32)
    return total


def start_inverse(g32):
    coef, const, rho = polynomial()
    g = g32.astype(BF16)
    g2 = dot(g, g)
    g2b = g2.astype(BF16)
    g3 = dot(g2b, g)
    g4 = dot(g2b, g2b)
    g3b, g4b = g3.astype(BF16), g4.astype(BF16)
    eye = (iota((SUBS, SUBS), 0) == iota((SUBS, SUBS), 1)).astype(F32)
    x = coef[0] * eye + const + coef[1] * g32 + coef[2] * g2 + coef[3] * g3 + coef[4] * g4
    x = x + coef[5] * dot(g4b, g) + coef[6] * dot(g4b, g2b) + coef[7] * dot(g4b, g3b)
    return x, rho


def newton(x, g, rho, last):
    xs = split(x, 3)
    gx = dot(g, xs[0]) + (dot(g, xs[1]) + dot(g, xs[2]))
    ones = (SIGMA / SUBS) * jnp.sum(x, axis=0, keepdims=True)
    eye = (iota((SUBS, SUBS), 0) == iota((SUBS, SUBS), 1)).astype(F32)
    rest = eye - ((128.0 + SHIFT) * x - 32.0 * gx + ones)
    x = x + mm3(xs[:2], split(rest, 2))
    if last:
        return x, 0.0
    scale = 2.0 / (2.0 - rho * rho)
    return scale * x, rho * rho / (2.0 - rho * rho)


def to_vectors(slots, c):
    wide = spread(slots, c["cmp"])
    row, lane = iota((PLANE, SUBS), 0), iota((PLANE, SUBS), 1)
    keep = (lax.shift_right_logical(lane * 21846, jnp.int32(16)) & 15) == row
    rows = []
    for k in range(slots.shape[0] // PLANE):
        block = wide[PLANE * k : PLANE * k + PLANE]
        rows.append(jnp.sum(jnp.where(keep, block, 0.0), axis=0, keepdims=True))
    return rows


def inverse_rows(first, xh, xl, mass):
    delta = mass - SHIFT

    def apply(d, fine):
        e = d * delta
        if not fine:
            return d + dot(e.astype(BF16), xh)
        eh, el = split(e, 2)
        n = e.shape[0]
        high = dot(stack([eh, el]), xh)
        return d + (high[:n] + (high[n:] + dot(eh, xl)))

    sig = 1.0 / RHO
    rk = 1.0 / sig
    rest = first
    d = rest
    y = d
    for k in range(CHEB):
        rest = rest - apply(d, k < 3)
        nxt = 1.0 / (2.0 * sig - rk)
        d = (nxt * rk) * d + (2.0 * nxt / RHO) * rest
        y = y + d
        rk = nxt
    u = y[38:39]
    t = jnp.sum(u, axis=1, keepdims=True)
    w = jnp.sum(y, axis=1, keepdims=True)
    share = (SIGMA / SUBS) / (1.0 - (SIGMA / SUBS) * t)
    return y + (w * share) * u


def coarse_parts(y, s0, s1):
    row = iota((8, SUBS), 0)
    s = jnp.where(row < EACH, s0, s1)
    group = lax.shift_right_logical(iota((8, 128), 1), jnp.int32(5))
    edges = jnp.zeros((8, 128), F32)
    for k in range(4):
        edges = jnp.where(group == k, jnp.sum(y[8 * k : 8 * k + 8] * s, axis=1, keepdims=True), edges)
    own = jnp.sum(y[32:40] * s, axis=1, keepdims=True)
    at = (iota((8, 128), 1) < SIDE) & (iota((8, 128), 0) < 6)
    return edges, jnp.where(at, own, 0.0)


def finish(r, local, mass, rims, flip, edges, own, c):
    turned = spread(rims, c["rev"])
    rims = jnp.where(flip > 0.5, turned, rims)
    e = jnp.where(iota((8, 128), 0) < 6, edges - rims, 0.0)
    lane = iota((8, 128), 1)
    left = roll(e, 33, 1)
    both = jnp.where((lane >= 1) & (lane < 32), left, jnp.where((lane >= 32) & (lane < 64), e, 0.0))
    f, fr, fm = by_row(local), by_row(r), by_row(mass)
    z, image = [], []
    for i in range(SIDE):
        zi = f[i] + own
        moved = roll(both, 127 - i, 1)
        if i == 31:
            moved = jnp.where(lane == 0, roll(left, 96, 1), moved)
        extra = jnp.where((lane == 0) | (lane == 31), moved, 0.0)
        if i == 0:
            extra = extra + jnp.where(lane < SIDE, e, 0.0)
        if i == 31:
            extra = extra + jnp.where(lane < SIDE, roll(e, 64, 1), 0.0)
        z.append(zi)
        image.append(fr[i] + fm[i] * zi + extra)
    return jnp.concatenate(z, axis=0), jnp.concatenate(image, axis=0)


def dots_row(pairs):
    lane, row = iota((8, 128), 1), iota((8, 128), 0)
    total = jnp.zeros((8, 128), F32)
    for k, (a, b) in enumerate(pairs):
        one = jnp.sum(jnp.sum(by_row(a * b), axis=0), axis=1, keepdims=True)
        at = ((lane == k) & (row < EACH)) | ((lane == 6 + k) & (row >= EACH) & (row < 6))
        total = jnp.where(at, one, total)
    return jnp.sum(total, axis=0, keepdims=True)


def steps(row, p):
    ga, de, rw, qw, zv, wv = [row[:, 6 * p + k : 6 * p + k + 1] for k in range(6)]
    a0 = ga / de
    g1 = ga - a0 * (de + rw) + a0 * a0 * qw
    d1 = de - a0 * (qw + zv) + a0 * a0 * wv
    beta = g1 / ga
    cross = de - a0 * (0.5 * (qw + zv))
    den = d1 + 2.0 * beta * cross + beta * beta * de
    a1 = g1 / den
    return a0 + a1 * (1.0 + beta), a1 * a0


def kernel(src_hbm, mass_hbm, nb_hbm, ns_hbm, fl_hbm, s8_hbm, small_hbm, wide_hbm, inv_hbm, out_ref,
           src_v, mass_v, nb_v, ns_v, fl_v, s8_v, small_v, wide_v, inv_v,
           r_v, m_v, l_v, choose_v, e0_v, flip_v, x_v, g_v, xh_v, xl_v, first_v,
           stga0, stga1, bufa0, bufa1, stgb0, stgb1, bufb0, bufb1, st3a, st3b, buf3a, buf3b,
           nat_v, stgm, bufm, y_v, edge_v, own_v, insem, ssem, rsem, opensem):
    t = lax.axis_index("tile")
    lev = lax.axis_index("lev")
    plane, q = t // PLANE, t % PLANE
    line, x_at = q // LINE, q % LINE
    ready = t >= 0

    def at(dy, dz, dx, dl):
        where = ((plane + dy) % COLUMN * LINE + (line + dz) % LINE) * LINE + (x_at + dx) % LINE
        return (where, (lev + dl) % LEVS)

    a_peers = [(dy, 0, 0, 0) for dy in (4, 3, 5, 2, 6, 1, 7)]
    b_peers = [(0, dz, dx, 0) for dz in (3, 2, 1, 0) for dx in (2, 1, 3, 0) if dz or dx]
    xy_peers = [(dy, 0, dx, 0) for dy in (4, 3, 5, 2, 6, 1, 7, 0) for dx in (2, 1, 3, 0) if dy or dx]
    zc_peers = [(0, dz, 0, dl) for dz in (3, 2, 1, 0) for dl in range(LEVS) if dz or dl]
    l_peers = [(0, 0, 0, dl) for dl in (2, 3, 4, 5, 1)]
    everyone = a_peers + b_peers + l_peers

    moves = [(src_hbm.at[p, n], src_v.at[pl.ds(p * EACH + n, 1)]) for p in range(2) for n in range(EACH)]
    moves += [(mass_hbm, mass_v), (s8_hbm, s8_v), (small_hbm, small_v), (inv_hbm, inv_v),
              (nb_hbm, nb_v), (ns_hbm, ns_v), (fl_hbm, fl_v), (wide_hbm, wide_v)]
    copies = [pltpu.make_async_copy(a, b, insem.at[k]) for k, (a, b) in enumerate(moves)]
    for copy in copies:
        copy.start()

    barrier = pltpu.get_barrier_semaphore()
    for peer in everyone:
        pl.semaphore_signal(barrier, 1, device_id=at(*peer), device_id_type=pl.DeviceIdType.MESH)

    for copy in copies:
        copy.wait()

    def spot(peer):
        return (line + peer[1]) % LINE * LINE + (x_at + peer[2]) % LINE

    def send(peers, src_of, dst, n):
        for peer in peers:
            pltpu.make_async_remote_copy(
                src_ref=src_of(peer), dst_ref=dst, send_sem=ssem.at[n], recv_sem=rsem.at[n],
                device_id=at(*peer), device_id_type=pl.DeviceIdType.MESH,
            ).start()

    def done(peers, buf, n, recv):
        view = buf.at[pl.ds(0, len(peers))]
        copy = pltpu.make_async_remote_copy(
            src_ref=view, dst_ref=view, send_sem=ssem.at[n], recv_sem=rsem.at[n],
            device_id=at(*peers[0]), device_id_type=pl.DeviceIdType.MESH,
        )
        if recv:
            copy.wait_recv()
        else:
            copy.wait_send()

    def consts():
        return {
            "s8": (s8_v[:256], s8_v[256:]),
            "s": (small_v[:SIDE], small_v[SIDE : 2 * SIDE]),
            "ends": (small_v[64:96], small_v[96:128]),
            "quad": (small_v[128:256], small_v[256:384]),
            "rev": small_v[384:],
            "inv": inv_v[...],
            "cmp": wide_v[...],
        }

    c = consts()
    zrow = jnp.zeros((1, 128), F32)

    first = src_v[...]
    r = to_field(jnp.where(iota(first.shape, 0) < 6, first, 0.0))
    mass = to_field(stack_fields(mass_v[...], mass_v[...]))
    r_v[...] = r
    m_v[...] = mass
    x0 = coefficients(r, c)
    rims = local_rims(x0, c)
    tile = tile_a(rims, packed(r, plane), packed(mass, plane))
    stga0[...] = tile
    bufa0[plane] = tile
    pl.semaphore_wait(barrier, len(everyone))
    send(a_peers, lambda peer: stga0, bufa0.at[plane], 0)

    polys = polynomial()[2]
    rhos = [polys]
    for _ in range(2):
        rhos.append(rhos[-1] ** 2 / (2.0 - rhos[-1] ** 2))

    @pl.when(ready)
    def _():
        l_v[...] = local_field(x0, c)
        choose, e0, flip = tables(nb_v[...], ns_v[...], fl_v[...], t)
        choose_v[...] = choose
        e0_v[...] = e0
        flip_v[...] = flip
        g32 = graph(nb_v[...])
        g_v[...] = g32.astype(BF16)
        x_v[...] = start_inverse(g32)[0]

    @pl.when(ready)
    def _():
        x_v[...] = newton(x_v[...], g_v[...], rhos[0], False)[0]

    done(a_peers, bufa0, 0, True)
    total = jnp.sum(bufa0[...], axis=0)[6:8]
    stgm[...] = total
    bufm[q] = total
    send(b_peers, lambda peer: stgm, bufm.at[q], 6)
    stgb0[...] = tiles_b(bufa0[...], choose_v[...])
    bufb0[q] = stgb0[q]
    send(b_peers, lambda peer: stgb0.at[spot(peer)], bufb0.at[q], 1)

    @pl.when(ready)
    def _():
        x_v[...] = newton(x_v[...], g_v[...], rhos[1], False)[0]

    @pl.when(ready)
    def _():
        x = newton(x_v[...], g_v[...], rhos[2], True)[0]
        xs = split(x, 3)
        e0 = e0_v[...]
        first_v[...] = dot(e0, xs[0]) + (dot(e0, xs[1]) + dot(e0, xs[2]))
        xh_v[...] = xs[0]
        xl_v[...] = xs[1]

    done(b_peers, bufm, 6, True)

    @pl.when(ready)
    def _():
        sums = bufm[:, 0, :]
        three = jnp.concatenate([bufm[:, 1, :], sums, roll(sums, 128 - EACH, 1)], axis=0)
        dvec, s0, s1 = to_vectors(three, consts())
        y = inverse_rows(first_v[...], xh_v[...], xl_v[...], dvec)
        y_v[...] = y
        edge_v[...], own_v[...] = coarse_parts(y, s0, s1)

    done(b_peers, bufb0, 1, True)
    for peer in l_peers:
        pl.semaphore_signal(opensem, 1, device_id=at(*peer), device_id_type=pl.DeviceIdType.MESH)
    c = consts()
    flip = flip_v[...]
    r, mass = r_v[...], m_v[...]
    z0, q0 = finish(r, l_v[...], mass, jnp.sum(bufb0[...], axis=0), flip, edge_v[...], own_v[...], c)

    x1 = coefficients(q0, c)
    rims = local_rims(x1, c)
    tile = tile_a(rims, packed(q0, plane), zrow)
    stga1[...] = tile
    bufa1[plane] = tile
    send(a_peers, lambda peer: stga1, bufa1.at[plane], 2)

    @pl.when(ready)
    def _():
        l_v[...] = local_field(x1, c)

    done(a_peers, bufa1, 2, True)
    stgb1[...] = tiles_b(bufa1[...], choose_v[...])
    bufb1[q] = stgb1[q]
    send(b_peers, lambda peer: stgb1.at[spot(peer)], bufb1.at[q], 3)
    done(b_peers, bufb1, 3, True)
    sums = bufb1[:, 6, :]
    s0, s1 = to_vectors(jnp.concatenate([sums, roll(sums, 128 - EACH, 1)], axis=0), c)
    edges, own = coarse_parts(y_v[...], s0, s1)
    w, v = finish(q0, l_v[...], mass, jnp.sum(bufb1[...], axis=0), flip, edges, own, c)

    row = dots_row(((r, z0), (z0, q0), (r, w), (q0, w), (z0, v), (w, v)))
    st3a[...] = row
    buf3a[plane * LINE + x_at] = row
    send(xy_peers, lambda peer: st3a, buf3a.at[plane * LINE + x_at], 4)

    @pl.when(ready)
    def _():
        for k, field in enumerate((z0, q0, w, v)):
            nat_v[k] = from_field(by_row(field))

    done(xy_peers, buf3a, 4, True)
    row = jnp.sum(buf3a[...], axis=0)
    st3b[...] = row
    buf3b[line * LEVS + lev] = row
    pl.semaphore_wait(opensem, len(l_peers))
    send(zc_peers, lambda peer: st3b, buf3b.at[line * LEVS + lev], 5)
    done(zc_peers, buf3b, 5, True)
    row = jnp.sum(buf3b[...], axis=0)

    upper = iota((8, 1), 0) < EACH
    a0, b0 = steps(row, 0)
    a1, b1 = steps(row, 1)
    a, b = jnp.where(upper, a0, a1), jnp.where(upper, b0, b1)
    outs = [a * nat_v[0] - b * nat_v[2], src_v[...] - a * nat_v[1] + b * nat_v[3]]
    for k, out in enumerate(outs):
        for p in range(2):
            for n in range(EACH):
                out_ref[k, p, n] = out[p * EACH + n : p * EACH + n + 1]

    done(a_peers, bufa0, 0, False)
    done(b_peers, bufb0, 1, False)
    done(a_peers, bufa1, 2, False)
    done(b_peers, bufb1, 3, False)
    done(xy_peers, buf3a, 4, False)
    done(zc_peers, buf3b, 5, False)
    done(b_peers, bufm, 6, False)


def shards(sources, mass_coef, neighbour_sub, neighbour_side, side_flip):
    s8, small, wide, inv = [jnp.asarray(a) for a in constants()]
    hbm = pl.BlockSpec(memory_space=pltpu.HBM)
    rows = sources.transpose(0, 2, 1, 3)
    args = [rows, mass_coef, neighbour_sub.T, neighbour_side.T, side_flip.T, s8, small, wide, inv]
    one = pltpu.VMEM((8, 128), F32)
    line = pltpu.VMEM((1, 128), F32)
    field = pltpu.VMEM((ROWS, 128), F32)
    square = lambda kind: pltpu.VMEM((SUBS, SUBS), kind)
    plane = pltpu.VMEM((PLANE, 8, 128), F32)
    column = pltpu.VMEM((COLUMN, 8, 128), F32)
    scratch = [pltpu.VMEM((8, SIDE * SIDE), F32)] + [pltpu.VMEM(a.shape, a.dtype) for a in args[1:]] + [
        field, field, field, pltpu.VMEM((512, 256), BF16), pltpu.VMEM((40, SUBS), BF16), one,
        square(F32), square(BF16), square(BF16), square(BF16), pltpu.VMEM((40, SUBS), F32),
        one, one, column, column, plane, plane, plane, plane, line, line,
        pltpu.VMEM((COLUMN * LINE, 1, 128), F32), pltpu.VMEM((LINE * LEVS, 1, 128), F32),
        pltpu.VMEM((4, 8, SIDE * SIDE), F32),
        pltpu.VMEM((2, 128), F32), pltpu.VMEM((PLANE, 2, 128), F32), pltpu.VMEM((40, SUBS), F32), one, one,
        pltpu.SemaphoreType.DMA((14,)),
        pltpu.SemaphoreType.DMA((7,)), pltpu.SemaphoreType.DMA((7,)), pltpu.SemaphoreType.REGULAR,
    ]
    out = pltpu.VMEM((2,) + rows.shape, F32)
    both = pl.pallas_call(
        kernel,
        out_shape=out,
        in_specs=[hbm] * len(args),
        out_specs=pl.BlockSpec(memory_space=pltpu.VMEM),
        scratch_shapes=scratch,
        compiler_params=pltpu.CompilerParams(collective_id=0, has_side_effects=True, vmem_limit_bytes=60 << 20),
        name="schwarz",
    )(*args)
    both = both.transpose(0, 1, 3, 2, 4)
    return both[0], both[1]


def solution(mesh):
    placed = (P(None, "lev", "tile", None), P("tile", None), P(), P(), P())
    return jax.shard_map(
        shards,
        mesh=mesh,
        in_specs=placed,
        out_specs=(P(None, "lev", "tile", None), P(None, "lev", "tile", None)),
        check_vma=False,
    )
```

```python
import math

import jax
import jax.numpy as jnp
import numpy as np
from jax import lax
from jax.experimental import pallas as pl
from jax.experimental.pallas import tpu as pltpu
from jax.sharding import PartitionSpec as P

F32 = jnp.float32
BF16 = jnp.bfloat16
SIDE = 32
SUBS = 384
PLANE = 16
COLUMN = 8
LEVS = 6
EACH = 3
LINE = 4
ROWS = 8 * SIDE

SHIFT = 1.28
SIGMA = 3.0
LOW = 32.0 * 0.06486 + SHIFT
TOP = 32.0 * 8.0 + SHIFT
RHO = 0.7681 / LOW
CHEB = 6


def roll(x, shift, axis):
    return pltpu.roll(x, shift, axis)


def iota(shape, dim):
    return lax.broadcasted_iota(jnp.int32, shape, dim)


def dot(a, b):
    return jnp.dot(a, b, preferred_element_type=F32)


def split(x, n):
    parts = []
    for _ in range(n):
        part = x.astype(BF16)
        parts.append(part)
        x = x - part.astype(F32)
    return parts


def stack(parts):
    return jnp.concatenate([part.astype(F32) for part in parts], axis=0).astype(BF16)


def spread(x, onehot):
    n = x.shape[0]
    out = dot(stack(split(x, 3)), onehot)
    return out[:n] + out[n : 2 * n] + out[2 * n :]


def mm3(a, b):
    ah, al = a
    bh, bl = b
    return dot(ah, bh) + (dot(ah, bl) + dot(al, bh))


def np_split(x):
    hi = x.astype(np.float32).astype(jnp.bfloat16)
    lo = (x - hi.astype(np.float64)).astype(np.float32).astype(jnp.bfloat16)
    return hi, lo


def polynomial():
    deg = 7
    nodes = np.cos(np.pi * (np.arange(deg + 1) + 0.5) / (deg + 1))
    g = 4.0 * nodes
    x = 128.0 + SHIFT - 32.0 * g

    def cheb(n, t):
        return np.where(
            np.abs(t) <= 1,
            np.cos(n * np.arccos(np.clip(t, -1, 1))),
            np.sign(t) ** n * np.cosh(n * np.arccosh(np.maximum(np.abs(t), 1))),
        )

    def tau(v):
        return (TOP + LOW - 2 * v) / (TOP - LOW)

    top = cheb(deg + 1, tau(0.0))
    vals = (1.0 - cheb(deg + 1, tau(x)) / top) / x
    coef = np.polynomial.polynomial.polyfit(nodes, vals, deg)
    at_one = np.polynomial.polynomial.polyval(1.0, coef)
    const = (1.0 / (SHIFT + SIGMA) - at_one) / SUBS
    return [float(c / 4.0**k) for k, c in enumerate(coef)], float(const), float(1.0 / top)


def constants():
    o = np.arange(SIDE) + 1.0
    step = math.pi / (SIDE + 1.0)
    sine = math.sqrt(2.0 / (SIDE + 1.0)) * np.sin(step * o[:, None] * o[None, :])
    lam = 2.0 - 2.0 * np.cos(step * o)
    inv = np.repeat(1.0 / (lam[:, None] + lam[None, :]), 8, axis=0)
    lanes = np.arange(128)
    side, kk = lanes // SIDE, lanes % SIDE
    m = np.arange(SUBS)
    cmp = ((lanes // 8)[:, None] == (m // EACH // PLANE)[None]) & ((lanes % 8)[:, None] == (m % EACH)[None])
    rev = (side[:, None] == side[None]) & (kk[:, None] == 31 - kk[None])
    s8 = np.concatenate(np_split(np.kron(sine, np.eye(8))), axis=0)
    s = np.concatenate([np.pad(a, ((0, 0), (0, 128 - SIDE))) for a in np_split(sine)], axis=0)
    ends = np.zeros((SIDE, 128))
    ends[:, 32:64] = sine[:, 31:32]
    ends[:, 96:] = sine[:, 0:1]
    quad = np.kron(np.eye(4), sine)
    rev = rev.astype(np.float32).astype(jnp.bfloat16)
    small = np.concatenate([s, *np_split(ends), *np_split(quad), rev], axis=0)
    wide = cmp.astype(np.float32).astype(jnp.bfloat16)
    return s8, small, wide, inv.astype(np.float32)


def by_row(v):
    return v.reshape(SIDE, 8, 128)


def stack_fields(first, second):
    return jnp.concatenate([first, second, jnp.zeros((2, first.shape[1]), F32)], axis=0)


def to_field(x):
    lane = iota((8, 128), 1)
    rows = []
    for i in range(SIDE):
        g, h = i // 4, i % 4
        part = x[:, 128 * g : 128 * g + 128]
        part = part if h == 0 else roll(part, 128 - 32 * h, 1)
        rows.append(jnp.where(lane < SIDE, part, 0.0))
    return jnp.concatenate(rows, axis=0)


def from_field(v):
    parts = []
    for g in range(8):
        total = v[4 * g]
        for h in (1, 2, 3):
            total = total + roll(v[4 * g + h], 32 * h, 1)
        parts.append(total)
    return jnp.concatenate(parts, axis=1)


def coefficients(r, c):
    v = mm3(c["s8"], split(r[:, :SIDE], 2))
    return mm3(split(v, 2), c["s"])[:, :SIDE] * c["inv"]


def local_rims(x, c):
    w = by_row(mm3(split(x, 2), c["ends"]))
    f = x.reshape(SIDE, 8, SIDE)
    lane = iota((8, 128), 1) & 63
    scale = [math.sqrt(2.0 / 33.0) * math.sin(math.pi * (i + 1) / 33.0) for i in range(SIDE)]
    even = sum(scale[i] * f[i] for i in range(0, SIDE, 2))
    odd = sum(scale[i] * f[i] for i in range(1, SIDE, 2))
    blank = jnp.zeros((8, SIDE), F32)
    tile = jnp.concatenate([even + odd, blank, even - odd, blank], axis=1)
    for i in range(SIDE):
        tile = jnp.where(lane == 32 + i, w[i], tile)
    th, tl = split(tile, 2)
    qh, ql = c["quad"]
    both = dot(stack([th, tl]), qh)
    return both[:8] + (both[8:] + dot(th, ql))


def local_field(x, c):
    v = mm3(split(x, 2), c["s"])
    return mm3(c["s8"], split(v, 2))


def packed(v, place):
    total = jnp.sum(jnp.sum(by_row(v), axis=0), axis=1, keepdims=True)
    at = iota((8, 128), 1) == place * 8 + iota((8, 128), 0)
    return jnp.sum(jnp.where(at, total, 0.0), axis=0, keepdims=True)


def tile_a(rims, sums, mass):
    row = iota((8, 128), 0)
    return jnp.where(row == 6, sums, jnp.where(row == 7, mass, rims))


def tables(nb, ns, fl, t):
    plane, q = t // PLANE, t % PLANE
    row, lane = iota((136, SUBS), 0), iota((136, SUBS), 1)
    target = jnp.where(row < 128, lax.shift_right_logical(row, jnp.int32(3)), q)
    field = row & 7
    sub = (plane * PLANE + target) * EACH + jnp.where(field >= EACH, field - EACH, field)
    take = (lane == sub) & (field < 6)

    def column(a, s):
        return jnp.sum(jnp.where(take, a[s : s + 1].astype(F32), 0.0), axis=1, keepdims=True)

    nbs = [column(nb, s).astype(jnp.int32) for s in range(4)]
    nss = [column(ns, s).astype(jnp.int32) for s in range(4)]
    fls = [column(fl, s) for s in range(4)]

    field = iota((128, 1), 0) & 7
    third = jnp.where(field >= EACH, EACH, 0)
    cols = iota((128, 256), 1)
    choose = []
    for s in range(4):
        sub = nbs[s][:128]
        device = lax.shift_right_logical(sub * 21846, jnp.int32(16))
        at = ((s - nss[s][:128]) & 3) * 64 + lax.shift_right_logical(device, jnp.int32(4)) * 8 + (sub - EACH * device) + third
        inside = ((device & 15) == q) & (field < 6)
        choose.append((cols == jnp.where(inside, at, -1)).astype(F32).astype(BF16))

    field, lane = iota((8, SUBS), 0), iota((8, SUBS), 1)
    own = (lane == t * EACH + jnp.where(field >= EACH, field - EACH, field)).astype(F32)
    rows = []
    for s in range(4):
        rows.append(jnp.where(field < 6, own - (lane == nbs[s][128:136]).astype(F32), 0.0))
    rows.append(jnp.where(field < 6, own, jnp.where(field == 6, 1.0, 0.0)))
    group = lax.shift_right_logical(iota((8, 128), 1), jnp.int32(5))
    flip = jnp.zeros((8, 128), F32)
    for s in range(4):
        flip = jnp.where(group == s, fls[s][128:136], flip)
    return jnp.concatenate(choose, axis=0), jnp.concatenate(rows, axis=0).astype(BF16), flip


def tiles_b(buf, choose):
    flat = buf.reshape(64, 128)
    turned = jnp.concatenate([flat] + [roll(flat, 32 * t, 1) for t in (1, 2, 3)], axis=0)
    a, b, c = split(turned, 3)
    wide = dot(choose, jnp.concatenate([a, b], axis=1))
    got = (wide[:, :128] + wide[:, 128:]) + dot(choose, c)
    group = lax.shift_right_logical(iota((128, 128), 1), jnp.int32(5))
    out = jnp.where(group == 0, got[:128], 0.0)
    for s in (1, 2, 3):
        out = jnp.where(group == s, got[128 * s : 128 * s + 128], out)
    row = iota((8, 128), 0)
    column = jnp.where(row >= 6, jnp.sum(buf, axis=0), 0.0)
    return out.reshape(PLANE, 8, 128) + column[None]


def graph(nb):
    row = iota((SUBS, SUBS), 0)
    total = jnp.zeros((SUBS, SUBS), F32)
    for s in range(4):
        total = total + (row == nb[s : s + 1]).astype(F32)
    return total


def start_inverse(g32):
    coef, const, rho = polynomial()
    g = g32.astype(BF16)
    g2 = dot(g, g)
    g2b = g2.astype(BF16)
    g3 = dot(g2b, g)
    g4 = dot(g2b, g2b)
    g3b, g4b = g3.astype(BF16), g4.astype(BF16)
    eye = (iota((SUBS, SUBS), 0) == iota((SUBS, SUBS), 1)).astype(F32)
    x = coef[0] * eye + const + coef[1] * g32 + coef[2] * g2 + coef[3] * g3 + coef[4] * g4
    x = x + coef[5] * dot(g4b, g) + coef[6] * dot(g4b, g2b) + coef[7] * dot(g4b, g3b)
    return x, rho


def newton(x, g, rho, last):
    xs = split(x, 3)
    gx = dot(g, xs[0]) + (dot(g, xs[1]) + dot(g, xs[2]))
    ones = (SIGMA / SUBS) * jnp.sum(x, axis=0, keepdims=True)
    eye = (iota((SUBS, SUBS), 0) == iota((SUBS, SUBS), 1)).astype(F32)
    rest = eye - ((128.0 + SHIFT) * x - 32.0 * gx + ones)
    x = x + mm3(xs[:2], split(rest, 2))
    if last:
        return x, 0.0
    scale = 2.0 / (2.0 - rho * rho)
    return scale * x, rho * rho / (2.0 - rho * rho)


def to_vectors(slots, c):
    wide = spread(slots, c["cmp"])
    row, lane = iota((PLANE, SUBS), 0), iota((PLANE, SUBS), 1)
    keep = (lax.shift_right_logical(lane * 21846, jnp.int32(16)) & 15) == row
    rows = []
    for k in range(slots.shape[0] // PLANE):
        block = wide[PLANE * k : PLANE * k + PLANE]
        rows.append(jnp.sum(jnp.where(keep, block, 0.0), axis=0, keepdims=True))
    return rows


def inverse_rows(first, xh, xl, mass):
    delta = mass - SHIFT

    def apply(d, fine):
        e = d * delta
        if not fine:
            return d + dot(e.astype(BF16), xh)
        eh, el = split(e, 2)
        n = e.shape[0]
        high = dot(stack([eh, el]), xh)
        return d + (high[:n] + (high[n:] + dot(eh, xl)))

    sig = 1.0 / RHO
    rk = 1.0 / sig
    rest = first
    d = rest
    y = d
    for k in range(CHEB):
        rest = rest - apply(d, k < 3)
        nxt = 1.0 / (2.0 * sig - rk)
        d = (nxt * rk) * d + (2.0 * nxt / RHO) * rest
        y = y + d
        rk = nxt
    u = y[38:39]
    t = jnp.sum(u, axis=1, keepdims=True)
    w = jnp.sum(y, axis=1, keepdims=True)
    share = (SIGMA / SUBS) / (1.0 - (SIGMA / SUBS) * t)
    return y + (w * share) * u


def coarse_parts(y, s0, s1):
    row = iota((8, SUBS), 0)
    s = jnp.where(row < EACH, s0, s1)
    group = lax.shift_right_logical(iota((8, 128), 1), jnp.int32(5))
    edges = jnp.zeros((8, 128), F32)
    for k in range(4):
        edges = jnp.where(group == k, jnp.sum(y[8 * k : 8 * k + 8] * s, axis=1, keepdims=True), edges)
    own = jnp.sum(y[32:40] * s, axis=1, keepdims=True)
    at = (iota((8, 128), 1) < SIDE) & (iota((8, 128), 0) < 6)
    return edges, jnp.where(at, own, 0.0)


def finish(r, local, mass, rims, flip, edges, own, c):
    turned = spread(rims, c["rev"])
    rims = jnp.where(flip > 0.5, turned, rims)
    e = jnp.where(iota((8, 128), 0) < 6, edges - rims, 0.0)
    lane = iota((8, 128), 1)
    left = roll(e, 33, 1)
    both = jnp.where((lane >= 1) & (lane < 32), left, jnp.where((lane >= 32) & (lane < 64), e, 0.0))
    f, fr, fm = by_row(local), by_row(r), by_row(mass)
    z, image = [], []
    for i in range(SIDE):
        zi = f[i] + own
        moved = roll(both, 127 - i, 1)
        if i == 31:
            moved = jnp.where(lane == 0, roll(left, 96, 1), moved)
        extra = jnp.where((lane == 0) | (lane == 31), moved, 0.0)
        if i == 0:
            extra = extra + jnp.where(lane < SIDE, e, 0.0)
        if i == 31:
            extra = extra + jnp.where(lane < SIDE, roll(e, 64, 1), 0.0)
        z.append(zi)
        image.append(fr[i] + fm[i] * zi + extra)
    return jnp.concatenate(z, axis=0), jnp.concatenate(image, axis=0)


def dots_tile(pairs, first):
    lane, row = iota((8, 128), 1), iota((8, 128), 0)
    total = jnp.zeros((8, 128), F32)
    for k, (a, b) in enumerate(pairs, first):
        one = jnp.sum(jnp.sum(by_row(a * b), axis=0), axis=1, keepdims=True)
        at = ((lane == k) & (row < EACH)) | ((lane == 6 + k) & (row >= EACH) & (row < 6))
        total = jnp.where(at, one, total)
    return total


def steps(row, p):
    ga, de, rw, qw, zv, wv = [row[:, 6 * p + k : 6 * p + k + 1] for k in range(6)]
    a0 = ga / de
    g1 = ga - a0 * (de + rw) + a0 * a0 * qw
    d1 = de - a0 * (qw + zv) + a0 * a0 * wv
    beta = g1 / ga
    cross = de - a0 * (0.5 * (qw + zv))
    den = d1 + 2.0 * beta * cross + beta * beta * de
    a1 = g1 / den
    return a0 + a1 * (1.0 + beta), a1 * a0


def kernel(src_hbm, mass_hbm, nb_hbm, ns_hbm, fl_hbm, s8_hbm, small_hbm, wide_hbm, inv_hbm, out_ref,
           src_v, mass_v, nb_v, ns_v, fl_v, s8_v, small_v, wide_v, inv_v,
           r_v, m_v, l_v, choose_v, e0_v, flip_v, x_v, g_v, xh_v, xl_v, first_v,
           stga0, stga1, bufa0, bufa1, stgb0, stgb1, bufb0, bufb1, st3a, st3b, buf3a, buf3b,
           nat_v, stgm, bufm, y_v, edge_v, own_v, dots_v, insem, ssem, rsem, opensem, farsem):
    t = lax.axis_index("tile")
    lev = lax.axis_index("lev")
    plane, q = t // PLANE, t % PLANE
    line, x_at = q // LINE, q % LINE
    ready = t >= 0

    def at(dy, dz, dx, dl):
        where = ((plane + dy) % COLUMN * LINE + (line + dz) % LINE) * LINE + (x_at + dx) % LINE
        return (where, (lev + dl) % LEVS)

    a_peers = [(dy, 0, 0, 0) for dy in (4, 3, 5, 2, 6, 1, 7)]
    b_peers = [(0, dz, dx, 0) for dz in (3, 2, 1, 0) for dx in (2, 1, 3, 0) if dz or dx]
    xy_peers = [(dy, 0, dx, 0) for dy in (4, 3, 5, 2, 6, 1, 7, 0) for dx in (2, 1, 3, 0) if dy or dx]
    zc_peers = [(0, dz, 0, dl) for dz in (3, 2, 1, 0) for dl in range(LEVS) if dz or dl]
    l_peers = [(0, 0, 0, dl) for dl in (2, 3, 4, 5, 1)]
    far_peers = [(0, 1, 2, 0), (0, 3, 2, 0)]
    between = [(0, 1, 0, 0), (0, 3, 0, 0)]
    everyone = a_peers + l_peers + [peer for peer in b_peers if peer not in far_peers]

    moves = [(src_hbm.at[p, n], src_v.at[pl.ds(p * EACH + n, 1)]) for p in range(2) for n in range(EACH)]
    moves += [(mass_hbm, mass_v), (s8_hbm, s8_v), (small_hbm, small_v), (inv_hbm, inv_v),
              (nb_hbm, nb_v), (ns_hbm, ns_v), (fl_hbm, fl_v), (wide_hbm, wide_v)]
    copies = [pltpu.make_async_copy(a, b, insem.at[k]) for k, (a, b) in enumerate(moves)]
    for copy in copies:
        copy.start()

    barrier = pltpu.get_barrier_semaphore()
    for peer in everyone:
        pl.semaphore_signal(barrier, 1, device_id=at(*peer), device_id_type=pl.DeviceIdType.MESH)

    for copy in copies:
        copy.wait()

    def spot(peer):
        return (line + peer[1]) % LINE * LINE + (x_at + peer[2]) % LINE

    def send(peers, src_of, dst, n):
        for peer in peers:
            pltpu.make_async_remote_copy(
                src_ref=src_of(peer), dst_ref=dst, send_sem=ssem.at[n], recv_sem=rsem.at[n],
                device_id=at(*peer), device_id_type=pl.DeviceIdType.MESH,
            ).start()

    def done(peers, buf, n, recv):
        view = buf.at[pl.ds(0, len(peers))]
        copy = pltpu.make_async_remote_copy(
            src_ref=view, dst_ref=view, send_sem=ssem.at[n], recv_sem=rsem.at[n],
            device_id=at(*peers[0]), device_id_type=pl.DeviceIdType.MESH,
        )
        if recv:
            copy.wait_recv()
        else:
            copy.wait_send()

    def consts():
        return {
            "s8": (s8_v[:256], s8_v[256:]),
            "s": (small_v[:SIDE], small_v[SIDE : 2 * SIDE]),
            "ends": (small_v[64:96], small_v[96:128]),
            "quad": (small_v[128:256], small_v[256:384]),
            "rev": small_v[384:],
            "inv": inv_v[...],
            "cmp": wide_v[...],
        }

    c = consts()
    zrow = jnp.zeros((1, 128), F32)

    first = src_v[...]
    r = to_field(jnp.where(iota(first.shape, 0) < 6, first, 0.0))
    mass = to_field(stack_fields(mass_v[...], mass_v[...]))
    r_v[...] = r
    m_v[...] = mass
    x0 = coefficients(r, c)
    rims = local_rims(x0, c)
    tile = tile_a(rims, packed(r, plane), packed(mass, plane))
    stga0[...] = tile
    bufa0[plane] = tile
    pl.semaphore_wait(barrier, len(everyone))
    send(a_peers, lambda peer: stga0, bufa0.at[plane], 0)
    for peer in between:
        pl.semaphore_signal(farsem, 1, device_id=at(*peer), device_id_type=pl.DeviceIdType.MESH)

    polys = polynomial()[2]
    rhos = [polys]
    for _ in range(2):
        rhos.append(rhos[-1] ** 2 / (2.0 - rhos[-1] ** 2))

    @pl.when(ready)
    def _():
        l_v[...] = local_field(x0, c)
        choose, e0, flip = tables(nb_v[...], ns_v[...], fl_v[...], t)
        choose_v[...] = choose
        e0_v[...] = e0
        flip_v[...] = flip
        g32 = graph(nb_v[...])
        g_v[...] = g32.astype(BF16)
        x_v[...] = start_inverse(g32)[0]

    @pl.when(ready)
    def _():
        x_v[...] = newton(x_v[...], g_v[...], rhos[0], False)[0]

    done(a_peers, bufa0, 0, True)
    pl.semaphore_wait(farsem, len(between))
    total = jnp.sum(bufa0[...], axis=0)[6:8]
    stgm[...] = total
    bufm[q] = total
    send(b_peers, lambda peer: stgm, bufm.at[q], 6)
    stgb0[...] = tiles_b(bufa0[...], choose_v[...])
    bufb0[q] = stgb0[q]
    send(b_peers, lambda peer: stgb0.at[spot(peer)], bufb0.at[q], 1)

    @pl.when(ready)
    def _():
        x_v[...] = newton(x_v[...], g_v[...], rhos[1], False)[0]

    @pl.when(ready)
    def _():
        x = newton(x_v[...], g_v[...], rhos[2], True)[0]
        xs = split(x, 3)
        e0 = e0_v[...]
        first_v[...] = dot(e0, xs[0]) + (dot(e0, xs[1]) + dot(e0, xs[2]))
        xh_v[...] = xs[0]
        xl_v[...] = xs[1]

    done(b_peers, bufm, 6, True)

    @pl.when(ready)
    def _():
        sums = bufm[:, 0, :]
        three = jnp.concatenate([bufm[:, 1, :], sums, roll(sums, 128 - EACH, 1)], axis=0)
        dvec, s0, s1 = to_vectors(three, consts())
        y = inverse_rows(first_v[...], xh_v[...], xl_v[...], dvec)
        y_v[...] = y
        edge_v[...], own_v[...] = coarse_parts(y, s0, s1)

    done(b_peers, bufb0, 1, True)
    for peer in l_peers:
        pl.semaphore_signal(opensem, 1, device_id=at(*peer), device_id_type=pl.DeviceIdType.MESH)
    c = consts()
    flip = flip_v[...]
    r, mass = r_v[...], m_v[...]
    z0, q0 = finish(r, l_v[...], mass, jnp.sum(bufb0[...], axis=0), flip, edge_v[...], own_v[...], c)

    x1 = coefficients(q0, c)
    rims = local_rims(x1, c)
    tile = tile_a(rims, packed(q0, plane), zrow)
    stga1[...] = tile
    bufa1[plane] = tile
    send(a_peers, lambda peer: stga1, bufa1.at[plane], 2)

    @pl.when(ready)
    def _():
        l_v[...] = local_field(x1, c)
        dots_v[...] = dots_tile(((r, z0), (z0, q0)), 0)

    done(a_peers, bufa1, 2, True)
    stgb1[...] = tiles_b(bufa1[...], choose_v[...])
    bufb1[q] = stgb1[q]
    send(b_peers, lambda peer: stgb1.at[spot(peer)], bufb1.at[q], 3)
    done(b_peers, bufb1, 3, True)
    sums = bufb1[:, 6, :]
    s0, s1 = to_vectors(jnp.concatenate([sums, roll(sums, 128 - EACH, 1)], axis=0), c)
    edges, own = coarse_parts(y_v[...], s0, s1)
    w, v = finish(q0, l_v[...], mass, jnp.sum(bufb1[...], axis=0), flip, edges, own, c)

    tile = dots_v[...] + dots_tile(((r, w), (q0, w), (z0, v), (w, v)), 2)
    row = jnp.sum(tile, axis=0, keepdims=True)
    st3a[...] = row
    buf3a[plane * LINE + x_at] = row
    send(xy_peers, lambda peer: st3a, buf3a.at[plane * LINE + x_at], 4)

    @pl.when(ready)
    def _():
        for k, field in enumerate((z0, q0, w, v)):
            nat_v[k] = from_field(by_row(field))

    done(xy_peers, buf3a, 4, True)
    row = jnp.sum(buf3a[...], axis=0)
    st3b[...] = row
    buf3b[line * LEVS + lev] = row
    pl.semaphore_wait(opensem, len(l_peers))
    send(zc_peers, lambda peer: st3b, buf3b.at[line * LEVS + lev], 5)
    done(zc_peers, buf3b, 5, True)
    row = jnp.sum(buf3b[...], axis=0)

    upper = iota((8, 1), 0) < EACH
    a0, b0 = steps(row, 0)
    a1, b1 = steps(row, 1)
    a, b = jnp.where(upper, a0, a1), jnp.where(upper, b0, b1)
    outs = [a * nat_v[0] - b * nat_v[2], src_v[...] - a * nat_v[1] + b * nat_v[3]]
    for k, out in enumerate(outs):
        for p in range(2):
            for n in range(EACH):
                out_ref[k, p, n] = out[p * EACH + n : p * EACH + n + 1]

    done(a_peers, bufa0, 0, False)
    done(b_peers, bufb0, 1, False)
    done(a_peers, bufa1, 2, False)
    done(b_peers, bufb1, 3, False)
    done(xy_peers, buf3a, 4, False)
    done(zc_peers, buf3b, 5, False)
    done(b_peers, bufm, 6, False)


def shards(sources, mass_coef, neighbour_sub, neighbour_side, side_flip):
    s8, small, wide, inv = [jnp.asarray(a) for a in constants()]
    hbm = pl.BlockSpec(memory_space=pltpu.HBM)
    rows = sources.transpose(0, 2, 1, 3)
    args = [rows, mass_coef, neighbour_sub.T, neighbour_side.T, side_flip.T, s8, small, wide, inv]
    one = pltpu.VMEM((8, 128), F32)
    line = pltpu.VMEM((1, 128), F32)
    field = pltpu.VMEM((ROWS, 128), F32)
    square = lambda kind: pltpu.VMEM((SUBS, SUBS), kind)
    plane = pltpu.VMEM((PLANE, 8, 128), F32)
    column = pltpu.VMEM((COLUMN, 8, 128), F32)
    scratch = [pltpu.VMEM((8, SIDE * SIDE), F32)] + [pltpu.VMEM(a.shape, a.dtype) for a in args[1:]] + [
        field, field, field, pltpu.VMEM((512, 256), BF16), pltpu.VMEM((40, SUBS), BF16), one,
        square(F32), square(BF16), square(BF16), square(BF16), pltpu.VMEM((40, SUBS), F32),
        one, one, column, column, plane, plane, plane, plane, line, line,
        pltpu.VMEM((COLUMN * LINE, 1, 128), F32), pltpu.VMEM((LINE * LEVS, 1, 128), F32),
        pltpu.VMEM((4, 8, SIDE * SIDE), F32),
        pltpu.VMEM((2, 128), F32), pltpu.VMEM((PLANE, 2, 128), F32), pltpu.VMEM((40, SUBS), F32), one, one, one,
        pltpu.SemaphoreType.DMA((14,)),
        pltpu.SemaphoreType.DMA((7,)), pltpu.SemaphoreType.DMA((7,)), pltpu.SemaphoreType.REGULAR, pltpu.SemaphoreType.REGULAR,
    ]
    out = pltpu.VMEM((2,) + rows.shape, F32)
    both = pl.pallas_call(
        kernel,
        out_shape=out,
        in_specs=[hbm] * len(args),
        out_specs=pl.BlockSpec(memory_space=pltpu.VMEM),
        scratch_shapes=scratch,
        compiler_params=pltpu.CompilerParams(collective_id=0, has_side_effects=True, vmem_limit_bytes=60 << 20),
        name="schwarz",
    )(*args)
    both = both.transpose(0, 1, 3, 2, 4)
    return both[0], both[1]


def solution(mesh):
    placed = (P(None, "lev", "tile", None), P("tile", None), P(), P(), P())
    return jax.shard_map(
        shards,
        mesh=mesh,
        in_specs=placed,
        out_specs=(P(None, "lev", "tile", None), P(None, "lev", "tile", None)),
        check_vma=False,
    )
```

```python
import math

import jax
import jax.numpy as jnp
import numpy as np
from jax import lax
from jax.experimental import pallas as pl
from jax.experimental.pallas import tpu as pltpu
from jax.sharding import PartitionSpec as P

F32 = jnp.float32
BF16 = jnp.bfloat16
SIDE = 32
SUBS = 384
PLANE = 16
COLUMN = 8
LEVS = 6
EACH = 3
LINE = 4
ROWS = 8 * SIDE

SHIFT = 1.28
SIGMA = 3.0
LOW = 32.0 * 0.06486 + SHIFT
TOP = 32.0 * 8.0 + SHIFT
RHO = 0.7681 / LOW
CHEB = 6


def roll(x, shift, axis):
    return pltpu.roll(x, shift, axis)


def iota(shape, dim):
    return lax.broadcasted_iota(jnp.int32, shape, dim)


def dot(a, b):
    return jnp.dot(a, b, preferred_element_type=F32)


def split(x, n):
    parts = []
    for _ in range(n):
        part = x.astype(BF16)
        parts.append(part)
        x = x - part.astype(F32)
    return parts


def stack(parts):
    return jnp.concatenate([part.astype(F32) for part in parts], axis=0).astype(BF16)


def spread(x, onehot):
    n = x.shape[0]
    out = dot(stack(split(x, 3)), onehot)
    return out[:n] + out[n : 2 * n] + out[2 * n :]


def mm3(a, b):
    ah, al = a
    bh, bl = b
    return dot(ah, bh) + (dot(ah, bl) + dot(al, bh))


def np_split(x):
    hi = x.astype(np.float32).astype(jnp.bfloat16)
    lo = (x - hi.astype(np.float64)).astype(np.float32).astype(jnp.bfloat16)
    return hi, lo


def polynomial():
    deg = 7
    nodes = np.cos(np.pi * (np.arange(deg + 1) + 0.5) / (deg + 1))
    g = 4.0 * nodes
    x = 128.0 + SHIFT - 32.0 * g

    def cheb(n, t):
        return np.where(
            np.abs(t) <= 1,
            np.cos(n * np.arccos(np.clip(t, -1, 1))),
            np.sign(t) ** n * np.cosh(n * np.arccosh(np.maximum(np.abs(t), 1))),
        )

    def tau(v):
        return (TOP + LOW - 2 * v) / (TOP - LOW)

    top = cheb(deg + 1, tau(0.0))
    vals = (1.0 - cheb(deg + 1, tau(x)) / top) / x
    coef = np.polynomial.polynomial.polyfit(nodes, vals, deg)
    at_one = np.polynomial.polynomial.polyval(1.0, coef)
    const = (1.0 / (SHIFT + SIGMA) - at_one) / SUBS
    return [float(c / 4.0**k) for k, c in enumerate(coef)], float(const), float(1.0 / top)


def constants():
    o = np.arange(SIDE) + 1.0
    step = math.pi / (SIDE + 1.0)
    sine = math.sqrt(2.0 / (SIDE + 1.0)) * np.sin(step * o[:, None] * o[None, :])
    lam = 2.0 - 2.0 * np.cos(step * o)
    inv = np.repeat(1.0 / (lam[:, None] + lam[None, :]), 8, axis=0)
    lanes = np.arange(128)
    side, kk = lanes // SIDE, lanes % SIDE
    m = np.arange(SUBS)
    cmp = ((lanes // 8)[:, None] == (m // EACH // PLANE)[None]) & ((lanes % 8)[:, None] == (m % EACH)[None])
    rev = (side[:, None] == side[None]) & (kk[:, None] == 31 - kk[None])
    s8 = np.concatenate(np_split(np.kron(sine, np.eye(8))), axis=0)
    s = np.concatenate([np.pad(a, ((0, 0), (0, 128 - SIDE))) for a in np_split(sine)], axis=0)
    ends = np.zeros((SIDE, 128))
    ends[:, 32:64] = sine[:, 31:32]
    ends[:, 96:] = sine[:, 0:1]
    quad = np.kron(np.eye(4), sine)
    rev = rev.astype(np.float32).astype(jnp.bfloat16)
    small = np.concatenate([s, *np_split(ends), *np_split(quad), rev], axis=0)
    wide = cmp.astype(np.float32).astype(jnp.bfloat16)
    return s8, small, wide, inv.astype(np.float32)


def by_row(v):
    return v.reshape(SIDE, 8, 128)


def stack_fields(first, second):
    return jnp.concatenate([first, second, jnp.zeros((2, first.shape[1]), F32)], axis=0)


def to_field(x):
    lane = iota((8, 128), 1)
    rows = []
    for i in range(SIDE):
        g, h = i // 4, i % 4
        part = x[:, 128 * g : 128 * g + 128]
        part = part if h == 0 else roll(part, 128 - 32 * h, 1)
        rows.append(jnp.where(lane < SIDE, part, 0.0))
    return jnp.concatenate(rows, axis=0)


def from_field(v):
    parts = []
    for g in range(8):
        total = v[4 * g]
        for h in (1, 2, 3):
            total = total + roll(v[4 * g + h], 32 * h, 1)
        parts.append(total)
    return jnp.concatenate(parts, axis=1)


def coefficients(r, c):
    v = mm3(c["s8"], split(r[:, :SIDE], 2))
    return mm3(split(v, 2), c["s"])[:, :SIDE] * c["inv"]


def local_rims(x, c):
    w = by_row(mm3(split(x, 2), c["ends"]))
    f = x.reshape(SIDE, 8, SIDE)
    lane = iota((8, 128), 1) & 63
    scale = [math.sqrt(2.0 / 33.0) * math.sin(math.pi * (i + 1) / 33.0) for i in range(SIDE)]
    even = sum(scale[i] * f[i] for i in range(0, SIDE, 2))
    odd = sum(scale[i] * f[i] for i in range(1, SIDE, 2))
    blank = jnp.zeros((8, SIDE), F32)
    tile = jnp.concatenate([even + odd, blank, even - odd, blank], axis=1)
    for i in range(SIDE):
        tile = jnp.where(lane == 32 + i, w[i], tile)
    th, tl = split(tile, 2)
    qh, ql = c["quad"]
    both = dot(stack([th, tl]), qh)
    return both[:8] + (both[8:] + dot(th, ql))


def local_field(x, c):
    v = mm3(split(x, 2), c["s"])
    return mm3(c["s8"], split(v, 2))


def packed(v, place):
    total = jnp.sum(jnp.sum(by_row(v), axis=0), axis=1, keepdims=True)
    at = iota((8, 128), 1) == place * 8 + iota((8, 128), 0)
    return jnp.sum(jnp.where(at, total, 0.0), axis=0, keepdims=True)


def tile_a(rims, sums, mass):
    row = iota((8, 128), 0)
    return jnp.where(row == 6, sums, jnp.where(row == 7, mass, rims))


def tables(nb, ns, fl, t):
    plane, q = t // PLANE, t % PLANE
    row, lane = iota((136, SUBS), 0), iota((136, SUBS), 1)
    target = jnp.where(row < 128, lax.shift_right_logical(row, jnp.int32(3)), q)
    field = row & 7
    sub = (plane * PLANE + target) * EACH + jnp.where(field >= EACH, field - EACH, field)
    take = (lane == sub) & (field < 6)

    def column(a, s):
        return jnp.sum(jnp.where(take, a[s : s + 1].astype(F32), 0.0), axis=1, keepdims=True)

    nbs = [column(nb, s).astype(jnp.int32) for s in range(4)]
    nss = [column(ns, s).astype(jnp.int32) for s in range(4)]
    fls = [column(fl, s) for s in range(4)]

    field = iota((128, 1), 0) & 7
    third = jnp.where(field >= EACH, EACH, 0)
    cols = iota((128, 256), 1)
    choose = []
    for s in range(4):
        sub = nbs[s][:128]
        device = lax.shift_right_logical(sub * 21846, jnp.int32(16))
        at = ((s - nss[s][:128]) & 3) * 64 + lax.shift_right_logical(device, jnp.int32(4)) * 8 + (sub - EACH * device) + third
        inside = ((device & 15) == q) & (field < 6)
        choose.append((cols == jnp.where(inside, at, -1)).astype(F32).astype(BF16))

    field, lane = iota((8, SUBS), 0), iota((8, SUBS), 1)
    own = (lane == t * EACH + jnp.where(field >= EACH, field - EACH, field)).astype(F32)
    rows = []
    for s in range(4):
        rows.append(jnp.where(field < 6, own - (lane == nbs[s][128:136]).astype(F32), 0.0))
    rows.append(jnp.where(field < 6, own, jnp.where(field == 6, 1.0, 0.0)))
    group = lax.shift_right_logical(iota((8, 128), 1), jnp.int32(5))
    flip = jnp.zeros((8, 128), F32)
    for s in range(4):
        flip = jnp.where(group == s, fls[s][128:136], flip)
    return jnp.concatenate(choose, axis=0), jnp.concatenate(rows, axis=0).astype(BF16), flip


def tiles_b(buf, choose):
    flat = buf.reshape(64, 128)
    turned = jnp.concatenate([flat] + [roll(flat, 32 * t, 1) for t in (1, 2, 3)], axis=0)
    a, b, c = split(turned, 3)
    wide = dot(choose, jnp.concatenate([a, b], axis=1))
    got = (wide[:, :128] + wide[:, 128:]) + dot(choose, c)
    group = lax.shift_right_logical(iota((128, 128), 1), jnp.int32(5))
    out = jnp.where(group == 0, got[:128], 0.0)
    for s in (1, 2, 3):
        out = jnp.where(group == s, got[128 * s : 128 * s + 128], out)
    row = iota((8, 128), 0)
    column = jnp.where(row >= 6, jnp.sum(buf, axis=0), 0.0)
    return out.reshape(PLANE, 8, 128) + column[None]


def graph(nb):
    row = iota((SUBS, SUBS), 0)
    total = jnp.zeros((SUBS, SUBS), F32)
    for s in range(4):
        total = total + (row == nb[s : s + 1]).astype(F32)
    return total


def start_inverse(g32):
    coef, const, rho = polynomial()
    g = g32.astype(BF16)
    g2 = dot(g, g)
    g2b = g2.astype(BF16)
    g3 = dot(g2b, g)
    g4 = dot(g2b, g2b)
    g3b, g4b = g3.astype(BF16), g4.astype(BF16)
    eye = (iota((SUBS, SUBS), 0) == iota((SUBS, SUBS), 1)).astype(F32)
    x = coef[0] * eye + const + coef[1] * g32 + coef[2] * g2 + coef[3] * g3 + coef[4] * g4
    x = x + coef[5] * dot(g4b, g) + coef[6] * dot(g4b, g2b) + coef[7] * dot(g4b, g3b)
    return x, rho


def newton(x, g, rho, last):
    xs = split(x, 3 if last else 2)
    gx = dot(g, xs[0]) + dot(g, xs[1])
    if last:
        gx = gx + dot(g, xs[2])
    ones = (SIGMA / SUBS) * jnp.sum(x, axis=0, keepdims=True)
    eye = (iota((SUBS, SUBS), 0) == iota((SUBS, SUBS), 1)).astype(F32)
    rest = eye - ((128.0 + SHIFT) * x - 32.0 * gx + ones)
    x = x + mm3(xs[:2], split(rest, 2))
    if last:
        return x, 0.0
    scale = 2.0 / (2.0 - rho * rho)
    return scale * x, rho * rho / (2.0 - rho * rho)


def to_vectors(slots, c):
    wide = spread(slots, c["cmp"])
    row, lane = iota((PLANE, SUBS), 0), iota((PLANE, SUBS), 1)
    keep = (lax.shift_right_logical(lane * 21846, jnp.int32(16)) & 15) == row
    rows = []
    for k in range(slots.shape[0] // PLANE):
        block = wide[PLANE * k : PLANE * k + PLANE]
        rows.append(jnp.sum(jnp.where(keep, block, 0.0), axis=0, keepdims=True))
    return rows


def inverse_rows(first, xh, xl, mass):
    delta = mass - SHIFT

    def apply(d, fine):
        e = d * delta
        if not fine:
            return d + dot(e.astype(BF16), xh)
        eh, el = split(e, 2)
        n = e.shape[0]
        high = dot(stack([eh, el]), xh)
        return d + (high[:n] + (high[n:] + dot(eh, xl)))

    sig = 1.0 / RHO
    rk = 1.0 / sig
    rest = first
    d = rest
    y = d
    for k in range(CHEB):
        rest = rest - apply(d, k < 3)
        nxt = 1.0 / (2.0 * sig - rk)
        d = (nxt * rk) * d + (2.0 * nxt / RHO) * rest
        y = y + d
        rk = nxt
    u = y[38:39]
    t = jnp.sum(u, axis=1, keepdims=True)
    w = jnp.sum(y, axis=1, keepdims=True)
    share = (SIGMA / SUBS) / (1.0 - (SIGMA / SUBS) * t)
    return y + (w * share) * u


def coarse_parts(y, s0, s1):
    row = iota((8, SUBS), 0)
    s = jnp.where(row < EACH, s0, s1)
    group = lax.shift_right_logical(iota((8, 128), 1), jnp.int32(5))
    edges = jnp.zeros((8, 128), F32)
    for k in range(4):
        edges = jnp.where(group == k, jnp.sum(y[8 * k : 8 * k + 8] * s, axis=1, keepdims=True), edges)
    own = jnp.sum(y[32:40] * s, axis=1, keepdims=True)
    at = (iota((8, 128), 1) < SIDE) & (iota((8, 128), 0) < 6)
    return edges, jnp.where(at, own, 0.0)


def finish(r, local, mass, rims, flip, edges, own, c):
    turned = spread(rims, c["rev"])
    rims = jnp.where(flip > 0.5, turned, rims)
    e = jnp.where(iota((8, 128), 0) < 6, edges - rims, 0.0)
    lane = iota((8, 128), 1)
    left = roll(e, 33, 1)
    both = jnp.where((lane >= 1) & (lane < 32), left, jnp.where((lane >= 32) & (lane < 64), e, 0.0))
    f, fr, fm = by_row(local), by_row(r), by_row(mass)
    z, image = [], []
    for i in range(SIDE):
        zi = f[i] + own
        moved = roll(both, 127 - i, 1)
        if i == 31:
            moved = jnp.where(lane == 0, roll(left, 96, 1), moved)
        extra = jnp.where((lane == 0) | (lane == 31), moved, 0.0)
        if i == 0:
            extra = extra + jnp.where(lane < SIDE, e, 0.0)
        if i == 31:
            extra = extra + jnp.where(lane < SIDE, roll(e, 64, 1), 0.0)
        z.append(zi)
        image.append(fr[i] + fm[i] * zi + extra)
    return jnp.concatenate(z, axis=0), jnp.concatenate(image, axis=0)


def dots_tile(pairs, first):
    lane, row = iota((8, 128), 1), iota((8, 128), 0)
    total = jnp.zeros((8, 128), F32)
    for k, (a, b) in enumerate(pairs, first):
        one = jnp.sum(jnp.sum(by_row(a * b), axis=0), axis=1, keepdims=True)
        at = ((lane == k) & (row < EACH)) | ((lane == 6 + k) & (row >= EACH) & (row < 6))
        total = jnp.where(at, one, total)
    return total


def steps(row, p):
    ga, de, rw, qw, zv, wv = [row[:, 6 * p + k : 6 * p + k + 1] for k in range(6)]
    a0 = ga / de
    g1 = ga - a0 * (de + rw) + a0 * a0 * qw
    d1 = de - a0 * (qw + zv) + a0 * a0 * wv
    beta = g1 / ga
    cross = de - a0 * (0.5 * (qw + zv))
    den = d1 + 2.0 * beta * cross + beta * beta * de
    a1 = g1 / den
    return a0 + a1 * (1.0 + beta), a1 * a0


def kernel(src_hbm, mass_hbm, nb_hbm, ns_hbm, fl_hbm, s8_hbm, small_hbm, wide_hbm, inv_hbm, out_ref,
           src_v, mass_v, nb_v, ns_v, fl_v, s8_v, small_v, wide_v, inv_v,
           r_v, m_v, l_v, choose_v, e0_v, flip_v, x_v, g_v, xh_v, xl_v, first_v,
           stga0, stga1, bufa0, bufa1, stgb0, stgb1, bufb0, bufb1, st3a, st3b, buf3a, buf3b,
           nat_v, stgm, bufm, y_v, edge_v, own_v, dots_v, insem, ssem, rsem, opensem, farsem):
    t = lax.axis_index("tile")
    lev = lax.axis_index("lev")
    plane, q = t // PLANE, t % PLANE
    line, x_at = q // LINE, q % LINE
    ready = t >= 0

    def at(dy, dz, dx, dl):
        where = ((plane + dy) % COLUMN * LINE + (line + dz) % LINE) * LINE + (x_at + dx) % LINE
        return (where, (lev + dl) % LEVS)

    a_peers = [(dy, 0, 0, 0) for dy in (4, 3, 5, 2, 6, 1, 7)]
    b_peers = [(0, dz, dx, 0) for dz in (3, 2, 1, 0) for dx in (2, 1, 3, 0) if dz or dx]
    xy_peers = [(dy, 0, dx, 0) for dy in (4, 3, 5, 2, 6, 1, 7, 0) for dx in (2, 1, 3, 0) if dy or dx]
    zc_peers = [(0, dz, 0, dl) for dz in (3, 2, 1, 0) for dl in range(LEVS) if dz or dl]
    l_peers = [(0, 0, 0, dl) for dl in (2, 3, 4, 5, 1)]
    far_peers = [(0, 1, 2, 0), (0, 3, 2, 0)]
    between = [(0, 1, 0, 0), (0, 3, 0, 0)]
    everyone = a_peers + l_peers + [peer for peer in b_peers if peer not in far_peers]

    moves = [(src_hbm.at[p, n], src_v.at[pl.ds(p * EACH + n, 1)]) for p in range(2) for n in range(EACH)]
    moves += [(mass_hbm, mass_v), (s8_hbm, s8_v), (small_hbm, small_v), (inv_hbm, inv_v),
              (nb_hbm, nb_v), (ns_hbm, ns_v), (fl_hbm, fl_v), (wide_hbm, wide_v)]
    copies = [pltpu.make_async_copy(a, b, insem.at[k]) for k, (a, b) in enumerate(moves)]
    for copy in copies:
        copy.start()

    barrier = pltpu.get_barrier_semaphore()
    for peer in everyone:
        pl.semaphore_signal(barrier, 1, device_id=at(*peer), device_id_type=pl.DeviceIdType.MESH)

    for copy in copies:
        copy.wait()

    def spot(peer):
        return (line + peer[1]) % LINE * LINE + (x_at + peer[2]) % LINE

    def send(peers, src_of, dst, n):
        for peer in peers:
            pltpu.make_async_remote_copy(
                src_ref=src_of(peer), dst_ref=dst, send_sem=ssem.at[n], recv_sem=rsem.at[n],
                device_id=at(*peer), device_id_type=pl.DeviceIdType.MESH,
            ).start()

    def done(peers, buf, n, recv):
        view = buf.at[pl.ds(0, len(peers))]
        copy = pltpu.make_async_remote_copy(
            src_ref=view, dst_ref=view, send_sem=ssem.at[n], recv_sem=rsem.at[n],
            device_id=at(*peers[0]), device_id_type=pl.DeviceIdType.MESH,
        )
        if recv:
            copy.wait_recv()
        else:
            copy.wait_send()

    def consts():
        return {
            "s8": (s8_v[:256], s8_v[256:]),
            "s": (small_v[:SIDE], small_v[SIDE : 2 * SIDE]),
            "ends": (small_v[64:96], small_v[96:128]),
            "quad": (small_v[128:256], small_v[256:384]),
            "rev": small_v[384:],
            "inv": inv_v[...],
            "cmp": wide_v[...],
        }

    c = consts()
    zrow = jnp.zeros((1, 128), F32)

    first = src_v[...]
    r = to_field(jnp.where(iota(first.shape, 0) < 6, first, 0.0))
    mass = to_field(stack_fields(mass_v[...], mass_v[...]))
    r_v[...] = r
    m_v[...] = mass
    x0 = coefficients(r, c)
    rims = local_rims(x0, c)
    tile = tile_a(rims, packed(r, plane), packed(mass, plane))
    stga0[...] = tile
    bufa0[plane] = tile
    pl.semaphore_wait(barrier, len(everyone))
    send(a_peers, lambda peer: stga0, bufa0.at[plane], 0)
    for peer in between:
        pl.semaphore_signal(farsem, 1, device_id=at(*peer), device_id_type=pl.DeviceIdType.MESH)

    polys = polynomial()[2]
    rhos = [polys]
    for _ in range(2):
        rhos.append(rhos[-1] ** 2 / (2.0 - rhos[-1] ** 2))

    @pl.when(ready)
    def _():
        l_v[...] = local_field(x0, c)
        choose, e0, flip = tables(nb_v[...], ns_v[...], fl_v[...], t)
        choose_v[...] = choose
        e0_v[...] = e0
        flip_v[...] = flip
        g32 = graph(nb_v[...])
        g_v[...] = g32.astype(BF16)
        x_v[...] = start_inverse(g32)[0]

    @pl.when(ready)
    def _():
        x_v[...] = newton(x_v[...], g_v[...], rhos[0], False)[0]

    done(a_peers, bufa0, 0, True)
    pl.semaphore_wait(farsem, len(between))
    total = jnp.sum(bufa0[...], axis=0)[6:8]
    stgm[...] = total
    bufm[q] = total
    send(b_peers, lambda peer: stgm, bufm.at[q], 6)
    stgb0[...] = tiles_b(bufa0[...], choose_v[...])
    bufb0[q] = stgb0[q]
    send(b_peers, lambda peer: stgb0.at[spot(peer)], bufb0.at[q], 1)

    @pl.when(ready)
    def _():
        x_v[...] = newton(x_v[...], g_v[...], rhos[1], False)[0]

    @pl.when(ready)
    def _():
        x = newton(x_v[...], g_v[...], rhos[2], True)[0]
        xs = split(x, 3)
        e0 = e0_v[...]
        first_v[...] = dot(e0, xs[0]) + (dot(e0, xs[1]) + dot(e0, xs[2]))
        xh_v[...] = xs[0]
        xl_v[...] = xs[1]

    done(b_peers, bufm, 6, True)

    @pl.when(ready)
    def _():
        sums = bufm[:, 0, :]
        three = jnp.concatenate([bufm[:, 1, :], sums, roll(sums, 128 - EACH, 1)], axis=0)
        dvec, s0, s1 = to_vectors(three, consts())
        y = inverse_rows(first_v[...], xh_v[...], xl_v[...], dvec)
        y_v[...] = y
        edge_v[...], own_v[...] = coarse_parts(y, s0, s1)

    done(b_peers, bufb0, 1, True)
    for peer in l_peers:
        pl.semaphore_signal(opensem, 1, device_id=at(*peer), device_id_type=pl.DeviceIdType.MESH)
    c = consts()
    flip = flip_v[...]
    r, mass = r_v[...], m_v[...]
    z0, q0 = finish(r, l_v[...], mass, jnp.sum(bufb0[...], axis=0), flip, edge_v[...], own_v[...], c)

    x1 = coefficients(q0, c)
    rims = local_rims(x1, c)
    tile = tile_a(rims, packed(q0, plane), zrow)
    stga1[...] = tile
    bufa1[plane] = tile
    send(a_peers, lambda peer: stga1, bufa1.at[plane], 2)

    @pl.when(ready)
    def _():
        l_v[...] = local_field(x1, c)
        dots_v[...] = dots_tile(((r, z0), (z0, q0)), 0)

    done(a_peers, bufa1, 2, True)
    stgb1[...] = tiles_b(bufa1[...], choose_v[...])
    bufb1[q] = stgb1[q]
    send(b_peers, lambda peer: stgb1.at[spot(peer)], bufb1.at[q], 3)
    done(b_peers, bufb1, 3, True)
    sums = bufb1[:, 6, :]
    s0, s1 = to_vectors(jnp.concatenate([sums, roll(sums, 128 - EACH, 1)], axis=0), c)
    edges, own = coarse_parts(y_v[...], s0, s1)
    w, v = finish(q0, l_v[...], mass, jnp.sum(bufb1[...], axis=0), flip, edges, own, c)

    tile = dots_v[...] + dots_tile(((r, w), (q0, w), (z0, v), (w, v)), 2)
    row = jnp.sum(tile, axis=0, keepdims=True)
    st3a[...] = row
    buf3a[plane * LINE + x_at] = row
    send(xy_peers, lambda peer: st3a, buf3a.at[plane * LINE + x_at], 4)

    @pl.when(ready)
    def _():
        for k, field in enumerate((z0, q0, w, v)):
            nat_v[k] = from_field(by_row(field))

    done(xy_peers, buf3a, 4, True)
    row = jnp.sum(buf3a[...], axis=0)
    st3b[...] = row
    buf3b[line * LEVS + lev] = row
    pl.semaphore_wait(opensem, len(l_peers))
    send(zc_peers, lambda peer: st3b, buf3b.at[line * LEVS + lev], 5)
    done(zc_peers, buf3b, 5, True)
    row = jnp.sum(buf3b[...], axis=0)

    upper = iota((8, 1), 0) < EACH
    a0, b0 = steps(row, 0)
    a1, b1 = steps(row, 1)
    a, b = jnp.where(upper, a0, a1), jnp.where(upper, b0, b1)
    outs = [a * nat_v[0] - b * nat_v[2], src_v[...] - a * nat_v[1] + b * nat_v[3]]
    for k, out in enumerate(outs):
        for p in range(2):
            for n in range(EACH):
                out_ref[k, p, n] = out[p * EACH + n : p * EACH + n + 1]

    done(a_peers, bufa0, 0, False)
    done(b_peers, bufb0, 1, False)
    done(a_peers, bufa1, 2, False)
    done(b_peers, bufb1, 3, False)
    done(xy_peers, buf3a, 4, False)
    done(zc_peers, buf3b, 5, False)
    done(b_peers, bufm, 6, False)


def shards(sources, mass_coef, neighbour_sub, neighbour_side, side_flip):
    s8, small, wide, inv = [jnp.asarray(a) for a in constants()]
    hbm = pl.BlockSpec(memory_space=pltpu.HBM)
    rows = sources.transpose(0, 2, 1, 3)
    args = [rows, mass_coef, neighbour_sub.T, neighbour_side.T, side_flip.T, s8, small, wide, inv]
    one = pltpu.VMEM((8, 128), F32)
    line = pltpu.VMEM((1, 128), F32)
    field = pltpu.VMEM((ROWS, 128), F32)
    square = lambda kind: pltpu.VMEM((SUBS, SUBS), kind)
    plane = pltpu.VMEM((PLANE, 8, 128), F32)
    column = pltpu.VMEM((COLUMN, 8, 128), F32)
    scratch = [pltpu.VMEM((8, SIDE * SIDE), F32)] + [pltpu.VMEM(a.shape, a.dtype) for a in args[1:]] + [
        field, field, field, pltpu.VMEM((512, 256), BF16), pltpu.VMEM((40, SUBS), BF16), one,
        square(F32), square(BF16), square(BF16), square(BF16), pltpu.VMEM((40, SUBS), F32),
        one, one, column, column, plane, plane, plane, plane, line, line,
        pltpu.VMEM((COLUMN * LINE, 1, 128), F32), pltpu.VMEM((LINE * LEVS, 1, 128), F32),
        pltpu.VMEM((4, 8, SIDE * SIDE), F32),
        pltpu.VMEM((2, 128), F32), pltpu.VMEM((PLANE, 2, 128), F32), pltpu.VMEM((40, SUBS), F32), one, one, one,
        pltpu.SemaphoreType.DMA((14,)),
        pltpu.SemaphoreType.DMA((7,)), pltpu.SemaphoreType.DMA((7,)), pltpu.SemaphoreType.REGULAR, pltpu.SemaphoreType.REGULAR,
    ]
    out = pltpu.VMEM((2,) + rows.shape, F32)
    both = pl.pallas_call(
        kernel,
        out_shape=out,
        in_specs=[hbm] * len(args),
        out_specs=pl.BlockSpec(memory_space=pltpu.VMEM),
        scratch_shapes=scratch,
        compiler_params=pltpu.CompilerParams(collective_id=0, has_side_effects=True, vmem_limit_bytes=60 << 20),
        name="schwarz",
    )(*args)
    both = both.transpose(0, 1, 3, 2, 4)
    return both[0], both[1]


def solution(mesh):
    placed = (P(None, "lev", "tile", None), P("tile", None), P(), P(), P())
    return jax.shard_map(
        shards,
        mesh=mesh,
        in_specs=placed,
        out_specs=(P(None, "lev", "tile", None), P(None, "lev", "tile", None)),
        check_vma=False,
    )
```

```python
import math

import jax
import jax.numpy as jnp
import numpy as np
from jax import lax
from jax.experimental import pallas as pl
from jax.experimental.pallas import tpu as pltpu
from jax.sharding import PartitionSpec as P

F32 = jnp.float32
BF16 = jnp.bfloat16
SIDE = 32
SUBS = 384
PLANE = 16
COLUMN = 8
LEVS = 6
EACH = 3
LINE = 4
ROWS = 8 * SIDE

SHIFT = 1.28
SIGMA = 3.0
LOW = 32.0 * 0.06486 + SHIFT
TOP = 32.0 * 8.0 + SHIFT
RHO = 0.7681 / LOW
CHEB = 6


def roll(x, shift, axis):
    return pltpu.roll(x, shift, axis)


def iota(shape, dim):
    return lax.broadcasted_iota(jnp.int32, shape, dim)


def dot(a, b):
    return jnp.dot(a, b, preferred_element_type=F32)


def split(x, n):
    parts = []
    for _ in range(n):
        part = x.astype(BF16)
        parts.append(part)
        x = x - part.astype(F32)
    return parts


def stack(parts):
    return jnp.concatenate([part.astype(F32) for part in parts], axis=0).astype(BF16)


def spread(x, onehot):
    n = x.shape[0]
    out = dot(stack(split(x, 3)), onehot)
    return out[:n] + out[n : 2 * n] + out[2 * n :]


def mm3(a, b):
    ah, al = a
    bh, bl = b
    return dot(ah, bh) + (dot(ah, bl) + dot(al, bh))


def np_split(x):
    hi = x.astype(np.float32).astype(jnp.bfloat16)
    lo = (x - hi.astype(np.float64)).astype(np.float32).astype(jnp.bfloat16)
    return hi, lo


def polynomial():
    deg = 7
    nodes = np.cos(np.pi * (np.arange(deg + 1) + 0.5) / (deg + 1))
    g = 4.0 * nodes
    x = 128.0 + SHIFT - 32.0 * g

    def cheb(n, t):
        return np.where(
            np.abs(t) <= 1,
            np.cos(n * np.arccos(np.clip(t, -1, 1))),
            np.sign(t) ** n * np.cosh(n * np.arccosh(np.maximum(np.abs(t), 1))),
        )

    def tau(v):
        return (TOP + LOW - 2 * v) / (TOP - LOW)

    top = cheb(deg + 1, tau(0.0))
    vals = (1.0 - cheb(deg + 1, tau(x)) / top) / x
    coef = np.polynomial.polynomial.polyfit(nodes, vals, deg)
    at_one = np.polynomial.polynomial.polyval(1.0, coef)
    const = (1.0 / (SHIFT + SIGMA) - at_one) / SUBS
    return [float(c / 4.0**k) for k, c in enumerate(coef)], float(const), float(1.0 / top)


def constants():
    o = np.arange(SIDE) + 1.0
    step = math.pi / (SIDE + 1.0)
    sine = math.sqrt(2.0 / (SIDE + 1.0)) * np.sin(step * o[:, None] * o[None, :])
    lam = 2.0 - 2.0 * np.cos(step * o)
    inv = np.repeat(1.0 / (lam[:, None] + lam[None, :]), 8, axis=0)
    lanes = np.arange(128)
    side, kk = lanes // SIDE, lanes % SIDE
    m = np.arange(SUBS)
    cmp = ((lanes // 8)[:, None] == (m // EACH // PLANE)[None]) & ((lanes % 8)[:, None] == (m % EACH)[None])
    rev = (side[:, None] == side[None]) & (kk[:, None] == 31 - kk[None])
    s8 = np.concatenate(np_split(np.kron(sine, np.eye(8))), axis=0)
    s = np.concatenate([np.pad(a, ((0, 0), (0, 128 - SIDE))) for a in np_split(sine)], axis=0)
    ends = np.zeros((SIDE, 128))
    ends[:, 32:64] = sine[:, 31:32]
    ends[:, 96:] = sine[:, 0:1]
    quad = np.kron(np.eye(4), sine)
    rev = rev.astype(np.float32).astype(jnp.bfloat16)
    small = np.concatenate([s, *np_split(ends), *np_split(quad), rev], axis=0)
    wide = cmp.astype(np.float32).astype(jnp.bfloat16)
    return s8, small, wide, inv.astype(np.float32)


def by_row(v):
    return v.reshape(SIDE, 8, 128)


def stack_fields(first, second):
    return jnp.concatenate([first, second, jnp.zeros((2, first.shape[1]), F32)], axis=0)


def to_field(x):
    lane = iota((8, 128), 1)
    rows = []
    for i in range(SIDE):
        g, h = i // 4, i % 4
        part = x[:, 128 * g : 128 * g + 128]
        part = part if h == 0 else roll(part, 128 - 32 * h, 1)
        rows.append(jnp.where(lane < SIDE, part, 0.0))
    return jnp.concatenate(rows, axis=0)


def from_field(v):
    parts = []
    for g in range(8):
        total = v[4 * g]
        for h in (1, 2, 3):
            total = total + roll(v[4 * g + h], 32 * h, 1)
        parts.append(total)
    return jnp.concatenate(parts, axis=1)


def coefficients(r, c):
    v = mm3(c["s8"], split(r[:, :SIDE], 2))
    return mm3(split(v, 2), c["s"])[:, :SIDE] * c["inv"]


def local_rims(x, c):
    w = by_row(mm3(split(x, 2), c["ends"]))
    f = x.reshape(SIDE, 8, SIDE)
    lane = iota((8, 128), 1) & 63
    scale = [math.sqrt(2.0 / 33.0) * math.sin(math.pi * (i + 1) / 33.0) for i in range(SIDE)]
    even = sum(scale[i] * f[i] for i in range(0, SIDE, 2))
    odd = sum(scale[i] * f[i] for i in range(1, SIDE, 2))
    blank = jnp.zeros((8, SIDE), F32)
    tile = jnp.concatenate([even + odd, blank, even - odd, blank], axis=1)
    for i in range(SIDE):
        tile = jnp.where(lane == 32 + i, w[i], tile)
    th, tl = split(tile, 2)
    qh, ql = c["quad"]
    both = dot(stack([th, tl]), qh)
    return both[:8] + (both[8:] + dot(th, ql))


def local_field(x, c):
    v = mm3(split(x, 2), c["s"])
    return mm3(c["s8"], split(v, 2))


def packed(v, place):
    total = jnp.sum(jnp.sum(by_row(v), axis=0), axis=1, keepdims=True)
    at = iota((8, 128), 1) == place * 8 + iota((8, 128), 0)
    return jnp.sum(jnp.where(at, total, 0.0), axis=0, keepdims=True)


def tile_a(rims, sums, mass):
    row = iota((8, 128), 0)
    return jnp.where(row == 6, sums, jnp.where(row == 7, mass, rims))


def tables(nb, ns, fl, t):
    plane, q = t // PLANE, t % PLANE
    row, lane = iota((136, SUBS), 0), iota((136, SUBS), 1)
    target = jnp.where(row < 128, lax.shift_right_logical(row, jnp.int32(3)), q)
    field = row & 7
    sub = (plane * PLANE + target) * EACH + jnp.where(field >= EACH, field - EACH, field)
    take = (lane == sub) & (field < 6)

    def column(a, s):
        return jnp.sum(jnp.where(take, a[s : s + 1].astype(F32), 0.0), axis=1, keepdims=True)

    nbs = [column(nb, s).astype(jnp.int32) for s in range(4)]
    nss = [column(ns, s).astype(jnp.int32) for s in range(4)]
    fls = [column(fl, s) for s in range(4)]

    field = iota((128, 1), 0) & 7
    third = jnp.where(field >= EACH, EACH, 0)
    cols = iota((128, 256), 1)
    choose = []
    for s in range(4):
        sub = nbs[s][:128]
        device = lax.shift_right_logical(sub * 21846, jnp.int32(16))
        at = ((s - nss[s][:128]) & 3) * 64 + lax.shift_right_logical(device, jnp.int32(4)) * 8 + (sub - EACH * device) + third
        inside = ((device & 15) == q) & (field < 6)
        choose.append((cols == jnp.where(inside, at, -1)).astype(F32).astype(BF16))

    field, lane = iota((8, SUBS), 0), iota((8, SUBS), 1)
    own = (lane == t * EACH + jnp.where(field >= EACH, field - EACH, field)).astype(F32)
    rows = []
    for s in range(4):
        rows.append(jnp.where(field < 6, own - (lane == nbs[s][128:136]).astype(F32), 0.0))
    rows.append(jnp.where(field < 6, own, jnp.where(field == 6, 1.0, 0.0)))
    group = lax.shift_right_logical(iota((8, 128), 1), jnp.int32(5))
    flip = jnp.zeros((8, 128), F32)
    for s in range(4):
        flip = jnp.where(group == s, fls[s][128:136], flip)
    return jnp.concatenate(choose, axis=0), jnp.concatenate(rows, axis=0).astype(BF16), flip


def tiles_b(buf, choose):
    flat = buf.reshape(64, 128)
    turned = jnp.concatenate([flat] + [roll(flat, 32 * t, 1) for t in (1, 2, 3)], axis=0)
    a, b, c = split(turned, 3)
    wide = dot(choose, jnp.concatenate([a, b], axis=1))
    got = (wide[:, :128] + wide[:, 128:]) + dot(choose, c)
    group = lax.shift_right_logical(iota((128, 128), 1), jnp.int32(5))
    out = jnp.where(group == 0, got[:128], 0.0)
    for s in (1, 2, 3):
        out = jnp.where(group == s, got[128 * s : 128 * s + 128], out)
    row = iota((8, 128), 0)
    column = jnp.where(row >= 6, jnp.sum(buf, axis=0), 0.0)
    return out.reshape(PLANE, 8, 128) + column[None]


def graph(nb):
    row = iota((SUBS, SUBS), 0)
    total = jnp.zeros((SUBS, SUBS), F32)
    for s in range(4):
        total = total + (row == nb[s : s + 1]).astype(F32)
    return total


def start_inverse(g32):
    coef, const, rho = polynomial()
    g = g32.astype(BF16)
    g2 = dot(g, g)
    g2b = g2.astype(BF16)
    g3 = dot(g2b, g)
    g4 = dot(g2b, g2b)
    g3b, g4b = g3.astype(BF16), g4.astype(BF16)
    eye = (iota((SUBS, SUBS), 0) == iota((SUBS, SUBS), 1)).astype(F32)
    x = coef[0] * eye + const + coef[1] * g32 + coef[2] * g2 + coef[3] * g3 + coef[4] * g4
    x = x + coef[5] * dot(g4b, g) + coef[6] * dot(g4b, g2b) + coef[7] * dot(g4b, g3b)
    return x, rho


def newton(x, g, rho, last):
    xs = split(x, 3 if last else 2)
    gx = dot(g, xs[0]) + dot(g, xs[1])
    if last:
        gx = gx + dot(g, xs[2])
    ones = (SIGMA / SUBS) * jnp.sum(x, axis=0, keepdims=True)
    eye = (iota((SUBS, SUBS), 0) == iota((SUBS, SUBS), 1)).astype(F32)
    rest = eye - ((128.0 + SHIFT) * x - 32.0 * gx + ones)
    x = x + mm3(xs[:2], split(rest, 2))
    if last:
        return x, 0.0
    scale = 2.0 / (2.0 - rho * rho)
    return scale * x, rho * rho / (2.0 - rho * rho)


def to_vectors(slots, c):
    wide = spread(slots, c["cmp"])
    row, lane = iota((PLANE, SUBS), 0), iota((PLANE, SUBS), 1)
    keep = (lax.shift_right_logical(lane * 21846, jnp.int32(16)) & 15) == row
    rows = []
    for k in range(slots.shape[0] // PLANE):
        block = wide[PLANE * k : PLANE * k + PLANE]
        rows.append(jnp.sum(jnp.where(keep, block, 0.0), axis=0, keepdims=True))
    return rows


def inverse_rows(first, xh, xl, mass):
    delta = mass - SHIFT

    def apply(d, fine):
        e = d * delta
        if not fine:
            return d + dot(e.astype(BF16), xh)
        eh, el = split(e, 2)
        n = e.shape[0]
        high = dot(stack([eh, el]), xh)
        return d + (high[:n] + (high[n:] + dot(eh, xl)))

    sig = 1.0 / RHO
    rk = 1.0 / sig
    rest = first
    d = rest
    y = d
    for k in range(CHEB):
        rest = rest - apply(d, k < 3)
        nxt = 1.0 / (2.0 * sig - rk)
        d = (nxt * rk) * d + (2.0 * nxt / RHO) * rest
        y = y + d
        rk = nxt
    u = y[38:39]
    t = jnp.sum(u, axis=1, keepdims=True)
    w = jnp.sum(y, axis=1, keepdims=True)
    share = (SIGMA / SUBS) / (1.0 - (SIGMA / SUBS) * t)
    return y + (w * share) * u


def coarse_parts(y, s0, s1):
    row = iota((8, SUBS), 0)
    s = jnp.where(row < EACH, s0, s1)
    group = lax.shift_right_logical(iota((8, 128), 1), jnp.int32(5))
    edges = jnp.zeros((8, 128), F32)
    for k in range(4):
        edges = jnp.where(group == k, jnp.sum(y[8 * k : 8 * k + 8] * s, axis=1, keepdims=True), edges)
    own = jnp.sum(y[32:40] * s, axis=1, keepdims=True)
    at = (iota((8, 128), 1) < SIDE) & (iota((8, 128), 0) < 6)
    return edges, jnp.where(at, own, 0.0)


def finish(r, local, mass, rims, flip, edges, own, c):
    turned = spread(rims, c["rev"])
    rims = jnp.where(flip > 0.5, turned, rims)
    e = jnp.where(iota((8, 128), 0) < 6, edges - rims, 0.0)
    lane = iota((8, 128), 1)
    left = roll(e, 33, 1)
    both = jnp.where((lane >= 1) & (lane < 32), left, jnp.where((lane >= 32) & (lane < 64), e, 0.0))
    f, fr, fm = by_row(local), by_row(r), by_row(mass)
    z, image = [], []
    for i in range(SIDE):
        zi = f[i] + own
        moved = roll(both, 127 - i, 1)
        if i == 31:
            moved = jnp.where(lane == 0, roll(left, 96, 1), moved)
        extra = jnp.where((lane == 0) | (lane == 31), moved, 0.0)
        if i == 0:
            extra = extra + jnp.where(lane < SIDE, e, 0.0)
        if i == 31:
            extra = extra + jnp.where(lane < SIDE, roll(e, 64, 1), 0.0)
        z.append(zi)
        image.append(fr[i] + fm[i] * zi + extra)
    return jnp.concatenate(z, axis=0), jnp.concatenate(image, axis=0)


def dots_tile(pairs, first):
    lane, row = iota((8, 128), 1), iota((8, 128), 0)
    total = jnp.zeros((8, 128), F32)
    for k, (a, b) in enumerate(pairs, first):
        one = jnp.sum(jnp.sum(by_row(a * b), axis=0), axis=1, keepdims=True)
        at = ((lane == k) & (row < EACH)) | ((lane == 6 + k) & (row >= EACH) & (row < 6))
        total = jnp.where(at, one, total)
    return total


def steps(row, p):
    ga, de, rw, qw, zv, wv = [row[:, 6 * p + k : 6 * p + k + 1] for k in range(6)]
    a0 = ga / de
    g1 = ga - a0 * (de + rw) + a0 * a0 * qw
    d1 = de - a0 * (qw + zv) + a0 * a0 * wv
    beta = g1 / ga
    cross = de - a0 * (0.5 * (qw + zv))
    den = d1 + 2.0 * beta * cross + beta * beta * de
    a1 = g1 / den
    return a0 + a1 * (1.0 + beta), a1 * a0


def stack_rows(tiles):
    return jnp.concatenate([jnp.sum(tiles, axis=0), jnp.zeros((2, 128), F32)], axis=0)


def kernel(src_hbm, mass_hbm, nb_hbm, ns_hbm, fl_hbm, s8_hbm, small_hbm, wide_hbm, inv_hbm, out_ref,
           src_v, mass_v, nb_v, ns_v, fl_v, s8_v, small_v, wide_v, inv_v,
           r_v, m_v, l_v, choose_v, e0_v, flip_v, x_v, g_v, xh_v, xl_v, first_v,
           stga0, stga1, bufa0, bufa1, stgb0, stgb1, bufb0, bufb1, st3a, st3b, buf3a, buf3b,
           nat_v, stgm, bufm, y_v, edge_v, own_v, dots_v, insem, ssem, rsem, opensem, farsem):
    t = lax.axis_index("tile")
    lev = lax.axis_index("lev")
    plane, q = t // PLANE, t % PLANE
    line, x_at = q // LINE, q % LINE
    ready = t >= 0

    def at(dy, dz, dx, dl):
        where = ((plane + dy) % COLUMN * LINE + (line + dz) % LINE) * LINE + (x_at + dx) % LINE
        return (where, (lev + dl) % LEVS)

    a_peers = [(dy, 0, 0, 0) for dy in (4, 3, 5, 2, 6, 1, 7)]
    b_peers = [(0, dz, dx, 0) for dz in (3, 2, 1, 0) for dx in (2, 1, 3, 0) if dz or dx]
    xy_peers = [(dy, 0, dx, 0) for dy in (4, 3, 5, 2, 6, 1, 7, 0) for dx in (2, 1, 3, 0) if dy or dx]
    zc_peers = [(0, dz, 0, dl) for dz in (3, 2, 1, 0) for dl in range(LEVS) if dz or dl]
    l_peers = [(0, 0, 0, dl) for dl in (2, 3, 4, 5, 1)]
    far_peers = [(0, 1, 2, 0), (0, 3, 2, 0)]
    between = [(0, 1, 0, 0), (0, 3, 0, 0)]
    everyone = a_peers + l_peers + [peer for peer in b_peers if peer not in far_peers]

    moves = [(src_hbm.at[p, n], src_v.at[pl.ds(p * EACH + n, 1)]) for p in range(2) for n in range(EACH)]
    moves += [(mass_hbm, mass_v), (s8_hbm, s8_v), (small_hbm, small_v), (inv_hbm, inv_v),
              (nb_hbm, nb_v), (ns_hbm, ns_v), (fl_hbm, fl_v), (wide_hbm, wide_v)]
    copies = [pltpu.make_async_copy(a, b, insem.at[k]) for k, (a, b) in enumerate(moves)]
    for copy in copies:
        copy.start()

    barrier = pltpu.get_barrier_semaphore()
    for peer in everyone:
        pl.semaphore_signal(barrier, 1, device_id=at(*peer), device_id_type=pl.DeviceIdType.MESH)

    for copy in copies:
        copy.wait()

    def spot(peer):
        return (line + peer[1]) % LINE * LINE + (x_at + peer[2]) % LINE

    def send(peers, src_of, dst, n):
        for peer in peers:
            pltpu.make_async_remote_copy(
                src_ref=src_of(peer), dst_ref=dst, send_sem=ssem.at[n], recv_sem=rsem.at[n],
                device_id=at(*peer), device_id_type=pl.DeviceIdType.MESH,
            ).start()

    def done(peers, buf, n, recv):
        view = buf.at[pl.ds(0, len(peers))]
        copy = pltpu.make_async_remote_copy(
            src_ref=view, dst_ref=view, send_sem=ssem.at[n], recv_sem=rsem.at[n],
            device_id=at(*peers[0]), device_id_type=pl.DeviceIdType.MESH,
        )
        if recv:
            copy.wait_recv()
        else:
            copy.wait_send()

    def consts():
        return {
            "s8": (s8_v[:256], s8_v[256:]),
            "s": (small_v[:SIDE], small_v[SIDE : 2 * SIDE]),
            "ends": (small_v[64:96], small_v[96:128]),
            "quad": (small_v[128:256], small_v[256:384]),
            "rev": small_v[384:],
            "inv": inv_v[...],
            "cmp": wide_v[...],
        }

    c = consts()
    zrow = jnp.zeros((1, 128), F32)

    first = src_v[...]
    r = to_field(jnp.where(iota(first.shape, 0) < 6, first, 0.0))
    mass = to_field(stack_fields(mass_v[...], mass_v[...]))
    r_v[...] = r
    m_v[...] = mass
    x0 = coefficients(r, c)
    rims = local_rims(x0, c)
    tile = tile_a(rims, packed(r, plane), packed(mass, plane))
    stga0[...] = tile
    bufa0[plane] = tile
    pl.semaphore_wait(barrier, len(everyone))
    send(a_peers, lambda peer: stga0, bufa0.at[plane], 0)
    for peer in between:
        pl.semaphore_signal(farsem, 1, device_id=at(*peer), device_id_type=pl.DeviceIdType.MESH)

    polys = polynomial()[2]
    rhos = [polys]
    for _ in range(2):
        rhos.append(rhos[-1] ** 2 / (2.0 - rhos[-1] ** 2))

    @pl.when(ready)
    def _():
        l_v[...] = local_field(x0, c)
        choose, e0, flip = tables(nb_v[...], ns_v[...], fl_v[...], t)
        choose_v[...] = choose
        e0_v[...] = e0
        flip_v[...] = flip
        g32 = graph(nb_v[...])
        g_v[...] = g32.astype(BF16)
        x_v[...] = start_inverse(g32)[0]

    @pl.when(ready)
    def _():
        x_v[...] = newton(x_v[...], g_v[...], rhos[0], False)[0]

    done(a_peers, bufa0, 0, True)
    pl.semaphore_wait(farsem, len(between))
    total = jnp.sum(bufa0[...], axis=0)[6:8]
    stgm[...] = total
    bufm[q] = total
    send(b_peers, lambda peer: stgm, bufm.at[q], 6)
    stgb0[...] = tiles_b(bufa0[...], choose_v[...])
    bufb0[q] = stgb0[q]
    send(b_peers, lambda peer: stgb0.at[spot(peer), pl.ds(0, 6)], bufb0.at[q, pl.ds(0, 6)], 1)

    @pl.when(ready)
    def _():
        x_v[...] = newton(x_v[...], g_v[...], rhos[1], False)[0]

    @pl.when(ready)
    def _():
        x = newton(x_v[...], g_v[...], rhos[2], True)[0]
        xs = split(x, 3)
        e0 = e0_v[...]
        first_v[...] = dot(e0, xs[0]) + (dot(e0, xs[1]) + dot(e0, xs[2]))
        xh_v[...] = xs[0]
        xl_v[...] = xs[1]

    done(b_peers, bufm, 6, True)

    @pl.when(ready)
    def _():
        sums = bufm[:, 0, :]
        three = jnp.concatenate([bufm[:, 1, :], sums, roll(sums, 128 - EACH, 1)], axis=0)
        dvec, s0, s1 = to_vectors(three, consts())
        y = inverse_rows(first_v[...], xh_v[...], xl_v[...], dvec)
        y_v[...] = y
        edge_v[...], own_v[...] = coarse_parts(y, s0, s1)

    done(b_peers, bufb0.at[:, pl.ds(0, 6)], 1, True)
    c = consts()
    flip = flip_v[...]
    r, mass = r_v[...], m_v[...]
    z0, q0 = finish(r, l_v[...], mass, stack_rows(bufb0[:, 0:6, :]), flip, edge_v[...], own_v[...], c)

    x1 = coefficients(q0, c)
    rims = local_rims(x1, c)
    tile = tile_a(rims, packed(q0, plane), zrow)
    stga1[...] = tile
    bufa1[plane] = tile
    send(a_peers, lambda peer: stga1, bufa1.at[plane], 2)
    for peer in l_peers:
        pl.semaphore_signal(opensem, 1, device_id=at(*peer), device_id_type=pl.DeviceIdType.MESH)

    @pl.when(ready)
    def _():
        l_v[...] = local_field(x1, c)
        dots_v[...] = dots_tile(((r, z0), (z0, q0)), 0)

    done(a_peers, bufa1, 2, True)
    stgb1[...] = tiles_b(bufa1[...], choose_v[...])
    bufb1[q] = stgb1[q]
    send(b_peers, lambda peer: stgb1.at[spot(peer)], bufb1.at[q], 3)
    done(b_peers, bufb1, 3, True)
    sums = bufb1[:, 6, :]
    s0, s1 = to_vectors(jnp.concatenate([sums, roll(sums, 128 - EACH, 1)], axis=0), c)
    edges, own = coarse_parts(y_v[...], s0, s1)
    w, v = finish(q0, l_v[...], mass, jnp.sum(bufb1[...], axis=0), flip, edges, own, c)

    tile = dots_v[...] + dots_tile(((r, w), (q0, w), (z0, v), (w, v)), 2)
    row = jnp.sum(tile, axis=0, keepdims=True)
    st3a[...] = row
    buf3a[plane * LINE + x_at] = row
    send(xy_peers, lambda peer: st3a, buf3a.at[plane * LINE + x_at], 4)

    @pl.when(ready)
    def _():
        for k, field in enumerate((z0, q0, w, v)):
            nat_v[k] = from_field(by_row(field))

    done(xy_peers, buf3a, 4, True)
    row = jnp.sum(buf3a[...], axis=0)
    st3b[...] = row
    buf3b[line * LEVS + lev] = row
    pl.semaphore_wait(opensem, len(l_peers))
    send(zc_peers, lambda peer: st3b, buf3b.at[line * LEVS + lev], 5)
    done(zc_peers, buf3b, 5, True)
    row = jnp.sum(buf3b[...], axis=0)

    upper = iota((8, 1), 0) < EACH
    a0, b0 = steps(row, 0)
    a1, b1 = steps(row, 1)
    a, b = jnp.where(upper, a0, a1), jnp.where(upper, b0, b1)
    outs = [a * nat_v[0] - b * nat_v[2], src_v[...] - a * nat_v[1] + b * nat_v[3]]
    for k, out in enumerate(outs):
        for p in range(2):
            for n in range(EACH):
                out_ref[k, p, n] = out[p * EACH + n : p * EACH + n + 1]

    done(a_peers, bufa0, 0, False)
    done(b_peers, bufb0.at[:, pl.ds(0, 6)], 1, False)
    done(a_peers, bufa1, 2, False)
    done(b_peers, bufb1, 3, False)
    done(xy_peers, buf3a, 4, False)
    done(zc_peers, buf3b, 5, False)
    done(b_peers, bufm, 6, False)


def shards(sources, mass_coef, neighbour_sub, neighbour_side, side_flip):
    s8, small, wide, inv = [jnp.asarray(a) for a in constants()]
    hbm = pl.BlockSpec(memory_space=pltpu.HBM)
    rows = sources.transpose(0, 2, 1, 3)
    args = [rows, mass_coef, neighbour_sub.T, neighbour_side.T, side_flip.T, s8, small, wide, inv]
    one = pltpu.VMEM((8, 128), F32)
    line = pltpu.VMEM((1, 128), F32)
    field = pltpu.VMEM((ROWS, 128), F32)
    square = lambda kind: pltpu.VMEM((SUBS, SUBS), kind)
    plane = pltpu.VMEM((PLANE, 8, 128), F32)
    column = pltpu.VMEM((COLUMN, 8, 128), F32)
    scratch = [pltpu.VMEM((8, SIDE * SIDE), F32)] + [pltpu.VMEM(a.shape, a.dtype) for a in args[1:]] + [
        field, field, field, pltpu.VMEM((512, 256), BF16), pltpu.VMEM((40, SUBS), BF16), one,
        square(F32), square(BF16), square(BF16), square(BF16), pltpu.VMEM((40, SUBS), F32),
        one, one, column, column, plane, plane, plane, plane, line, line,
        pltpu.VMEM((COLUMN * LINE, 1, 128), F32), pltpu.VMEM((LINE * LEVS, 1, 128), F32),
        pltpu.VMEM((4, 8, SIDE * SIDE), F32),
        pltpu.VMEM((2, 128), F32), pltpu.VMEM((PLANE, 2, 128), F32), pltpu.VMEM((40, SUBS), F32), one, one, one,
        pltpu.SemaphoreType.DMA((14,)),
        pltpu.SemaphoreType.DMA((7,)), pltpu.SemaphoreType.DMA((7,)), pltpu.SemaphoreType.REGULAR, pltpu.SemaphoreType.REGULAR,
    ]
    out = pltpu.VMEM((2,) + rows.shape, F32)
    both = pl.pallas_call(
        kernel,
        out_shape=out,
        in_specs=[hbm] * len(args),
        out_specs=pl.BlockSpec(memory_space=pltpu.VMEM),
        scratch_shapes=scratch,
        compiler_params=pltpu.CompilerParams(collective_id=0, has_side_effects=True, vmem_limit_bytes=60 << 20),
        name="schwarz",
    )(*args)
    both = both.transpose(0, 1, 3, 2, 4)
    return both[0], both[1]


def solution(mesh):
    placed = (P(None, "lev", "tile", None), P("tile", None), P(), P(), P())
    return jax.shard_map(
        shards,
        mesh=mesh,
        in_specs=placed,
        out_specs=(P(None, "lev", "tile", None), P(None, "lev", "tile", None)),
        check_vma=False,
    )
```

```python
import math

import jax
import jax.numpy as jnp
import numpy as np
from jax import lax
from jax.experimental import pallas as pl
from jax.experimental.pallas import tpu as pltpu
from jax.sharding import PartitionSpec as P

F32 = jnp.float32
BF16 = jnp.bfloat16
SIDE = 32
SUBS = 384
PLANE = 16
COLUMN = 8
LEVS = 6
EACH = 3
LINE = 4
ROWS = 8 * SIDE

SHIFT = 1.28
SIGMA = 3.0
LOW = 32.0 * 0.06486 + SHIFT
TOP = 32.0 * 8.0 + SHIFT
RHO = 0.7681 / LOW
CHEB = 6


def roll(x, shift, axis):
    return pltpu.roll(x, shift, axis)


def iota(shape, dim):
    return lax.broadcasted_iota(jnp.int32, shape, dim)


def dot(a, b):
    return jnp.dot(a, b, preferred_element_type=F32)


def split(x, n):
    parts = []
    for _ in range(n):
        part = x.astype(BF16)
        parts.append(part)
        x = x - part.astype(F32)
    return parts


def stack(parts):
    return jnp.concatenate([part.astype(F32) for part in parts], axis=0).astype(BF16)


def spread(x, onehot):
    n = x.shape[0]
    out = dot(stack(split(x, 3)), onehot)
    return out[:n] + out[n : 2 * n] + out[2 * n :]


def mm3(a, b):
    ah, al = a
    bh, bl = b
    return dot(ah, bh) + (dot(ah, bl) + dot(al, bh))


def np_split(x):
    hi = x.astype(np.float32).astype(jnp.bfloat16)
    lo = (x - hi.astype(np.float64)).astype(np.float32).astype(jnp.bfloat16)
    return hi, lo


def polynomial():
    deg = 7
    nodes = np.cos(np.pi * (np.arange(deg + 1) + 0.5) / (deg + 1))
    g = 4.0 * nodes
    x = 128.0 + SHIFT - 32.0 * g

    def cheb(n, t):
        return np.where(
            np.abs(t) <= 1,
            np.cos(n * np.arccos(np.clip(t, -1, 1))),
            np.sign(t) ** n * np.cosh(n * np.arccosh(np.maximum(np.abs(t), 1))),
        )

    def tau(v):
        return (TOP + LOW - 2 * v) / (TOP - LOW)

    top = cheb(deg + 1, tau(0.0))
    vals = (1.0 - cheb(deg + 1, tau(x)) / top) / x
    coef = np.polynomial.polynomial.polyfit(nodes, vals, deg)
    at_one = np.polynomial.polynomial.polyval(1.0, coef)
    const = (1.0 / (SHIFT + SIGMA) - at_one) / SUBS
    return [float(c / 4.0**k) for k, c in enumerate(coef)], float(const), float(1.0 / top)


def constants():
    o = np.arange(SIDE) + 1.0
    step = math.pi / (SIDE + 1.0)
    sine = math.sqrt(2.0 / (SIDE + 1.0)) * np.sin(step * o[:, None] * o[None, :])
    lam = 2.0 - 2.0 * np.cos(step * o)
    inv = np.repeat(1.0 / (lam[:, None] + lam[None, :]), 8, axis=0)
    lanes = np.arange(128)
    side, kk = lanes // SIDE, lanes % SIDE
    m = np.arange(SUBS)
    cmp = ((lanes // 8)[:, None] == (m // EACH // PLANE)[None]) & ((lanes % 8)[:, None] == (m % EACH)[None])
    rev = (side[:, None] == side[None]) & (kk[:, None] == 31 - kk[None])
    s8 = np.concatenate(np_split(np.kron(sine, np.eye(8))), axis=0)
    s = np.concatenate([np.pad(a, ((0, 0), (0, 128 - SIDE))) for a in np_split(sine)], axis=0)
    ends = np.zeros((SIDE, 128))
    ends[:, 32:64] = sine[:, 31:32]
    ends[:, 96:] = sine[:, 0:1]
    quad = np.kron(np.eye(4), sine)
    rev = rev.astype(np.float32).astype(jnp.bfloat16)
    small = np.concatenate([s, *np_split(ends), *np_split(quad), rev], axis=0)
    wide = cmp.astype(np.float32).astype(jnp.bfloat16)
    return s8, small, wide, inv.astype(np.float32)


def by_row(v):
    return v.reshape(SIDE, 8, 128)


def stack_fields(first, second):
    return jnp.concatenate([first, second, jnp.zeros((2, first.shape[1]), F32)], axis=0)


def to_field(x):
    lane = iota((8, 128), 1)
    rows = []
    for i in range(SIDE):
        g, h = i // 4, i % 4
        part = x[:, 128 * g : 128 * g + 128]
        part = part if h == 0 else roll(part, 128 - 32 * h, 1)
        rows.append(jnp.where(lane < SIDE, part, 0.0))
    return jnp.concatenate(rows, axis=0)


def from_field(v):
    parts = []
    for g in range(8):
        total = v[4 * g]
        for h in (1, 2, 3):
            total = total + roll(v[4 * g + h], 32 * h, 1)
        parts.append(total)
    return jnp.concatenate(parts, axis=1)


def coefficients(r, c):
    v = mm3(c["s8"], split(r[:, :SIDE], 2))
    return mm3(split(v, 2), c["s"])[:, :SIDE] * c["inv"]


def local_rims(x, c):
    w = by_row(mm3(split(x, 2), c["ends"]))
    f = x.reshape(SIDE, 8, SIDE)
    lane = iota((8, 128), 1) & 63
    scale = [math.sqrt(2.0 / 33.0) * math.sin(math.pi * (i + 1) / 33.0) for i in range(SIDE)]
    even = sum(scale[i] * f[i] for i in range(0, SIDE, 2))
    odd = sum(scale[i] * f[i] for i in range(1, SIDE, 2))
    blank = jnp.zeros((8, SIDE), F32)
    tile = jnp.concatenate([even + odd, blank, even - odd, blank], axis=1)
    for i in range(SIDE):
        tile = jnp.where(lane == 32 + i, w[i], tile)
    th, tl = split(tile, 2)
    qh, ql = c["quad"]
    both = dot(stack([th, tl]), qh)
    return both[:8] + (both[8:] + dot(th, ql))


def local_field(x, c):
    v = mm3(split(x, 2), c["s"])
    return mm3(c["s8"], split(v, 2))


def packed(v, place):
    total = jnp.sum(jnp.sum(by_row(v), axis=0), axis=1, keepdims=True)
    at = iota((8, 128), 1) == place * 8 + iota((8, 128), 0)
    return jnp.sum(jnp.where(at, total, 0.0), axis=0, keepdims=True)


def tile_a(rims, sums, mass):
    row = iota((8, 128), 0)
    return jnp.where(row == 6, sums, jnp.where(row == 7, mass, rims))


def tables(nb, ns, fl, t):
    plane, q = t // PLANE, t % PLANE
    row, lane = iota((136, SUBS), 0), iota((136, SUBS), 1)
    target = jnp.where(row < 128, lax.shift_right_logical(row, jnp.int32(3)), q)
    field = row & 7
    sub = (plane * PLANE + target) * EACH + jnp.where(field >= EACH, field - EACH, field)
    take = (lane == sub) & (field < 6)

    def column(a, s):
        return jnp.sum(jnp.where(take, a[s : s + 1].astype(F32), 0.0), axis=1, keepdims=True)

    nbs = [column(nb, s).astype(jnp.int32) for s in range(4)]
    nss = [column(ns, s).astype(jnp.int32) for s in range(4)]
    fls = [column(fl, s) for s in range(4)]

    field = iota((128, 1), 0) & 7
    third = jnp.where(field >= EACH, EACH, 0)
    cols = iota((128, 256), 1)
    choose = []
    for s in range(4):
        sub = nbs[s][:128]
        device = lax.shift_right_logical(sub * 21846, jnp.int32(16))
        at = ((s - nss[s][:128]) & 3) * 64 + lax.shift_right_logical(device, jnp.int32(4)) * 8 + (sub - EACH * device) + third
        inside = ((device & 15) == q) & (field < 6)
        choose.append((cols == jnp.where(inside, at, -1)).astype(F32).astype(BF16))

    field, lane = iota((8, SUBS), 0), iota((8, SUBS), 1)
    own = (lane == t * EACH + jnp.where(field >= EACH, field - EACH, field)).astype(F32)
    rows = []
    for s in range(4):
        rows.append(jnp.where(field < 6, own - (lane == nbs[s][128:136]).astype(F32), 0.0))
    rows.append(jnp.where(field < 6, own, jnp.where(field == 6, 1.0, 0.0)))
    group = lax.shift_right_logical(iota((8, 128), 1), jnp.int32(5))
    flip = jnp.zeros((8, 128), F32)
    for s in range(4):
        flip = jnp.where(group == s, fls[s][128:136], flip)
    return jnp.concatenate(choose, axis=0), jnp.concatenate(rows, axis=0).astype(BF16), flip


def tiles_b(buf, choose):
    flat = buf.reshape(64, 128)
    turned = jnp.concatenate([flat] + [roll(flat, 32 * t, 1) for t in (1, 2, 3)], axis=0)
    a, b, c = split(turned, 3)
    wide = dot(choose, jnp.concatenate([a, b], axis=1))
    got = (wide[:, :128] + wide[:, 128:]) + dot(choose, c)
    group = lax.shift_right_logical(iota((128, 128), 1), jnp.int32(5))
    out = jnp.where(group == 0, got[:128], 0.0)
    for s in (1, 2, 3):
        out = jnp.where(group == s, got[128 * s : 128 * s + 128], out)
    row = iota((8, 128), 0)
    column = jnp.where(row >= 6, jnp.sum(buf, axis=0), 0.0)
    return out.reshape(PLANE, 8, 128) + column[None]


def graph(nb):
    row = iota((SUBS, SUBS), 0)
    total = jnp.zeros((SUBS, SUBS), F32)
    for s in range(4):
        total = total + (row == nb[s : s + 1]).astype(F32)
    return total


def start_inverse(g32):
    coef, const, rho = polynomial()
    g = g32.astype(BF16)
    g2 = dot(g, g)
    g2b = g2.astype(BF16)
    g3 = dot(g2b, g)
    g4 = dot(g2b, g2b)
    g3b, g4b = g3.astype(BF16), g4.astype(BF16)
    eye = (iota((SUBS, SUBS), 0) == iota((SUBS, SUBS), 1)).astype(F32)
    x = coef[0] * eye + const + coef[1] * g32 + coef[2] * g2 + coef[3] * g3 + coef[4] * g4
    x = x + coef[5] * dot(g4b, g) + coef[6] * dot(g4b, g2b) + coef[7] * dot(g4b, g3b)
    return x, rho


def newton(x, g, rho, last):
    xs = split(x, 3 if last else 2)
    gx = dot(g, xs[0]) + dot(g, xs[1])
    if last:
        gx = gx + dot(g, xs[2])
    ones = (SIGMA / SUBS) * jnp.sum(x, axis=0, keepdims=True)
    eye = (iota((SUBS, SUBS), 0) == iota((SUBS, SUBS), 1)).astype(F32)
    rest = eye - ((128.0 + SHIFT) * x - 32.0 * gx + ones)
    x = x + mm3(xs[:2], split(rest, 2))
    if last:
        return x, 0.0
    scale = 2.0 / (2.0 - rho * rho)
    return scale * x, rho * rho / (2.0 - rho * rho)


def to_vectors(slots, c):
    wide = spread(slots, c["cmp"])
    row, lane = iota((PLANE, SUBS), 0), iota((PLANE, SUBS), 1)
    keep = (lax.shift_right_logical(lane * 21846, jnp.int32(16)) & 15) == row
    rows = []
    for k in range(slots.shape[0] // PLANE):
        block = wide[PLANE * k : PLANE * k + PLANE]
        rows.append(jnp.sum(jnp.where(keep, block, 0.0), axis=0, keepdims=True))
    return rows


def inverse_rows(first, xh, xl, mass):
    delta = mass - SHIFT

    def apply(d, fine):
        e = d * delta
        if not fine:
            return d + dot(e.astype(BF16), xh)
        eh, el = split(e, 2)
        n = e.shape[0]
        high = dot(stack([eh, el]), xh)
        return d + (high[:n] + (high[n:] + dot(eh, xl)))

    sig = 1.0 / RHO
    rk = 1.0 / sig
    rest = first
    d = rest
    y = d
    for k in range(CHEB):
        rest = rest - apply(d, k < 3)
        nxt = 1.0 / (2.0 * sig - rk)
        d = (nxt * rk) * d + (2.0 * nxt / RHO) * rest
        y = y + d
        rk = nxt
    u = y[38:39]
    t = jnp.sum(u, axis=1, keepdims=True)
    w = jnp.sum(y, axis=1, keepdims=True)
    share = (SIGMA / SUBS) / (1.0 - (SIGMA / SUBS) * t)
    return y + (w * share) * u


def coarse_parts(y, s0, s1):
    row = iota((8, SUBS), 0)
    s = jnp.where(row < EACH, s0, s1)
    group = lax.shift_right_logical(iota((8, 128), 1), jnp.int32(5))
    edges = jnp.zeros((8, 128), F32)
    for k in range(4):
        edges = jnp.where(group == k, jnp.sum(y[8 * k : 8 * k + 8] * s, axis=1, keepdims=True), edges)
    own = jnp.sum(y[32:40] * s, axis=1, keepdims=True)
    at = (iota((8, 128), 1) < SIDE) & (iota((8, 128), 0) < 6)
    return edges, jnp.where(at, own, 0.0)


def finish(r, local, mass, rims, flip, edges, own, c):
    turned = spread(rims, c["rev"])
    rims = jnp.where(flip > 0.5, turned, rims)
    e = jnp.where(iota((8, 128), 0) < 6, edges - rims, 0.0)
    lane = iota((8, 128), 1)
    left = roll(e, 33, 1)
    both = jnp.where((lane >= 1) & (lane < 32), left, jnp.where((lane >= 32) & (lane < 64), e, 0.0))
    f, fr, fm = by_row(local), by_row(r), by_row(mass)
    z, image = [], []
    for i in range(SIDE):
        zi = f[i] + own
        moved = roll(both, 127 - i, 1)
        if i == 31:
            moved = jnp.where(lane == 0, roll(left, 96, 1), moved)
        extra = jnp.where((lane == 0) | (lane == 31), moved, 0.0)
        if i == 0:
            extra = extra + jnp.where(lane < SIDE, e, 0.0)
        if i == 31:
            extra = extra + jnp.where(lane < SIDE, roll(e, 64, 1), 0.0)
        z.append(zi)
        image.append(fr[i] + fm[i] * zi + extra)
    return jnp.concatenate(z, axis=0), jnp.concatenate(image, axis=0)


def dots_tile(pairs, first):
    lane, row = iota((8, 128), 1), iota((8, 128), 0)
    total = jnp.zeros((8, 128), F32)
    for k, (a, b) in enumerate(pairs, first):
        one = jnp.sum(jnp.sum(by_row(a * b), axis=0), axis=1, keepdims=True)
        at = ((lane == k) & (row < EACH)) | ((lane == 6 + k) & (row >= EACH) & (row < 6))
        total = jnp.where(at, one, total)
    return total


def steps(row, p):
    ga, de, rw, qw, zv, wv = [row[:, 6 * p + k : 6 * p + k + 1] for k in range(6)]
    a0 = ga / de
    g1 = ga - a0 * (de + rw) + a0 * a0 * qw
    d1 = de - a0 * (qw + zv) + a0 * a0 * wv
    beta = g1 / ga
    cross = de - a0 * (0.5 * (qw + zv))
    den = d1 + 2.0 * beta * cross + beta * beta * de
    a1 = g1 / den
    return a0 + a1 * (1.0 + beta), a1 * a0


def stack_rows(tiles):
    return jnp.concatenate([jnp.sum(tiles, axis=0), jnp.zeros((2, 128), F32)], axis=0)


def kernel(src_hbm, mass_hbm, nb_hbm, ns_hbm, fl_hbm, s8_hbm, small_hbm, wide_hbm, inv_hbm, out_ref,
           src_v, mass_v, nb_v, ns_v, fl_v, s8_v, small_v, wide_v, inv_v,
           r_v, m_v, l_v, choose_v, e0_v, flip_v, x_v, g_v, xh_v, xl_v, first_v,
           stga0, stga1, bufa0, bufa1, stgb0, stgb1, bufb0, bufb1, st3a, st3b, buf3a, buf3b,
           nat_v, stgm, bufm, y_v, edge_v, own_v, dots_v, insem, ssem, rsem, opensem, farsem):
    t = lax.axis_index("tile")
    lev = lax.axis_index("lev")
    plane, q = t // PLANE, t % PLANE
    line, x_at = q // LINE, q % LINE
    ready = t >= 0

    def at(dy, dz, dx, dl):
        where = ((plane + dy) % COLUMN * LINE + (line + dz) % LINE) * LINE + (x_at + dx) % LINE
        return (where, (lev + dl) % LEVS)

    a_peers = [(dy, 0, 0, 0) for dy in (4, 3, 5, 2, 6, 1, 7)]
    b_peers = [(0, dz, dx, 0) for dz in (3, 2, 1, 0) for dx in (2, 1, 3, 0) if dz or dx]
    xy_peers = [(dy, 0, dx, 0) for dy in (4, 3, 5, 2, 6, 1, 7, 0) for dx in (2, 1, 3, 0) if dy or dx]
    zc_peers = [(0, dz, 0, dl) for dz in (3, 2, 1, 0) for dl in range(LEVS) if dz or dl]
    l_peers = [(0, 0, 0, dl) for dl in (2, 3, 4, 5, 1)]
    far_peers = [(0, 1, 2, 0), (0, 3, 2, 0)]
    between = [(0, 1, 0, 0), (0, 3, 0, 0)]
    everyone = a_peers + l_peers + [peer for peer in b_peers if peer not in far_peers]

    moves = [(src_hbm.at[p, n], src_v.at[pl.ds(p * EACH + n, 1)]) for p in range(2) for n in range(EACH)]
    moves += [(mass_hbm, mass_v), (s8_hbm, s8_v), (small_hbm, small_v), (inv_hbm, inv_v),
              (nb_hbm, nb_v), (ns_hbm, ns_v), (fl_hbm, fl_v), (wide_hbm, wide_v)]
    copies = [pltpu.make_async_copy(a, b, insem.at[k]) for k, (a, b) in enumerate(moves)]
    for copy in copies:
        copy.start()

    barrier = pltpu.get_barrier_semaphore()
    for peer in everyone:
        pl.semaphore_signal(barrier, 1, device_id=at(*peer), device_id_type=pl.DeviceIdType.MESH)

    for copy in copies:
        copy.wait()

    def spot(peer):
        return (line + peer[1]) % LINE * LINE + (x_at + peer[2]) % LINE

    def send(peers, src_of, dst, n):
        for peer in peers:
            pltpu.make_async_remote_copy(
                src_ref=src_of(peer), dst_ref=dst, send_sem=ssem.at[n], recv_sem=rsem.at[n],
                device_id=at(*peer), device_id_type=pl.DeviceIdType.MESH,
            ).start()

    def done(peers, buf, n, recv):
        view = buf.at[pl.ds(0, len(peers))]
        copy = pltpu.make_async_remote_copy(
            src_ref=view, dst_ref=view, send_sem=ssem.at[n], recv_sem=rsem.at[n],
            device_id=at(*peers[0]), device_id_type=pl.DeviceIdType.MESH,
        )
        if recv:
            copy.wait_recv()
        else:
            copy.wait_send()

    def consts():
        return {
            "s8": (s8_v[:256], s8_v[256:]),
            "s": (small_v[:SIDE], small_v[SIDE : 2 * SIDE]),
            "ends": (small_v[64:96], small_v[96:128]),
            "quad": (small_v[128:256], small_v[256:384]),
            "rev": small_v[384:],
            "inv": inv_v[...],
            "cmp": wide_v[...],
        }

    c = consts()
    zrow = jnp.zeros((1, 128), F32)

    first = src_v[...]
    r = to_field(jnp.where(iota(first.shape, 0) < 6, first, 0.0))
    mass = to_field(stack_fields(mass_v[...], mass_v[...]))
    r_v[...] = r
    m_v[...] = mass
    x0 = coefficients(r, c)
    rims = local_rims(x0, c)
    tile = tile_a(rims, packed(r, plane), packed(mass, plane))
    stga0[...] = tile
    bufa0[plane] = tile
    pl.semaphore_wait(barrier, len(everyone))
    send(a_peers, lambda peer: stga0, bufa0.at[plane], 0)
    for peer in between:
        pl.semaphore_signal(farsem, 1, device_id=at(*peer), device_id_type=pl.DeviceIdType.MESH)

    polys = polynomial()[2]
    rhos = [polys]
    for _ in range(2):
        rhos.append(rhos[-1] ** 2 / (2.0 - rhos[-1] ** 2))

    @pl.when(ready)
    def _():
        l_v[...] = local_field(x0, c)
        choose, e0, flip = tables(nb_v[...], ns_v[...], fl_v[...], t)
        choose_v[...] = choose
        e0_v[...] = e0
        flip_v[...] = flip
        g32 = graph(nb_v[...])
        g_v[...] = g32.astype(BF16)
        x_v[...] = start_inverse(g32)[0]

    @pl.when(ready)
    def _():
        x_v[...] = newton(x_v[...], g_v[...], rhos[0], False)[0]

    done(a_peers, bufa0, 0, True)
    pl.semaphore_wait(farsem, len(between))
    total = jnp.sum(bufa0[...], axis=0)[6:8]
    stgm[...] = total
    bufm[q] = total
    send(b_peers, lambda peer: stgm, bufm.at[q], 6)
    stgb0[...] = tiles_b(bufa0[...], choose_v[...])
    bufb0[q] = stgb0[q]
    send(b_peers, lambda peer: stgb0.at[spot(peer), pl.ds(0, 6)], bufb0.at[q, pl.ds(0, 6)], 1)

    @pl.when(ready)
    def _():
        x_v[...] = newton(x_v[...], g_v[...], rhos[1], False)[0]

    @pl.when(ready)
    def _():
        x = newton(x_v[...], g_v[...], rhos[2], True)[0]
        xs = split(x, 3)
        e0 = e0_v[...]
        first_v[...] = dot(e0, xs[0]) + (dot(e0, xs[1]) + dot(e0, xs[2]))
        xh_v[...] = xs[0]
        xl_v[...] = xs[1]

    done(b_peers, bufm, 6, True)

    @pl.when(ready)
    def _():
        sums = bufm[:, 0, :]
        three = jnp.concatenate([bufm[:, 1, :], sums, roll(sums, 128 - EACH, 1)], axis=0)
        dvec, s0, s1 = to_vectors(three, consts())
        y = inverse_rows(first_v[...], xh_v[...], xl_v[...], dvec)
        y_v[...] = y
        edge_v[...], own_v[...] = coarse_parts(y, s0, s1)

    done(b_peers, bufb0.at[:, pl.ds(0, 6)], 1, True)
    c = consts()
    flip = flip_v[...]
    r, mass = r_v[...], m_v[...]
    z0, q0 = finish(r, l_v[...], mass, stack_rows(bufb0[:, 0:6, :]), flip, edge_v[...], own_v[...], c)

    x1 = coefficients(q0, c)
    rims = local_rims(x1, c)
    tile = tile_a(rims, packed(q0, plane), zrow)
    stga1[...] = tile
    bufa1[plane] = tile
    send(a_peers, lambda peer: stga1.at[pl.ds(0, 7)], bufa1.at[plane, pl.ds(0, 7)], 2)
    for peer in l_peers:
        pl.semaphore_signal(opensem, 1, device_id=at(*peer), device_id_type=pl.DeviceIdType.MESH)

    @pl.when(ready)
    def _():
        l_v[...] = local_field(x1, c)
        dots_v[...] = dots_tile(((r, z0), (z0, q0)), 0)

    done(a_peers, bufa1.at[:, pl.ds(0, 7)], 2, True)
    stgb1[...] = tiles_b(jnp.where(iota((COLUMN, 8, 128), 1) < 7, bufa1[...], 0.0), choose_v[...])
    bufb1[q] = stgb1[q]
    send(b_peers, lambda peer: stgb1.at[spot(peer), pl.ds(0, 7)], bufb1.at[q, pl.ds(0, 7)], 3)
    done(b_peers, bufb1.at[:, pl.ds(0, 7)], 3, True)
    sums = bufb1[:, 6, :]
    s0, s1 = to_vectors(jnp.concatenate([sums, roll(sums, 128 - EACH, 1)], axis=0), c)
    edges, own = coarse_parts(y_v[...], s0, s1)
    w, v = finish(q0, l_v[...], mass, stack_rows(bufb1[:, 0:6, :]), flip, edges, own, c)

    tile = dots_v[...] + dots_tile(((r, w), (q0, w), (z0, v), (w, v)), 2)
    row = jnp.sum(tile, axis=0, keepdims=True)
    st3a[...] = row
    buf3a[plane * LINE + x_at] = row
    send(xy_peers, lambda peer: st3a, buf3a.at[plane * LINE + x_at], 4)

    @pl.when(ready)
    def _():
        for k, field in enumerate((z0, q0, w, v)):
            nat_v[k] = from_field(by_row(field))

    done(xy_peers, buf3a, 4, True)
    row = jnp.sum(buf3a[...], axis=0)
    st3b[...] = row
    buf3b[line * LEVS + lev] = row
    pl.semaphore_wait(opensem, len(l_peers))
    send(zc_peers, lambda peer: st3b, buf3b.at[line * LEVS + lev], 5)
    done(zc_peers, buf3b, 5, True)
    row = jnp.sum(buf3b[...], axis=0)

    upper = iota((8, 1), 0) < EACH
    a0, b0 = steps(row, 0)
    a1, b1 = steps(row, 1)
    a, b = jnp.where(upper, a0, a1), jnp.where(upper, b0, b1)
    outs = [a * nat_v[0] - b * nat_v[2], src_v[...] - a * nat_v[1] + b * nat_v[3]]
    for k, out in enumerate(outs):
        for p in range(2):
            for n in range(EACH):
                out_ref[k, p, n] = out[p * EACH + n : p * EACH + n + 1]

    done(a_peers, bufa0, 0, False)
    done(b_peers, bufb0.at[:, pl.ds(0, 6)], 1, False)
    done(a_peers, bufa1.at[:, pl.ds(0, 7)], 2, False)
    done(b_peers, bufb1.at[:, pl.ds(0, 7)], 3, False)
    done(xy_peers, buf3a, 4, False)
    done(zc_peers, buf3b, 5, False)
    done(b_peers, bufm, 6, False)


def shards(sources, mass_coef, neighbour_sub, neighbour_side, side_flip):
    s8, small, wide, inv = [jnp.asarray(a) for a in constants()]
    hbm = pl.BlockSpec(memory_space=pltpu.HBM)
    rows = sources.transpose(0, 2, 1, 3)
    args = [rows, mass_coef, neighbour_sub.T, neighbour_side.T, side_flip.T, s8, small, wide, inv]
    one = pltpu.VMEM((8, 128), F32)
    line = pltpu.VMEM((1, 128), F32)
    field = pltpu.VMEM((ROWS, 128), F32)
    square = lambda kind: pltpu.VMEM((SUBS, SUBS), kind)
    plane = pltpu.VMEM((PLANE, 8, 128), F32)
    column = pltpu.VMEM((COLUMN, 8, 128), F32)
    scratch = [pltpu.VMEM((8, SIDE * SIDE), F32)] + [pltpu.VMEM(a.shape, a.dtype) for a in args[1:]] + [
        field, field, field, pltpu.VMEM((512, 256), BF16), pltpu.VMEM((40, SUBS), BF16), one,
        square(F32), square(BF16), square(BF16), square(BF16), pltpu.VMEM((40, SUBS), F32),
        one, one, column, column, plane, plane, plane, plane, line, line,
        pltpu.VMEM((COLUMN * LINE, 1, 128), F32), pltpu.VMEM((LINE * LEVS, 1, 128), F32),
        pltpu.VMEM((4, 8, SIDE * SIDE), F32),
        pltpu.VMEM((2, 128), F32), pltpu.VMEM((PLANE, 2, 128), F32), pltpu.VMEM((40, SUBS), F32), one, one, one,
        pltpu.SemaphoreType.DMA((14,)),
        pltpu.SemaphoreType.DMA((7,)), pltpu.SemaphoreType.DMA((7,)), pltpu.SemaphoreType.REGULAR, pltpu.SemaphoreType.REGULAR,
    ]
    out = pltpu.VMEM((2,) + rows.shape, F32)
    both = pl.pallas_call(
        kernel,
        out_shape=out,
        in_specs=[hbm] * len(args),
        out_specs=pl.BlockSpec(memory_space=pltpu.VMEM),
        scratch_shapes=scratch,
        compiler_params=pltpu.CompilerParams(collective_id=0, has_side_effects=True, vmem_limit_bytes=60 << 20),
        name="schwarz",
    )(*args)
    both = both.transpose(0, 1, 3, 2, 4)
    return both[0], both[1]


def solution(mesh):
    placed = (P(None, "lev", "tile", None), P("tile", None), P(), P(), P())
    return jax.shard_map(
        shards,
        mesh=mesh,
        in_specs=placed,
        out_specs=(P(None, "lev", "tile", None), P(None, "lev", "tile", None)),
        check_vma=False,
    )
```
